32 devices in a mesh: node: 4 (over y, x), rows: 8 (over z, core).
Axes of the slice: x: 2, y: 2, z: 4, core: 2. Of those that a mesh axis runs over, the one named last changes fastest.
Arguments:
- subspace: bfloat16 [6144, 256], P('rows'), may hold values from -6 to 6
- inverse: bfloat16 [4, 2, 6144, 768], P('node', None, 'rows')
- weights: float32 [4, 2], P('node'), may hold values from 0.25 to 1
- diag_tiles: float32 [6144, 128], P('rows'), may hold values from -0.5 to 0.5
- upper_tiles: float32 [6144, 128], P('rows'), may hold values from -0.5 to 0.5
Outputs:
- subspace_out: float32 [6144, 256], P('rows')
- projected: float32 [2, 256, 256], replicated
The draws below stay inside these ranges and needn't reach their ends.
All inputs are finite; a program needn't handle non-finite values.
Results may differ from the reference program's by a relative error of at most 0.0025.
Values may be sent and summed in bfloat16 or wider, within the bound.
No kernel may reach another device: no remote copies, remote signals or barrier semaphores. Data moves between devices by JAX's collectives and lax.ppermute only.
A program may use at most 64 MiB of HBM per device.

```python
import math
import jax
import jax.numpy as jnp
from jax import lax

HALF_BAND = 128
VECTORS = 256
ROWS_DEV = 768
ITERS = 2
NODES = 4
ORDER = 6144


def draw_inverse(key, part):
    noise_key = jax.random.fold_in(key, 7)
    spread = 0.866 / math.sqrt(ROWS_DEV)
    noise = jax.random.uniform(noise_key, (NODES, 2, ORDER, ROWS_DEV), jnp.float32, -spread, spread)
    row_index = lax.broadcasted_iota(jnp.int32, (ORDER, ROWS_DEV), 0) % ROWS_DEV
    column_index = lax.broadcasted_iota(jnp.int32, (ORDER, ROWS_DEV), 1)
    identity = (row_index == column_index).astype(jnp.float32)
    real_mark = (lax.broadcasted_iota(jnp.int32, (2,), 0) == 0).astype(jnp.float32)
    return (noise + identity[None, None] * real_mark[None, :, None, None]).astype(jnp.bfloat16)


def level_of(stream_key, dims, pieces, low, largest):
    gain, own = 1.0, jax.random.fold_in(stream_key, 6)
    for dim, blocks in pieces:
        heights = jnp.exp(jax.random.uniform(jax.random.fold_in(own, dim), (blocks,), jnp.float32, low / len(pieces), largest / len(pieces)))
        gain = gain * jnp.repeat(heights, dims[dim] // blocks).reshape([-1 if axis == dim else 1 for axis in range(len(dims))])
    return gain


def bell_draw(key, extent, deviation, limit, pieces=(), kind=jnp.bfloat16):
    values = jax.random.normal(key, extent, jnp.float32) * deviation
    if len(pieces) > 0:
        values = level_of(key, extent, pieces, -0.22, 0.18) * values
    return jnp.clip(values, min=-limit, max=limit).astype(kind)


def setup_inputs(seed: int = 0) -> dict:
    seeds = jax.random.split(jax.random.key(seed), 6)
    return {
        "subspace": bell_draw(seeds[0], (ORDER, VECTORS), 1.0, 6.0, ((0, 8),)),
        "inverse": draw_inverse(jax.random.fold_in(seeds[5], 71), 0),
        "weights": jnp.clip(0.25 + 0.75 * jax.random.uniform(seeds[2], (NODES, 2), jnp.float32) ** level_of(seeds[2], (NODES, 2), ((0, 4),), -0.2, 0.2), 0.25, 1.0),
        "diag_tiles": bell_draw(seeds[3], (ORDER, HALF_BAND), HALF_BAND ** -0.5, 0.5, ((0, 8),), jnp.float32),
        "upper_tiles": bell_draw(seeds[4], (ORDER, HALF_BAND), HALF_BAND ** -0.5, 0.5, ((0, 8),), jnp.float32),
    }


precise = lax.Precision.HIGHEST

def band_product(field, diag_tiles, upper_tiles):
    band_width = diag_tiles.shape[1]
    number = field.shape[0] // band_width
    field_tiles = field.reshape(number, band_width, field.shape[1])
    diagonal = diag_tiles.reshape(number, band_width, band_width)
    diagonal = 0.5 * (diagonal + jnp.swapaxes(diagonal, 1, 2))
    upper_part = upper_tiles.reshape(number, band_width, band_width)
    result = jnp.einsum('tij,tjm->tim', diagonal, field_tiles, precision=precise)
    forward = jnp.einsum('tij,tjm->tim', upper_part[:-1], field_tiles[1:], precision=precise)
    backward = jnp.einsum('tji,tjm->tim', upper_part[:-1], field_tiles[:-1], precision=precise)
    blank = jnp.zeros((1, band_width, field.shape[1]), jnp.float32)
    result = result + jnp.concatenate([forward, blank], 0) + jnp.concatenate([blank, backward], 0)
    return result.reshape(field.shape)

def to_half(values):
    return lax.optimization_barrier(values.astype(jnp.bfloat16)).astype(jnp.float32)

def node_filter(inverse, weight, current, couplings):
    parts = current.shape[0] // ROWS_DEV
    columns = current.shape[1]
    blocks = inverse.astype(jnp.float32).reshape(2, parts, ROWS_DEV, ROWS_DEV)
    vectors = current.astype(jnp.float32).reshape(parts, ROWS_DEV, columns)
    solved = jnp.einsum('cpij,pjm->cpim', blocks, vectors)
    first_tips = to_half(solved[:, :, :HALF_BAND])
    last_tips = to_half(solved[:, :, -HALF_BAND:])
    empty = jnp.zeros((2, 1, HALF_BAND, columns), jnp.float32)
    from_prior = jnp.concatenate([empty, last_tips[:, :-1]], 1)
    from_next = jnp.concatenate([first_tips[:, 1:], empty], 1)
    prior_coupling = jnp.concatenate([jnp.zeros((1, HALF_BAND, HALF_BAND), jnp.float32), couplings[:-1]], 0)
    edge_top = jnp.einsum('pji,cpjm->cpim', prior_coupling, from_prior, precision=precise)
    edge_bottom = jnp.einsum('pij,cpjm->cpim', couplings, from_next, precision=precise)
    edge_terms = to_half(jnp.concatenate([edge_top, edge_bottom], 2))
    corner = jnp.concatenate([blocks[..., :HALF_BAND], blocks[..., -HALF_BAND:]], 3)
    real_part = solved[0] + jnp.einsum('pij,pjm->pim', corner[0], edge_terms[0]) - jnp.einsum('pij,pjm->pim', corner[1], edge_terms[1])
    imag_part = solved[1] + jnp.einsum('pij,pjm->pim', corner[0], edge_terms[1]) + jnp.einsum('pij,pjm->pim', corner[1], edge_terms[0])
    return (weight[0] * real_part - weight[1] * imag_part).reshape(current.shape)

def reference(subspace, inverse, weights, diag_tiles, upper_tiles):
    order = subspace.shape[0]
    parts = order // ROWS_DEV
    couplings = upper_tiles.reshape(parts, ROWS_DEV, HALF_BAND)[:, -HALF_BAND:, :]
    current = subspace
    history = []
    orthonormal = jnp.zeros(subspace.shape, jnp.float32)
    for iteration in range(ITERS):

        def add_node(total, pair):
            return (total + node_filter(pair[0], pair[1], current, couplings), None)
        start = jnp.zeros(subspace.shape, jnp.float32)
        filtered, unused = lax.scan(add_node, start, (inverse, weights))
        gram_matrix = jnp.dot(filtered.T, filtered, precision=precise) / order
        factor = jnp.linalg.cholesky(gram_matrix)
        orthonormal = jax.scipy.linalg.solve_triangular(factor, filtered.T, lower=True).T
        imaged = band_product(orthonormal, diag_tiles, upper_tiles)
        history.append(jnp.dot(orthonormal.T, imaged, precision=precise) / order)
        current = orthonormal.astype(jnp.bfloat16)
    return (orthonormal, jnp.stack(history))
```

```python
import functools

import jax
import jax.numpy as jnp
from jax import lax
from jax.experimental import pallas as pl
from jax.experimental.pallas import tpu as pltpu
from jax.sharding import PartitionSpec as P

ITERS = 2
GROUP = 8
SEND_TYPES = (jnp.float32, jnp.bfloat16)

precise = lax.Precision.HIGHEST
F32 = jnp.float32
BF16 = jnp.bfloat16


def dot(left, right):
    return jnp.dot(left, right, precision=precise, preferred_element_type=F32)


def dot_tn(left, right):
    dims = (((0,), (0,)), ((), ()))
    return lax.dot_general(left, right, dims, precision=precise, preferred_element_type=F32)


def dot_nt(left, right):
    dims = (((1,), (1,)), ((), ()))
    return lax.dot_general(left, right, dims, precision=precise, preferred_element_type=F32)


def like(shape, dtype=F32):
    return jax.ShapeDtypeStruct(shape, dtype)


def whole(kernel, out_shape, *operands, scratch=(), flops=10**8, specs=None, name=None):
    size = sum(x.size * x.dtype.itemsize for x in operands)
    return pl.pallas_call(
        kernel,
        out_shape=out_shape,
        in_specs=specs or [pl.BlockSpec(memory_space=pltpu.VMEM) for _ in operands],
        scratch_shapes=list(scratch),
        cost_estimate=pl.CostEstimate(flops=flops, bytes_accessed=size, transcendentals=0),
        name=name,
    )(*operands)


def node_swap(block, step):
    count = lax.axis_size("node")
    return lax.ppermute(block, "node", [(i, i ^ step) for i in range(count)])


def core_swap(block):
    count = lax.axis_size("rows")
    return lax.ppermute(block, "rows", [(i, i ^ 1) for i in range(count)])


def link_swap(block):
    count = lax.axis_size("rows")
    pairs = [(i, i + 1) for i in range(1, count - 1, 2)]
    return lax.ppermute(block, "rows", pairs + [(b, a) for a, b in pairs])


def node_spread(blocks):
    return [node_swap(block, step + 1) for step, block in enumerate(blocks)]


def tree_sum(blocks):
    while len(blocks) > 1:
        blocks = [a + b for a, b in zip(blocks[::2], blocks[1::2])]
    return blocks[0]


def chip_sum(block):
    count = lax.axis_size("rows")
    chips = count // 2
    if chips <= 4:
        steps = range(1, chips)
        routes = [[(i, i ^ (2 * s)) for i in range(count)] for s in steps]
        return tree_sum([block] + [lax.ppermute(block, "rows", route) for route in routes])
    step = 2
    while step < count:
        block = block + lax.ppermute(block, "rows", [(i, i ^ step) for i in range(count)])
        step *= 2
    return block


def emit_messages(is_even, first, last, out_a, out_b):
    out_a[...] = jnp.where(is_even, last, first)
    out_b[...] = jnp.where(is_even, first, last)


def solve_kernel(pieces, weights, *refs):
    count = lax.axis_size("node")
    node = lax.axis_index("node")
    is_even = lax.rem(lax.axis_index("rows"), 2) == 0
    step = pl.program_id(0)
    steps = pl.num_programs(0)
    if pieces:
        blocks, (factor, coupling, inverse, base, out_a, out_b, full, head, tip, current) = (
            refs[:count],
            refs[count:],
        )

        @pl.when(step == 0)
        def _():
            size = blocks[0].shape[0]
            for s, block in enumerate(blocks):
                where = pl.multiple_of((node ^ s) * size, 8)
                full[pl.ds(where, size), :] = block[...]
            result = dot_nt(full[...], factor[...])
            full[...] = result
            head[...] = result[: coupling.shape[0]]
            current[...] = result.astype(BF16)

        vectors = current[...]
    else:
        subspace, coupling, inverse, base, out_a, out_b, tip = refs
        vectors = subspace[...]
    band = coupling.shape[0]
    real = jnp.dot(inverse[0, 0], vectors, preferred_element_type=F32)
    imag = jnp.dot(inverse[0, 1], vectors, preferred_element_type=F32)
    base[...] = weights[0, 0] * real - weights[0, 1] * imag

    @pl.when(step == 0)
    def _():
        tip[...] = jnp.concatenate([real[:band], imag[:band]], 1).astype(BF16)

    @pl.when(step == steps - 1)
    def _():
        last = jnp.concatenate([real[-band:], imag[-band:]], 1).astype(BF16)
        last = dot_tn(coupling[...], last.astype(F32)).astype(BF16)
        emit_messages(is_even, tip[...], last, out_a, out_b)


def solve(vectors, factor, weights, upper_tiles, inverse):
    _, _, rows, _ = inverse.shape
    band = upper_tiles.shape[1]
    tile = 2 * band if rows % (2 * band) == 0 else band
    pieces = factor is not None
    vectors = vectors if pieces else [vectors]
    columns = vectors[0].shape[1]
    operands = [weights] + vectors + ([factor] if pieces else []) + [upper_tiles, inverse]
    constant = lambda x: pl.BlockSpec(x.shape, lambda t: (0,) * x.ndim)
    in_specs = (
        [pl.BlockSpec(memory_space=pltpu.SMEM)]
        + [constant(x) for x in vectors]
        + ([constant(factor)] if pieces else [])
        + [
            pl.BlockSpec((band, band), lambda t: (rows // band - 1, 0)),
            pl.BlockSpec((1, 2, tile, rows), lambda t: (0, 0, t, 0)),
        ]
    )
    message = like((band, 2 * columns), BF16)
    outs = [like((rows, columns)), message, message]
    out_specs = [pl.BlockSpec((tile, columns), lambda t: (t, 0)), constant(message), constant(message)]
    scratch = [pltpu.VMEM((band, 2 * columns), BF16)]
    if pieces:
        outs += [like((rows, columns)), like((band, columns))]
        out_specs += [constant(outs[3]), constant(outs[4])]
        scratch += [pltpu.VMEM((rows, columns), BF16)]
    return pl.pallas_call(
        functools.partial(solve_kernel, pieces),
        grid=(rows // tile,),
        in_specs=in_specs,
        out_specs=out_specs,
        out_shape=outs,
        scratch_shapes=scratch,
        cost_estimate=pl.CostEstimate(
            flops=4 * rows * rows * columns, bytes_accessed=inverse.size * 2, transcendentals=0
        ),
        name="solve",
    )(*operands)


def correct_kernel(weights, base, got_a, got_b, coupling, left, right, own, *refs):
    sends, term = refs[:-1], refs[-1]
    node = lax.axis_index("node")
    is_even = lax.rem(lax.axis_index("rows"), 2) == 0
    from_prior = jnp.where(is_even, got_b[...], got_a[...])
    from_next = jnp.where(is_even, got_a[...], got_b[...])
    below = dot(coupling[...], from_next.astype(F32)).astype(BF16)
    product = lambda c: jnp.dot(left[0, c], from_prior, preferred_element_type=F32) + jnp.dot(
        right[0, c], below, preferred_element_type=F32
    )
    real_side, imag_side = product(0), product(1)
    columns = base.shape[1]
    real = real_side[:, :columns] - imag_side[:, columns:]
    imag = real_side[:, columns:] + imag_side[:, :columns]
    term[...] = base[...] + (weights[0, 0] * real - weights[0, 1] * imag)
    size = own.shape[0]
    for s, out in enumerate((own,) + sends):
        where = pl.multiple_of((node ^ s) * size, 8)
        out[...] = term[pl.ds(where, size), :].astype(out.dtype)


def correct(weights, base, got_a, got_b, upper_tiles, inverse, kind):
    rows, columns = base.shape
    band = upper_tiles.shape[1]
    count = lax.axis_size("node")
    size = rows // count
    vmem = pl.BlockSpec(memory_space=pltpu.VMEM)
    outs = [like((size, columns))] + [like((size, columns), kind)] * (count - 1)
    constant = lambda x: pl.BlockSpec(x.shape, lambda t: (0,) * x.ndim)
    return pl.pallas_call(
        correct_kernel,
        grid=(1,),
        in_specs=[
            pl.BlockSpec(memory_space=pltpu.SMEM),
            constant(base),
            constant(got_a),
            constant(got_b),
            pl.BlockSpec((band, band), lambda t: (rows // band - 1, 0)),
            pl.BlockSpec((1, 2, rows, band), lambda t: (0, 0, 0, 0)),
            pl.BlockSpec((1, 2, rows, band), lambda t: (0, 0, 0, rows // band - 1)),
        ],
        out_specs=[constant(x) for x in outs],
        out_shape=outs,
        scratch_shapes=[pltpu.VMEM((rows, columns), F32)],
        cost_estimate=pl.CostEstimate(
            flops=16 * rows * band * columns, bytes_accessed=4 * rows * band * 2, transcendentals=0
        ),
        name="correct",
    )(weights, base, got_a, got_b, upper_tiles, inverse, inverse)


def core_halves(matrix, keep, send):
    half = keep.shape[0]
    core = lax.rem(lax.axis_index("rows"), 2)
    keep[...] = matrix[pl.ds(pl.multiple_of(core * half, 8), half), :]
    send[...] = matrix[pl.ds(pl.multiple_of((1 - core) * half, 8), half), :]


def piece_kernel(*refs):
    *blocks, piece, keep, send, matrix = refs
    total = blocks[0][...]
    for block in blocks[1:]:
        total = total + block[...].astype(F32)
    piece[...] = total
    matrix[...] = dot_tn(total, total)
    core_halves(matrix, keep, send)


def gram_piece(blocks):
    rows, columns = blocks[0].shape
    half = like((columns // 2, columns))
    outs = [like((rows, columns)), half, half]
    scratch = [pltpu.VMEM((columns, columns), F32)]
    return whole(piece_kernel, outs, *blocks, scratch=scratch, name="gram")


def node_slices_kernel(keep, got, own, *refs):
    sends, total = refs[:-1], refs[-1]
    node = lax.axis_index("node")
    total[...] = keep[...] + got[...]
    size = own.shape[0]
    for s, out in enumerate((own,) + sends):
        out[...] = total[pl.ds(pl.multiple_of((node ^ s) * size, 8), size), :]


def node_slices(keep, got):
    rows, columns = keep.shape
    count = lax.axis_size("node")
    outs = [like((rows // count, columns))] * count
    return whole(node_slices_kernel, outs, keep, got, scratch=[pltpu.VMEM(keep.shape, F32)], name="slices")


def join_kernel(*refs):
    *blocks, out = refs
    node = lax.axis_index("node")
    size = blocks[0].shape[0]
    for s, block in enumerate(blocks):
        out[pl.ds(pl.multiple_of((node ^ s) * size, 8), size), :] = block[...]


def node_join(blocks):
    rows, columns = blocks[0].shape
    return whole(join_kernel, like((rows * len(blocks), columns)), *blocks, name="join")


def join_cores(first, second, out):
    half = first.shape[0]
    core = lax.rem(lax.axis_index("rows"), 2)
    out[pl.ds(pl.multiple_of(core * half, 8), half), :] = first[...]
    out[pl.ds(pl.multiple_of((1 - core) * half, 8), half), :] = second[...]


def eliminate(block, out, base):
    count = block.shape[0]
    full = (GROUP, count)
    lane = lax.broadcasted_iota(jnp.int32, full, 1)
    span = range(GROUP)
    tiles = [block[t * GROUP : (t + 1) * GROUP] for t in range(count // GROUP)]
    for t, tile in enumerate(tiles):
        k = t * GROUP
        tile = tiles[t]
        rows = [jnp.broadcast_to(tile[i : i + 1], full) for i in span]
        pivot = [[jnp.broadcast_to(rows[i][:, k + j : k + j + 1], full) for j in range(i + 1)] for i in span]
        scale = []
        low = [[None] * GROUP for _ in span]
        for j in span:
            scale.append(lax.rsqrt(pivot[j][j]))
            for i in range(j + 1, GROUP):
                low[i][j] = pivot[i][j] * scale[j]
            for i in range(j + 1, GROUP):
                for m in range(j + 1, i + 1):
                    pivot[i][m] = pivot[i][m] - low[i][j] * low[m][j]
        inv = [[None] * GROUP for _ in span]
        for j in span:
            inv[j][j] = scale[j]
            for i in range(j + 1, GROUP):
                total = low[i][j] * inv[j][j]
                for m in range(j + 1, i):
                    total = total + low[i][m] * inv[m][j]
                inv[i][j] = -total * scale[i]
        inside = (lane >= k) & (lane < k + GROUP)
        rows = [jnp.where(inside, jnp.where(lane == k + i, 1.0, 0.0), rows[i]) for i in span]
        done = []
        for i in span:
            total = inv[i][0] * rows[0]
            for j in range(1, i + 1):
                total = total + inv[i][j] * rows[j]
            done.append(total)
            at = base + k + i
            out[at : at + 1, base : base + count] = jnp.where(lane < k + GROUP, total, 0.0)[:1]
        if t + 1 < len(tiles):
            back = []
            for j in span:
                total = inv[j][j] * done[j]
                for i in range(j + 1, GROUP):
                    total = total + inv[i][j] * done[i]
                back.append(total)
            for u in range(t + 1, len(tiles)):
                old = tiles[u]
                new = jnp.where(inside, 0.0, old)
                for j in span:
                    new = new - old[:, k + j : k + j + 1] * back[j]
                tiles[u] = new


def factor_kernel(order, first, second, out, matrix):
    join_cores(first, second, matrix)
    count = matrix.shape[0]
    half = count // 2
    values = matrix[...] * (1.0 / order)
    eye = lax.broadcasted_iota(jnp.int32, (count, count), 0) == lax.broadcasted_iota(
        jnp.int32, (count, count), 1
    )
    diagonal = jnp.where(eye, values, 0.0)
    across = lax.rsqrt(jnp.sum(diagonal, 0, keepdims=True))
    down = lax.rsqrt(jnp.sum(diagonal, 1, keepdims=True))
    values = values * across * down
    out[:half, half:] = jnp.zeros((half, count - half), F32)
    eliminate(values[:half, :half], out, 0)
    top = out[:half, :half]
    beside = dot(top, values[:half, half:])
    corner = dot_tn(beside, top)
    eliminate(values[half:, half:] - dot_tn(beside, beside), out, half)
    out[half:, :half] = -dot(out[half:, half:], corner)
    out[...] = out[...] * across


def inverse_factor(halves, order):
    columns = halves[0].shape[1]
    return whole(
        functools.partial(factor_kernel, order),
        like((columns, columns)),
        *halves,
        scratch=[pltpu.VMEM((columns, columns), F32)],
        name="factor",
    )


def sum_halves(keep, send):
    slices = node_slices(keep, core_swap(send))
    total = tree_sum([slices[0]] + node_spread(slices[1:]))
    return gather_halves(chip_sum(total))


def gather_halves(block):
    half = node_join([block] + node_spread([block] * (lax.axis_size("node") - 1)))
    return half, core_swap(half)


def next_head(head):
    count = lax.axis_size("rows")
    return lax.ppermute(head, "rows", [(i + 1, i) for i in range(count - 1)])


def band_kernel(field, after, diag_tiles, upper_tiles, keep, send, image, matrix):
    band = after.shape[0]
    tiles = field.shape[0] // band
    for t in range(tiles):
        at = slice(t * band, (t + 1) * band)
        following = after[...] if t == tiles - 1 else field[(t + 1) * band : (t + 2) * band]
        image[at] = 0.5 * dot(diag_tiles[at], field[at]) + dot(upper_tiles[at], following)
    matrix[...] = dot_tn(field[...], image[...])
    size = keep.shape[0]
    half = matrix.shape[0] // 2
    node = lax.axis_index("node")
    core = lax.rem(lax.axis_index("rows"), 2)
    keep[...] = matrix[pl.ds(pl.multiple_of(core * half + node * size, 8), size), :]
    send[...] = matrix[pl.ds(pl.multiple_of((1 - core) * half + node * size, 8), size), :]


def band_slices(field, after, diag_tiles, upper_tiles):
    rows, columns = field.shape
    part = like((columns // 2 // lax.axis_size("node"), columns))
    return whole(
        band_kernel,
        [part, part],
        field,
        after,
        diag_tiles,
        upper_tiles,
        scratch=[pltpu.VMEM((rows, columns), F32), pltpu.VMEM((columns, columns), F32)],
        name="band",
    )


def last_kernel(field, factor, out):
    out[...] = dot_nt(field[...], factor[...])


def projected_kernel(order, first, second, factor, out, matrix):
    columns = factor.shape[0]
    half = columns // 2
    core = lax.rem(lax.axis_index("rows"), 2)
    size = first.shape[0] // lax.axis_size("node") // ITERS
    for ref, place in ((first, core), (second, 1 - core)):
        for j in range(half // size):
            for k in range(ITERS):
                at = pl.multiple_of(place * half + j * size, 8)
                start = (j * ITERS + k) * size
                matrix[k, pl.ds(at, size), :] = ref[start : start + size]
    scale = 1.0 / order
    for k in range(ITERS):
        value = matrix[k]
        if k == ITERS - 1:
            value = dot_nt(dot(factor[...], value), factor[...])
        out[k] = (value + value.T) * scale


def per_device(subspace, inverse, weights, diag_tiles, upper_tiles):
    order = float(subspace.shape[0] * lax.axis_size("rows"))
    factor, blocks = None, subspace
    kept, sent = [], []
    for iteration in range(ITERS):
        base, out_a, out_b, *rest = solve(blocks, factor, weights, upper_tiles, inverse)
        if iteration > 0:
            field, head = rest
            keep, send = band_slices(field, next_head(head), diag_tiles, upper_tiles)
            kept.append(keep)
            sent.append(send)
        got_a, got_b = core_swap(out_a), link_swap(out_b)
        own, *others = correct(
            weights, base, got_a, got_b, upper_tiles, inverse, SEND_TYPES[iteration]
        )
        piece, keep, send = gram_piece([own] + node_spread(others))
        blocks = [piece] + node_spread([piece] * len(others))
        factor = inverse_factor(sum_halves(keep, send), order)
    field = node_join(blocks)
    head = field[: diag_tiles.shape[1]]
    keep, send = band_slices(field, next_head(head), diag_tiles, upper_tiles)
    kept.append(keep)
    sent.append(send)
    part = jnp.concatenate(kept, 0) + core_swap(jnp.concatenate(sent, 0))
    halves = gather_halves(chip_sum(part))
    columns = subspace.shape[1]
    orthonormal = whole(last_kernel, like(subspace.shape), field, factor, name="last")
    projected = whole(
        functools.partial(projected_kernel, order),
        like((ITERS, columns, columns)),
        *halves,
        factor,
        scratch=[pltpu.VMEM((ITERS, columns, columns), F32)],
        name="projected",
    )
    return orthonormal, projected


def solution(mesh):
    placed = (
        P("rows", None),
        P("node", None, "rows", None),
        P("node", None),
        P("rows", None),
        P("rows", None),
    )
    return jax.shard_map(
        per_device, mesh=mesh, in_specs=placed, out_specs=(P("rows", None), P()), check_vma=False
    )
```

```python
import functools

import jax
import jax.numpy as jnp
from jax import lax
from jax.experimental import pallas as pl
from jax.experimental.pallas import tpu as pltpu
from jax.sharding import PartitionSpec as P


ITERS = 2
GROUP = 8
SEND_TYPES = (jnp.float32, jnp.bfloat16)

precise = lax.Precision.HIGHEST
F32 = jnp.float32
BF16 = jnp.bfloat16


def dot(left, right):
    return jnp.dot(left, right, precision=precise, preferred_element_type=F32)


def dot_tn(left, right):
    dims = (((0,), (0,)), ((), ()))
    return lax.dot_general(left, right, dims, precision=precise, preferred_element_type=F32)


def dot_nt(left, right):
    dims = (((1,), (1,)), ((), ()))
    return lax.dot_general(left, right, dims, precision=precise, preferred_element_type=F32)


def like(shape, dtype=F32):
    return jax.ShapeDtypeStruct(shape, dtype)


def whole(kernel, out_shape, *operands, scratch=(), flops=10**8, specs=None):
    size = sum(x.size * x.dtype.itemsize for x in operands)
    return pl.pallas_call(
        kernel,
        out_shape=out_shape,
        in_specs=specs or [pl.BlockSpec(memory_space=pltpu.VMEM) for _ in operands],
        scratch_shapes=list(scratch),
        cost_estimate=pl.CostEstimate(flops=flops, bytes_accessed=size, transcendentals=0),
    )(*operands)


def node_swap(block, step):
    count = lax.axis_size("node")
    return lax.ppermute(block, "node", [(i, i ^ step) for i in range(count)])


def core_swap(block):
    count = lax.axis_size("rows")
    return lax.ppermute(block, "rows", [(i, i ^ 1) for i in range(count)])


def link_swap(block):
    count = lax.axis_size("rows")
    pairs = [(i, i + 1) for i in range(1, count - 1, 2)]
    return lax.ppermute(block, "rows", pairs + [(b, a) for a, b in pairs])


def node_spread(blocks):
    return [node_swap(block, step + 1) for step, block in enumerate(blocks)]


def tree_sum(blocks):
    while len(blocks) > 1:
        odd = blocks[len(blocks) // 2 * 2 :]
        blocks = [a + b for a, b in zip(blocks[::2], blocks[1::2])] + odd
    return blocks[0]


def chip_sum(block):
    count = lax.axis_size("rows")
    chips = count // 2
    if chips <= 4:
        steps = range(1, chips)
        routes = [[(i, i ^ (2 * s)) for i in range(count)] for s in steps]
        return tree_sum([block] + [lax.ppermute(block, "rows", route) for route in routes])
    step = 2
    while step < count:
        block = block + lax.ppermute(block, "rows", [(i, i ^ step) for i in range(count)])
        step *= 2
    return block


def solve_kernel(refine, weights, vectors, *refs):
    is_even = lax.rem(lax.axis_index("rows"), 2) == 0
    step = pl.program_id(0)
    steps = pl.num_programs(0)
    if refine:
        factor, coupling, inverse, base, out_a, out_b, tip, current = refs

        @pl.when(step == 0)
        def _():
            current[...] = dot_nt(vectors[...], factor[...]).astype(BF16)

    else:
        coupling, inverse, base, out_a, out_b, tip = refs
        current = vectors
    band = coupling.shape[0]
    real = jnp.dot(inverse[0, 0], current[...], preferred_element_type=F32)
    imag = jnp.dot(inverse[0, 1], current[...], preferred_element_type=F32)
    base[...] = weights[0, 0] * real - weights[0, 1] * imag

    @pl.when(step == 0)
    def _():
        tip[...] = jnp.concatenate([real[:band], imag[:band]], 1).astype(BF16)

    @pl.when(step == steps - 1)
    def _():
        last = jnp.concatenate([real[-band:], imag[-band:]], 1).astype(BF16)
        last = dot_tn(coupling[...], last.astype(F32)).astype(BF16)
        out_a[...] = jnp.where(is_even, last, tip[...])
        out_b[...] = jnp.where(is_even, tip[...], last)


def solve(vectors, factor, weights, upper_tiles, inverse):
    rows, columns = vectors.shape
    band = upper_tiles.shape[1]
    tile = 2 * band if rows % (2 * band) == 0 else band
    refine = factor is not None
    constant = lambda x: pl.BlockSpec(x.shape, lambda t: (0,) * x.ndim)
    in_specs = [pl.BlockSpec(memory_space=pltpu.SMEM), constant(vectors)]
    operands = [weights, vectors]
    if refine:
        in_specs.append(constant(factor))
        operands.append(factor)
    in_specs += [
        pl.BlockSpec((band, band), lambda t: (rows // band - 1, 0)),
        pl.BlockSpec((1, 2, tile, rows), lambda t: (0, 0, t, 0)),
    ]
    message = like((band, 2 * columns), BF16)
    outs = [like((rows, columns)), message, message]
    out_specs = [pl.BlockSpec((tile, columns), lambda t: (t, 0)), constant(message), constant(message)]
    scratch = [pltpu.VMEM((band, 2 * columns), BF16)]
    if refine:
        scratch += [pltpu.VMEM((rows, columns), BF16)]
    return pl.pallas_call(
        functools.partial(solve_kernel, refine),
        grid=(rows // tile,),
        in_specs=in_specs,
        out_specs=out_specs,
        out_shape=outs,
        scratch_shapes=scratch,
        cost_estimate=pl.CostEstimate(
            flops=4 * rows * rows * columns, bytes_accessed=inverse.size * 2, transcendentals=0
        ),
        name="solve",
    )(*operands, upper_tiles, inverse)


def correct_kernel(weights, base, got_a, got_b, coupling, left, right, own, *refs):
    sends, term = refs[:-1], refs[-1]
    node = lax.axis_index("node")
    is_even = lax.rem(lax.axis_index("rows"), 2) == 0
    from_prior = jnp.where(is_even, got_b[...], got_a[...])
    from_next = jnp.where(is_even, got_a[...], got_b[...])
    below = dot(coupling[...], from_next.astype(F32)).astype(BF16)
    product = lambda c: jnp.dot(left[0, c], from_prior, preferred_element_type=F32) + jnp.dot(
        right[0, c], below, preferred_element_type=F32
    )
    real_side, imag_side = product(0), product(1)
    columns = base.shape[1]
    real = real_side[:, :columns] - imag_side[:, columns:]
    imag = real_side[:, columns:] + imag_side[:, :columns]
    term[...] = base[...] + (weights[0, 0] * real - weights[0, 1] * imag)
    size = own.shape[0]
    for s, out in enumerate((own,) + sends):
        where = pl.multiple_of((node ^ s) * size, 8)
        out[...] = term[pl.ds(where, size), :].astype(out.dtype)


def correct(weights, base, got_a, got_b, upper_tiles, inverse, kind):
    rows, columns = base.shape
    band = upper_tiles.shape[1]
    count = lax.axis_size("node")
    size = rows // count
    vmem = pl.BlockSpec(memory_space=pltpu.VMEM)
    outs = [like((size, columns))] + [like((size, columns), kind)] * (count - 1)
    constant = lambda x: pl.BlockSpec(x.shape, lambda t: (0,) * x.ndim)
    return pl.pallas_call(
        correct_kernel,
        grid=(1,),
        in_specs=[
            pl.BlockSpec(memory_space=pltpu.SMEM),
            constant(base),
            constant(got_a),
            constant(got_b),
            pl.BlockSpec((band, band), lambda t: (rows // band - 1, 0)),
            pl.BlockSpec((1, 2, rows, band), lambda t: (0, 0, 0, 0)),
            pl.BlockSpec((1, 2, rows, band), lambda t: (0, 0, 0, rows // band - 1)),
        ],
        out_specs=[constant(x) for x in outs],
        out_shape=outs,
        scratch_shapes=[pltpu.VMEM((rows, columns), F32)],
        cost_estimate=pl.CostEstimate(
            flops=16 * rows * band * columns, bytes_accessed=4 * rows * band * 2, transcendentals=0
        ),
        name="correct",
    )(weights, base, got_a, got_b, upper_tiles, inverse, inverse)


def place(blocks, out):
    node = lax.axis_index("node")
    size = blocks[0].shape[0]
    for step, block in enumerate(blocks):
        out[pl.ds(pl.multiple_of((node ^ step) * size, 8), size), :] = block[...]


def gram_kernel(*refs):
    *blocks, field, head, part, matrix = refs
    place(blocks, field)
    head[...] = field[: head.shape[0]]
    matrix[...] = dot_tn(field[...], field[...])
    size = part.shape[0]
    part[...] = matrix[pl.ds(pl.multiple_of(lax.axis_index("node") * size, 8), size), :]


def gram_slice(blocks, band):
    rows, columns = blocks[0].shape
    count = len(blocks)
    outs = [like((rows * count, columns)), like((band, columns)), like((columns // count, columns))]
    scratch = [pltpu.VMEM((columns, columns), F32)]
    return whole(gram_kernel, outs, *blocks, scratch=scratch)


def eliminate(block, out, base):
    count = block.shape[0]
    full = (GROUP, count)
    lane = lax.broadcasted_iota(jnp.int32, full, 1)
    span = range(GROUP)
    tiles = [block[t * GROUP : (t + 1) * GROUP] for t in range(count // GROUP)]
    for t, tile in enumerate(tiles):
        k = t * GROUP
        tile = tiles[t]
        rows = [jnp.broadcast_to(tile[i : i + 1], full) for i in span]
        pivot = [[jnp.broadcast_to(rows[i][:, k + j : k + j + 1], full) for j in range(i + 1)] for i in span]
        scale = []
        low = [[None] * GROUP for _ in span]
        for j in span:
            scale.append(lax.rsqrt(pivot[j][j]))
            for i in range(j + 1, GROUP):
                low[i][j] = pivot[i][j] * scale[j]
            for i in range(j + 1, GROUP):
                for m in range(j + 1, i + 1):
                    pivot[i][m] = pivot[i][m] - low[i][j] * low[m][j]
        inv = [[None] * GROUP for _ in span]
        for j in span:
            inv[j][j] = scale[j]
            for i in range(j + 1, GROUP):
                total = low[i][j] * inv[j][j]
                for m in range(j + 1, i):
                    total = total + low[i][m] * inv[m][j]
                inv[i][j] = -total * scale[i]
        inside = (lane >= k) & (lane < k + GROUP)
        rows = [jnp.where(inside, jnp.where(lane == k + i, 1.0, 0.0), rows[i]) for i in span]
        done = []
        for i in span:
            total = inv[i][0] * rows[0]
            for j in range(1, i + 1):
                total = total + inv[i][j] * rows[j]
            done.append(total)
            at = base + k + i
            out[at : at + 1, base : base + count] = jnp.where(lane < k + GROUP, total, 0.0)[:1]
        if t + 1 < len(tiles):
            back = []
            for j in span:
                total = inv[j][j] * done[j]
                for i in range(j + 1, GROUP):
                    total = total + inv[i][j] * done[i]
                back.append(total)
            for u in range(t + 1, len(tiles)):
                old = tiles[u]
                new = jnp.where(inside, 0.0, old)
                for j in span:
                    new = new - old[:, k + j : k + j + 1] * back[j]
                tiles[u] = new


def first_factor_kernel(order, *refs):
    *blocks, top, corner, rest, across, matrix = refs
    place(blocks, matrix)
    count = matrix.shape[0]
    half = count // 2
    values = matrix[...] * (1.0 / order)
    eye = lax.broadcasted_iota(jnp.int32, (count, count), 0) == lax.broadcasted_iota(
        jnp.int32, (count, count), 1
    )
    diagonal = jnp.where(eye, values, 0.0)
    scale = lax.rsqrt(jnp.sum(diagonal, 0, keepdims=True))
    down = lax.rsqrt(jnp.sum(diagonal, 1, keepdims=True))
    across[...] = scale
    values = values * scale * down
    eliminate(values[:half, :half], top, 0)
    beside = dot(top[...], values[:half, half:])
    corner[...] = dot_tn(beside, top[...])
    rest[...] = values[half:, half:] - dot_tn(beside, beside)


def second_factor_kernel(top, corner, rest, across, out):
    half = top.shape[0]
    out[:half, :half] = top[...]
    out[:half, half:] = jnp.zeros((half, half), F32)
    eliminate(rest[...], out, half)
    out[half:, :half] = -dot(out[half:, half:], corner[...])
    out[...] = out[...] * across[...]


def first_factor(blocks, order):
    columns = blocks[0].shape[1]
    half = like((columns // 2, columns // 2))
    return whole(
        functools.partial(first_factor_kernel, order),
        [half, half, half, like((1, columns))],
        *blocks,
        scratch=[pltpu.VMEM((columns, columns), F32)],
        flops=6 * 10**9,
    )


def second_factor(halves):
    columns = halves[3].shape[1]
    return whole(second_factor_kernel, like((columns, columns)), *halves, flops=6 * 10**9)


def next_head(head):
    count = lax.axis_size("rows")
    return lax.ppermute(head, "rows", [(i + 1, i) for i in range(count - 1)])


def band_kernel(field, after, diag_tiles, upper_tiles, part, image, matrix):
    band = after.shape[0]
    tiles = field.shape[0] // band
    for t in range(tiles):
        at = slice(t * band, (t + 1) * band)
        following = after[...] if t == tiles - 1 else field[(t + 1) * band : (t + 2) * band]
        image[at] = 0.5 * dot(diag_tiles[at], field[at]) + dot(upper_tiles[at], following)
    matrix[...] = dot_tn(field[...], image[...])
    size = part.shape[0]
    part[...] = matrix[pl.ds(pl.multiple_of(lax.axis_index("node") * size, 8), size), :]


def band_slice(field, after, diag_tiles, upper_tiles):
    rows, columns = field.shape
    return whole(
        band_kernel,
        like((columns // lax.axis_size("node"), columns)),
        field,
        after,
        diag_tiles,
        upper_tiles,
        scratch=[pltpu.VMEM((rows, columns), F32), pltpu.VMEM((columns, columns), F32)],
    )


def last_kernel(field, factor, out):
    out[...] = dot_nt(field[...], factor[...])


def projected_kernel(order, *refs):
    blocks, factors, (out, matrix) = refs[: -2 - ITERS], refs[-2 - ITERS : -2], refs[-2:]
    node = lax.axis_index("node")
    size = blocks[0].shape[0] // ITERS
    for k, factor in enumerate(factors):
        for step, block in enumerate(blocks):
            at = pl.multiple_of((node ^ step) * size, 8)
            matrix[pl.ds(at, size), :] = block[k * size : (k + 1) * size]
        value = dot_nt(dot(factor[...], matrix[...]), factor[...])
        out[k] = (value + value.T) * (1.0 / order)


def after(value, *others):
    return lax.optimization_barrier((value,) + others)[0]


def per_device(subspace, inverse, weights, diag_tiles, upper_tiles):
    order = float(subspace.shape[0] * lax.axis_size("rows"))
    band = upper_tiles.shape[1]
    partners = lax.axis_size("node") - 1
    columns = subspace.shape[1]
    factor, field = None, subspace
    factors, parts = [], []
    for iteration in range(ITERS):
        base, out_a, out_b = solve(field, factor, weights, upper_tiles, inverse)
        got_a, got_b = core_swap(out_a), link_swap(out_b)
        own, *others = correct(
            weights, base, got_a, got_b, upper_tiles, inverse, SEND_TYPES[iteration]
        )
        piece = tree_sum([own] + [x.astype(F32) for x in node_spread(others)])
        field, head, part = gram_slice([piece] + node_spread([piece] * partners), band)
        part = part + core_swap(part)
        following = next_head(after(head, part))
        total = chip_sum(part)
        gathered = [total] + node_spread([total] * partners)
        parts.append(band_slice(field, after(following, total), diag_tiles, upper_tiles))
        halves = first_factor(gathered, order)
        if iteration == ITERS - 1:
            pair = jnp.concatenate(parts, 0)
            pair = after(pair + core_swap(pair), *gathered)
            pair = chip_sum(pair)
            pair = after(pair, *halves)
            spread = [pair] + node_spread([pair] * partners)
        factor = second_factor(halves)
        factors.append(factor)
    orthonormal = whole(last_kernel, like(subspace.shape), field, factor)
    projected = whole(
        functools.partial(projected_kernel, order),
        like((ITERS, columns, columns)),
        *spread,
        *factors,
        scratch=[pltpu.VMEM((columns, columns), F32)],
    )
    return orthonormal, projected


def solution(mesh):
    placed = (
        P("rows", None),
        P("node", None, "rows", None),
        P("node", None),
        P("rows", None),
        P("rows", None),
    )
    return jax.shard_map(
        per_device, mesh=mesh, in_specs=placed, out_specs=(P("rows", None), P()), check_vma=False
    )
```

```python
import functools

import jax
import jax.numpy as jnp
from jax import lax
from jax.experimental import pallas as pl
from jax.experimental.pallas import tpu as pltpu
from jax.sharding import PartitionSpec as P


ITERS = 2
GROUP = 8
TERM_TYPES = (jnp.float32, jnp.bfloat16)
FIELD_TYPES = (jnp.float32, jnp.bfloat16)

precise = lax.Precision.HIGHEST
F32 = jnp.float32
BF16 = jnp.bfloat16


def dot(left, right):
    return jnp.dot(left, right, precision=precise, preferred_element_type=F32)


def dot_tn(left, right):
    dims = (((0,), (0,)), ((), ()))
    return lax.dot_general(left, right, dims, precision=precise, preferred_element_type=F32)


def halves_of(value):
    high = value.astype(BF16)
    return high, (value - high.astype(F32)).astype(BF16)


def dot_three(left, right, dims=(((1,), (0,)), ((), ()))):
    times = lambda a, b: lax.dot_general(a, b, dims, preferred_element_type=F32)
    (a, b), (c, d) = halves_of(left), halves_of(right)
    return times(a, c) + (times(a, d) + times(b, c))


def dot_two(left, right, dims=(((1,), (0,)), ((), ()))):
    times = lambda a, b: lax.dot_general(a, b, dims, preferred_element_type=F32)
    c, d = halves_of(right)
    return times(left, c) + times(left, d)


NT = (((1,), (1,)), ((), ()))
TN = (((0,), (0,)), ((), ()))


def like(shape, dtype=F32):
    return jax.ShapeDtypeStruct(shape, dtype)


def whole(kernel, out_shape, *operands, scratch=(), flops=10**8):
    size = sum(x.size * x.dtype.itemsize for x in operands)
    return pl.pallas_call(
        kernel,
        out_shape=out_shape,
        in_specs=[
            pl.BlockSpec(memory_space=pltpu.SMEM if x.size < 64 else pltpu.VMEM) for x in operands
        ],
        scratch_shapes=list(scratch),
        cost_estimate=pl.CostEstimate(flops=flops, bytes_accessed=size, transcendentals=0),
    )(*operands)


def node_swap(block, step):
    count = lax.axis_size("node")
    return lax.ppermute(block, "node", [(i, i ^ step) for i in range(count)])


def core_swap(block):
    count = lax.axis_size("rows")
    return lax.ppermute(block, "rows", [(i, i ^ 1) for i in range(count)])


def link_swap(block):
    count = lax.axis_size("rows")
    pairs = [(i, i + 1) for i in range(1, count - 1, 2)]
    return lax.ppermute(block, "rows", pairs + [(b, a) for a, b in pairs])


def node_spread(blocks):
    return [node_swap(block, step + 1) for step, block in enumerate(blocks)]


def tree_sum(blocks):
    while len(blocks) > 1:
        odd = blocks[len(blocks) // 2 * 2 :]
        blocks = [a + b for a, b in zip(blocks[::2], blocks[1::2])] + odd
    return blocks[0]


def chip_sum(block):
    count = lax.axis_size("rows")
    chips = count // 2
    if chips <= 4:
        steps = range(1, chips)
        routes = [[(i, i ^ (2 * s)) for i in range(count)] for s in steps]
        return tree_sum([block] + [lax.ppermute(block, "rows", route) for route in routes])
    step = 2
    while step < count:
        block = block + lax.ppermute(block, "rows", [(i, i ^ step) for i in range(count)])
        step *= 2
    return block


def emit_messages(is_even, first, last, out_a, out_b):
    out_a[...] = jnp.where(is_even, last, first)
    out_b[...] = jnp.where(is_even, first, last)


def emit_messages(real, imag, coupling, tip, out_a, out_b):
    band = coupling.shape[0]
    is_even = lax.rem(lax.axis_index("rows"), 2) == 0
    last = jnp.concatenate([real[-band:], imag[-band:]], 1).astype(BF16)
    last = dot_tn(coupling, last.astype(F32)).astype(BF16)
    out_a[...] = jnp.where(is_even, last, tip)
    out_b[...] = jnp.where(is_even, tip, last)


def tip_of(real, imag, band):
    return jnp.concatenate([real[:band], imag[:band]], 1).astype(BF16)


def start_kernel(weights, vectors, coupling, inverse, base, out_a, out_b, tip):
    step = pl.program_id(0)
    real = jnp.dot(inverse[0, 0], vectors[...], preferred_element_type=F32)
    imag = jnp.dot(inverse[0, 1], vectors[...], preferred_element_type=F32)
    base[...] = weights[0, 0] * real - weights[0, 1] * imag

    @pl.when(step == 0)
    def _():
        tip[...] = tip_of(real, imag, coupling.shape[0])

    @pl.when(step == pl.num_programs(0) - 1)
    def _():
        emit_messages(real, imag, coupling[...], tip[...], out_a, out_b)


def start(vectors, weights, upper_tiles, inverse):
    rows, columns = vectors.shape
    band = upper_tiles.shape[1]
    tile = 2 * band if rows % (2 * band) == 0 else band
    constant = lambda x: pl.BlockSpec(x.shape, lambda t: (0,) * x.ndim)
    message = like((band, 2 * columns), BF16)
    return pl.pallas_call(
        start_kernel,
        grid=(rows // tile,),
        in_specs=[
            pl.BlockSpec(memory_space=pltpu.SMEM),
            constant(vectors),
            pl.BlockSpec((band, band), lambda t: (rows // band - 1, 0)),
            pl.BlockSpec((1, 2, tile, rows), lambda t: (0, 0, t, 0)),
        ],
        out_specs=[
            pl.BlockSpec((tile, columns), lambda t: (t, 0)),
            constant(message),
            constant(message),
        ],
        out_shape=[like((rows, columns)), message, message],
        scratch_shapes=[pltpu.VMEM((band, 2 * columns), BF16)],
        cost_estimate=pl.CostEstimate(
            flops=4 * rows * rows * columns, bytes_accessed=inverse.size * 2, transcendentals=0
        ),
        name="start",
    )(weights, vectors, upper_tiles, inverse)


def solve_kernel(weights, field, factor, upper_tiles, inverse, base, out_a, out_b, tip, current):
    band = upper_tiles.shape[1]
    rows = field.shape[0]
    current[...] = dot_three(field[...], factor[...], NT).astype(BF16)
    tile = 2 * band if rows % (2 * band) == 0 else band
    for at in range(0, rows, tile):
        real = jnp.dot(inverse[0, 0, at : at + tile], current[...], preferred_element_type=F32)
        imag = jnp.dot(inverse[0, 1, at : at + tile], current[...], preferred_element_type=F32)
        base[at : at + tile] = weights[0, 0] * real - weights[0, 1] * imag
        if at == 0:
            tip[...] = tip_of(real, imag, band)
    emit_messages(real, imag, upper_tiles[-band:], tip[...], out_a, out_b)


def solve(field, factor, weights, upper_tiles, inverse):
    rows, columns = field.shape
    band = upper_tiles.shape[1]
    message = like((band, 2 * columns), BF16)
    return whole(
        solve_kernel,
        [like((rows, columns)), message, message],
        weights,
        field,
        factor,
        upper_tiles,
        inverse,
        scratch=[pltpu.VMEM((band, 2 * columns), BF16), pltpu.VMEM((rows, columns), BF16)],
        flops=4 * rows * rows * columns,
    )


def correct_kernel(weights, base, got_a, got_b, upper_tiles, inverse, own, *refs):
    sends, term = refs[:-1], refs[-1]
    band = upper_tiles.shape[1]
    rows, columns = base.shape
    node = lax.axis_index("node")
    is_even = lax.rem(lax.axis_index("rows"), 2) == 0
    above = jnp.where(is_even, got_b[...], got_a[...])
    from_next = jnp.where(is_even, got_a[...], got_b[...])
    below = dot(upper_tiles[-band:], from_next.astype(F32)).astype(BF16)
    total = base[...]
    for edge, columns_at in ((above, 0), (below, rows - band)):
        real, imag = edge[:, :columns].astype(F32), edge[:, columns:].astype(F32)
        part = slice(columns_at, columns_at + band)
        total = total + dot_two(inverse[0, 0, :, part], weights[0, 0] * real - weights[0, 1] * imag)
        total = total - dot_two(inverse[0, 1, :, part], weights[0, 0] * imag + weights[0, 1] * real)
    term[...] = total
    size = own.shape[0]
    for s, out in enumerate((own,) + sends):
        where = pl.multiple_of((node ^ s) * size, 8)
        out[...] = term[pl.ds(where, size), :].astype(out.dtype)


def correct(weights, base, got_a, got_b, upper_tiles, inverse, kind):
    rows, columns = base.shape
    band = upper_tiles.shape[1]
    count = lax.axis_size("node")
    size = rows // count
    outs = [like((size, columns))] + [like((size, columns), kind)] * (count - 1)
    return whole(
        correct_kernel,
        outs,
        weights,
        base,
        got_a,
        got_b,
        upper_tiles,
        inverse,
        scratch=[pltpu.VMEM((rows, columns), F32)],
        flops=16 * rows * band * columns,
    )


def place(blocks, out):
    node = lax.axis_index("node")
    size = blocks[0].shape[0]
    for step, block in enumerate(blocks):
        out[pl.ds(pl.multiple_of((node ^ step) * size, 8), size), :] = block[...]


def gram_kernel(*refs):
    *blocks, field, head, part, matrix = refs
    place(blocks, field)
    head[...] = field[: head.shape[0]]
    if field.dtype == BF16:
        matrix[...] = lax.dot_general(field[...], field[...], TN, preferred_element_type=F32)
    else:
        matrix[...] = dot_tn(field[...], field[...])
    size = part.shape[0]
    part[...] = matrix[pl.ds(pl.multiple_of(lax.axis_index("node") * size, 8), size), :]


def gram_slice(blocks, band):
    rows, columns = blocks[0].shape
    count = len(blocks)
    kind = blocks[0].dtype
    outs = [
        like((rows * count, columns), kind),
        like((band, columns), kind),
        like((columns // count, columns)),
    ]
    scratch = [pltpu.VMEM((columns, columns), F32)]
    return whole(gram_kernel, outs, *blocks, scratch=scratch)


def eliminate(block, out, base):
    count = block.shape[0]
    full = (GROUP, count)
    lane = lax.broadcasted_iota(jnp.int32, full, 1)
    span = range(GROUP)
    tiles = [block[t * GROUP : (t + 1) * GROUP] for t in range(count // GROUP)]
    for t, tile in enumerate(tiles):
        k = t * GROUP
        tile = tiles[t]
        rows = [jnp.broadcast_to(tile[i : i + 1], full) for i in span]
        pivot = [[jnp.broadcast_to(rows[i][:, k + j : k + j + 1], full) for j in range(i + 1)] for i in span]
        scale = []
        low = [[None] * GROUP for _ in span]
        for j in span:
            scale.append(lax.rsqrt(pivot[j][j]))
            for i in range(j + 1, GROUP):
                low[i][j] = pivot[i][j] * scale[j]
            for i in range(j + 1, GROUP):
                for m in range(j + 1, i + 1):
                    pivot[i][m] = pivot[i][m] - low[i][j] * low[m][j]
        inv = [[None] * GROUP for _ in span]
        for j in span:
            inv[j][j] = scale[j]
            for i in range(j + 1, GROUP):
                total = low[i][j] * inv[j][j]
                for m in range(j + 1, i):
                    total = total + low[i][m] * inv[m][j]
                inv[i][j] = -total * scale[i]
        inside = (lane >= k) & (lane < k + GROUP)
        rows = [jnp.where(inside, jnp.where(lane == k + i, 1.0, 0.0), rows[i]) for i in span]
        done = []
        for i in span:
            total = inv[i][0] * rows[0]
            for j in range(1, i + 1):
                total = total + inv[i][j] * rows[j]
            done.append(total)
            at = base + k + i
            out[at : at + 1, base : base + count] = jnp.where(lane < k + GROUP, total, 0.0)[:1]
        if t + 1 < len(tiles):
            back = []
            for j in span:
                total = inv[j][j] * done[j]
                for i in range(j + 1, GROUP):
                    total = total + inv[i][j] * done[i]
                back.append(total)
            for u in range(t + 1, len(tiles)):
                old = tiles[u]
                new = jnp.where(inside, 0.0, old)
                for j in span:
                    new = new - old[:, k + j : k + j + 1] * back[j]
                tiles[u] = new


def first_factor_kernel(order, *refs):
    *blocks, top, corner, rest, across, matrix = refs
    place(blocks, matrix)
    count = matrix.shape[0]
    half = count // 2
    values = matrix[...] * (1.0 / order)
    eye = lax.broadcasted_iota(jnp.int32, (count, count), 0) == lax.broadcasted_iota(
        jnp.int32, (count, count), 1
    )
    diagonal = jnp.where(eye, values, 0.0)
    scale = lax.rsqrt(jnp.sum(diagonal, 0, keepdims=True))
    down = lax.rsqrt(jnp.sum(diagonal, 1, keepdims=True))
    across[...] = scale
    values = values * scale * down
    eliminate(values[:half, :half], top, 0)
    beside = dot(top[...], values[:half, half:])
    corner[...] = dot_tn(beside, top[...])
    rest[...] = values[half:, half:] - dot_tn(beside, beside)


def second_factor_kernel(top, corner, rest, across, out):
    half = top.shape[0]
    out[:half, :half] = top[...]
    out[:half, half:] = jnp.zeros((half, half), F32)
    eliminate(rest[...], out, half)
    out[half:, :half] = -dot(out[half:, half:], corner[...])
    out[...] = out[...] * across[...]


def first_factor(blocks, order):
    columns = blocks[0].shape[1]
    half = like((columns // 2, columns // 2))
    return whole(
        functools.partial(first_factor_kernel, order),
        [half, half, half, like((1, columns))],
        *blocks,
        scratch=[pltpu.VMEM((columns, columns), F32)],
        flops=6 * 10**9,
    )


def second_factor(halves):
    columns = halves[3].shape[1]
    return whole(second_factor_kernel, like((columns, columns)), *halves, flops=6 * 10**9)


def next_head(head):
    count = lax.axis_size("rows")
    return lax.ppermute(head, "rows", [(i + 1, i) for i in range(count - 1)])


def band_kernel(field, after, diag_tiles, upper_tiles, *refs):
    earlier, (part, image, matrix) = refs[:-3], refs[-3:]
    band = after.shape[0]
    tiles = field.shape[0] // band
    values = lambda x: x.astype(F32)
    for t in range(tiles):
        at = slice(t * band, (t + 1) * band)
        following = after[...] if t == tiles - 1 else field[(t + 1) * band : (t + 2) * band]
        image[at] = 0.5 * dot_three(diag_tiles[at], values(field[at])) + dot_three(
            upper_tiles[at], values(following)
        )
    if field.dtype == BF16:
        matrix[...] = dot_two(field[...], image[...], TN)
    else:
        matrix[...] = dot_three(field[...], image[...], TN)
    size = matrix.shape[0] // lax.axis_size("node")
    for ref in earlier:
        part[:-size] = ref[...]
    part[-size:] = matrix[pl.ds(pl.multiple_of(lax.axis_index("node") * size, 8), size), :]


def band_slice(field, after, diag_tiles, upper_tiles, *earlier):
    rows, columns = field.shape
    size = columns // lax.axis_size("node")
    return whole(
        band_kernel,
        like((size * (1 + sum(x.shape[0] // size for x in earlier)), columns)),
        field,
        after,
        diag_tiles,
        upper_tiles,
        *earlier,
        scratch=[pltpu.VMEM((rows, columns), F32), pltpu.VMEM((columns, columns), F32)],
    )


def last_kernel(field, factor, out):
    if field.dtype == BF16:
        out[...] = dot_two(field[...], factor[...], NT)
    else:
        out[...] = dot_three(field[...], factor[...], NT)


def projected_kernel(order, *refs):
    blocks, factors, (out, matrix) = refs[: -2 - ITERS], refs[-2 - ITERS : -2], refs[-2:]
    node = lax.axis_index("node")
    size = blocks[0].shape[0] // ITERS
    for k, factor in enumerate(factors):
        for step, block in enumerate(blocks):
            at = pl.multiple_of((node ^ step) * size, 8)
            matrix[pl.ds(at, size), :] = block[k * size : (k + 1) * size]
        value = dot_three(dot_three(factor[...], matrix[...]), factor[...], NT)
        out[k] = (value + value.T) * (1.0 / order)


def after(value, *others):
    return lax.optimization_barrier((value,) + others)[0]


def per_device(subspace, inverse, weights, diag_tiles, upper_tiles):
    order = float(subspace.shape[0] * lax.axis_size("rows"))
    band = upper_tiles.shape[1]
    partners = lax.axis_size("node") - 1
    columns = subspace.shape[1]
    factors, parts = [], ()
    for iteration in range(ITERS):
        if iteration == 0:
            base, out_a, out_b = start(subspace, weights, upper_tiles, inverse)
        else:
            base, out_a, out_b = solve(field, factor, weights, upper_tiles, inverse)
        got_a, got_b = core_swap(out_a), link_swap(out_b)
        own, *others = correct(
            weights, base, got_a, got_b, upper_tiles, inverse, TERM_TYPES[iteration]
        )
        piece = tree_sum([own] + [x.astype(F32) for x in node_spread(others)])
        piece = piece.astype(FIELD_TYPES[iteration])
        field, head, part = gram_slice([piece] + node_spread([piece] * partners), band)
        part = part + core_swap(part)
        following = next_head(after(head, part))
        total = chip_sum(part)
        gathered = [total] + node_spread([total] * partners)
        pair = band_slice(field, after(following, total), diag_tiles, upper_tiles, *parts)
        parts = (pair,)
        halves = first_factor(gathered, order)
        if iteration == ITERS - 1:
            pair = pair + core_swap(after(pair, *gathered))
            pair = after(pair, *halves)
            pair = chip_sum(pair)
        factor = second_factor(halves)
        factors.append(factor)
    pair = after(pair, factor)
    spread = [pair] + node_spread([pair] * partners)
    orthonormal = whole(last_kernel, like(subspace.shape), field, factor)
    projected = whole(
        functools.partial(projected_kernel, order),
        like((ITERS, columns, columns)),
        *spread,
        *factors,
        scratch=[pltpu.VMEM((columns, columns), F32)],
    )
    return orthonormal, projected


def solution(mesh):
    placed = (
        P("rows", None),
        P("node", None, "rows", None),
        P("node", None),
        P("rows", None),
        P("rows", None),
    )
    return jax.shard_map(
        per_device, mesh=mesh, in_specs=placed, out_specs=(P("rows", None), P()), check_vma=False
    )
```

```python
import functools

import jax
import jax.numpy as jnp
from jax import lax
from jax.experimental import pallas as pl
from jax.experimental.pallas import tpu as pltpu
from jax.sharding import PartitionSpec as P


ITERS = 2
GROUP = 8
TERM_TYPES = (jnp.float32, jnp.bfloat16)
FIELD_TYPES = (jnp.float32, jnp.bfloat16)

precise = lax.Precision.HIGHEST
F32 = jnp.float32
BF16 = jnp.bfloat16


def dot(left, right):
    return jnp.dot(left, right, precision=precise, preferred_element_type=F32)


def dot_tn(left, right):
    dims = (((0,), (0,)), ((), ()))
    return lax.dot_general(left, right, dims, precision=precise, preferred_element_type=F32)


def halves_of(value):
    high = value.astype(BF16)
    return high, (value - high.astype(F32)).astype(BF16)


def dot_three(left, right, dims=(((1,), (0,)), ((), ()))):
    times = lambda a, b: lax.dot_general(a, b, dims, preferred_element_type=F32)
    (a, b), (c, d) = halves_of(left), halves_of(right)
    return times(a, c) + (times(a, d) + times(b, c))


def dot_two(left, right, dims=(((1,), (0,)), ((), ()))):
    times = lambda a, b: lax.dot_general(a, b, dims, preferred_element_type=F32)
    c, d = halves_of(right)
    return times(left, c) + times(left, d)


NT = (((1,), (1,)), ((), ()))
TN = (((0,), (0,)), ((), ()))


def like(shape, dtype=F32):
    return pltpu.VMEM(shape, dtype)


def halves_of(value):
    high = value.astype(BF16)
    return high, (value - high.astype(F32)).astype(BF16)


def dot_three(left, right, dims=(((1,), (0,)), ((), ()))):
    times = lambda a, b: lax.dot_general(a, b, dims, preferred_element_type=F32)
    (a, b), (c, d) = halves_of(left), halves_of(right)
    return times(a, c) + (times(a, d) + times(b, c))


def dot_two(left, right, dims=(((1,), (0,)), ((), ()))):
    times = lambda a, b: lax.dot_general(a, b, dims, preferred_element_type=F32)
    c, d = halves_of(right)
    return times(left, c) + times(left, d)


NT = (((1,), (1,)), ((), ()))
TN = (((0,), (0,)), ((), ()))


def like(shape, dtype=F32):
    return jax.ShapeDtypeStruct(shape, dtype)


def local(value):
    return pltpu.with_memory_space_constraint(value, pltpu.VMEM)


def whole(kernel, out_shape, *operands, scratch=(), flops=10**8):
    size = sum(x.size * x.dtype.itemsize for x in operands)
    vmem = pl.BlockSpec(memory_space=pltpu.VMEM)
    return pl.pallas_call(
        kernel,
        out_shape=out_shape,
        in_specs=[vmem for _ in operands],
        out_specs=jax.tree.map(lambda _: vmem, out_shape),
        scratch_shapes=list(scratch),
        cost_estimate=pl.CostEstimate(flops=flops, bytes_accessed=size, transcendentals=0),
    )(*[local(x) for x in operands])


def node_swap(block, step):
    count = lax.axis_size("node")
    return lax.ppermute(block, "node", [(i, i ^ step) for i in range(count)])


def core_swap(block):
    count = lax.axis_size("rows")
    return lax.ppermute(block, "rows", [(i, i ^ 1) for i in range(count)])


def link_swap(block):
    count = lax.axis_size("rows")
    pairs = [(i, i + 1) for i in range(1, count - 1, 2)]
    return lax.ppermute(block, "rows", pairs + [(b, a) for a, b in pairs])


def node_spread(blocks):
    return [node_swap(block, step + 1) for step, block in enumerate(blocks)]


def tree_sum(blocks):
    while len(blocks) > 1:
        odd = blocks[len(blocks) // 2 * 2 :]
        blocks = [a + b for a, b in zip(blocks[::2], blocks[1::2])] + odd
    return blocks[0]


def chip_sum(block):
    count = lax.axis_size("rows")
    chips = count // 2
    if chips <= 4:
        steps = range(1, chips)
        routes = [[(i, i ^ (2 * s)) for i in range(count)] for s in steps]
        return tree_sum([block] + [lax.ppermute(block, "rows", route) for route in routes])
    step = 2
    while step < count:
        block = block + lax.ppermute(block, "rows", [(i, i ^ step) for i in range(count)])
        step *= 2
    return block


def emit_messages(is_even, first, last, out_a, out_b):
    out_a[...] = jnp.where(is_even, last, first)
    out_b[...] = jnp.where(is_even, first, last)


def emit_messages(real, imag, coupling, tip, out_a, out_b):
    band = coupling.shape[0]
    is_even = lax.rem(lax.axis_index("rows"), 2) == 0
    last = jnp.concatenate([real[-band:], imag[-band:]], 1).astype(BF16)
    last = dot_tn(coupling, last.astype(F32)).astype(BF16)
    out_a[...] = jnp.where(is_even, last, tip)
    out_b[...] = jnp.where(is_even, tip, last)


def tip_of(real, imag, band):
    return jnp.concatenate([real[:band], imag[:band]], 1).astype(BF16)


def combine(weights, real, imag):
    return weights[:, 0:1] * real - weights[:, 1:2] * imag


def start_kernel(weights, source, vectors, coupling, base, out_a, out_b, inverse, tip, arrived):
    rows = vectors.shape[0]
    band = coupling.shape[0]
    tile = 2 * band if rows % (2 * band) == 0 else band
    spans = [pl.ds(at, tile) for at in range(0, rows, tile)]
    copies = [
        pltpu.make_async_copy(source.at[:, :, span], inverse.at[:, :, span], arrived.at[i])
        for i, span in enumerate(spans)
    ]
    for copy in copies:
        copy.start()
    for i, span in enumerate(spans):
        copies[i].wait()
        real = jnp.dot(inverse[0, 0, span], vectors[...], preferred_element_type=F32)
        imag = jnp.dot(inverse[0, 1, span], vectors[...], preferred_element_type=F32)
        base[span] = combine(weights, real, imag)
        if i == 0:
            tip[...] = tip_of(real, imag, band)
    emit_messages(real, imag, coupling[...], tip[...], out_a, out_b)


def start(vectors, weights, coupling, inverse):
    rows, columns = vectors.shape
    band = coupling.shape[1]
    message = like((band, 2 * columns), BF16)
    vmem = pl.BlockSpec(memory_space=pltpu.VMEM)
    return pl.pallas_call(
        start_kernel,
        in_specs=[vmem, pl.BlockSpec(memory_space=pltpu.HBM), vmem, vmem],
        out_specs=[vmem] * 4,
        out_shape=[like((rows, columns)), message, message, like(inverse.shape, BF16)],
        scratch_shapes=[
            pltpu.VMEM((band, 2 * columns), BF16),
            pltpu.SemaphoreType.DMA((rows // band,)),
        ],
        cost_estimate=pl.CostEstimate(
            flops=4 * rows * rows * columns, bytes_accessed=inverse.size * 2, transcendentals=0
        ),
        name="start",
    )(local(weights), inverse, local(vectors), local(coupling))


def solve_kernel(weights, field, factor, coupling, inverse, base, out_a, out_b, tip, current):
    band = coupling.shape[0]
    rows = field.shape[0]
    current[...] = dot_three(field[...], factor[...], NT).astype(BF16)
    tile = 2 * band if rows % (2 * band) == 0 else band
    for at in range(0, rows, tile):
        real = jnp.dot(inverse[0, 0, at : at + tile], current[...], preferred_element_type=F32)
        imag = jnp.dot(inverse[0, 1, at : at + tile], current[...], preferred_element_type=F32)
        base[at : at + tile] = combine(weights, real, imag)
        if at == 0:
            tip[...] = tip_of(real, imag, band)
    emit_messages(real, imag, coupling[...], tip[...], out_a, out_b)


def solve(field, factor, weights, coupling, inverse):
    rows, columns = field.shape
    band = coupling.shape[1]
    message = like((band, 2 * columns), BF16)
    return whole(
        solve_kernel,
        [like((rows, columns)), message, message],
        weights,
        field,
        factor,
        coupling,
        inverse,
        scratch=[pltpu.VMEM((band, 2 * columns), BF16), pltpu.VMEM((rows, columns), BF16)],
        flops=4 * rows * rows * columns,
    )


def correct_kernel(weights, base, got_a, got_b, coupling, inverse, own, *refs):
    sends, term = refs[:-1], refs[-1]
    band = coupling.shape[1]
    rows, columns = base.shape
    node = lax.axis_index("node")
    is_even = lax.rem(lax.axis_index("rows"), 2) == 0
    above = jnp.where(is_even, got_b[...], got_a[...])
    from_next = jnp.where(is_even, got_a[...], got_b[...])
    below = dot(coupling[...], from_next.astype(F32)).astype(BF16)
    total = base[...]
    for edge, columns_at in ((above, 0), (below, rows - band)):
        real, imag = edge[:, :columns].astype(F32), edge[:, columns:].astype(F32)
        part = slice(columns_at, columns_at + band)
        total = total + dot_two(inverse[0, 0, :, part], combine(weights, real, imag))
        total = total - dot_two(inverse[0, 1, :, part], weights[:, 0:1] * imag + weights[:, 1:2] * real)
    term[...] = total
    size = own.shape[0]
    for s, out in enumerate((own,) + sends):
        where = pl.multiple_of((node ^ s) * size, 8)
        out[...] = term[pl.ds(where, size), :].astype(out.dtype)


def correct(weights, base, got_a, got_b, coupling, inverse, kind):
    rows, columns = base.shape
    band = coupling.shape[1]
    count = lax.axis_size("node")
    size = rows // count
    outs = [like((size, columns))] + [like((size, columns), kind)] * (count - 1)
    return whole(
        correct_kernel,
        outs,
        weights,
        base,
        got_a,
        got_b,
        coupling,
        inverse,
        scratch=[pltpu.VMEM((rows, columns), F32)],
        flops=16 * rows * band * columns,
    )


def place(blocks, out):
    node = lax.axis_index("node")
    size = blocks[0].shape[0]
    for step, block in enumerate(blocks):
        out[pl.ds(pl.multiple_of((node ^ step) * size, 8), size), :] = block[...]


def gram_kernel(*refs):
    *blocks, field, head, part, matrix = refs
    place(blocks, field)
    head[...] = field[: head.shape[0]]
    if field.dtype == BF16:
        matrix[...] = lax.dot_general(field[...], field[...], TN, preferred_element_type=F32)
    else:
        matrix[...] = dot_tn(field[...], field[...])
    size = part.shape[0]
    part[...] = matrix[pl.ds(pl.multiple_of(lax.axis_index("node") * size, 8), size), :]


def gram_slice(blocks, band):
    rows, columns = blocks[0].shape
    count = len(blocks)
    kind = blocks[0].dtype
    outs = [
        like((rows * count, columns), kind),
        like((band, columns), kind),
        like((columns // count, columns)),
    ]
    scratch = [pltpu.VMEM((columns, columns), F32)]
    return whole(gram_kernel, outs, *blocks, scratch=scratch)


def eliminate(block, out, base):
    count = block.shape[0]
    full = (GROUP, count)
    lane = lax.broadcasted_iota(jnp.int32, full, 1)
    span = range(GROUP)
    tiles = [block[t * GROUP : (t + 1) * GROUP] for t in range(count // GROUP)]
    for t, tile in enumerate(tiles):
        k = t * GROUP
        tile = tiles[t]
        rows = [jnp.broadcast_to(tile[i : i + 1], full) for i in span]
        pivot = [[jnp.broadcast_to(rows[i][:, k + j : k + j + 1], full) for j in range(i + 1)] for i in span]
        scale = []
        low = [[None] * GROUP for _ in span]
        for j in span:
            scale.append(lax.rsqrt(pivot[j][j]))
            for i in range(j + 1, GROUP):
                low[i][j] = pivot[i][j] * scale[j]
            for i in range(j + 1, GROUP):
                for m in range(j + 1, i + 1):
                    pivot[i][m] = pivot[i][m] - low[i][j] * low[m][j]
        inv = [[None] * GROUP for _ in span]
        for j in span:
            inv[j][j] = scale[j]
            for i in range(j + 1, GROUP):
                total = low[i][j] * inv[j][j]
                for m in range(j + 1, i):
                    total = total + low[i][m] * inv[m][j]
                inv[i][j] = -total * scale[i]
        inside = (lane >= k) & (lane < k + GROUP)
        rows = [jnp.where(inside, jnp.where(lane == k + i, 1.0, 0.0), rows[i]) for i in span]
        done = []
        for i in span:
            total = inv[i][0] * rows[0]
            for j in range(1, i + 1):
                total = total + inv[i][j] * rows[j]
            done.append(total)
            at = base + k + i
            out[at : at + 1, base : base + count] = jnp.where(lane < k + GROUP, total, 0.0)[:1]
        if t + 1 < len(tiles):
            back = []
            for j in span:
                total = inv[j][j] * done[j]
                for i in range(j + 1, GROUP):
                    total = total + inv[i][j] * done[i]
                back.append(total)
            for u in range(t + 1, len(tiles)):
                old = tiles[u]
                new = jnp.where(inside, 0.0, old)
                for j in span:
                    new = new - old[:, k + j : k + j + 1] * back[j]
                tiles[u] = new


def first_factor_kernel(order, *refs):
    *blocks, top, corner, rest, across, matrix = refs
    place(blocks, matrix)
    count = matrix.shape[0]
    half = count // 2
    values = matrix[...] * (1.0 / order)
    eye = lax.broadcasted_iota(jnp.int32, (count, count), 0) == lax.broadcasted_iota(
        jnp.int32, (count, count), 1
    )
    diagonal = jnp.where(eye, values, 0.0)
    scale = lax.rsqrt(jnp.sum(diagonal, 0, keepdims=True))
    down = lax.rsqrt(jnp.sum(diagonal, 1, keepdims=True))
    across[...] = scale
    values = values * scale * down
    eliminate(values[:half, :half], top, 0)
    beside = dot(top[...], values[:half, half:])
    corner[...] = dot_tn(beside, top[...])
    rest[...] = values[half:, half:] - dot_tn(beside, beside)


def second_factor_kernel(top, corner, rest, across, out):
    half = top.shape[0]
    out[:half, :half] = top[...]
    out[:half, half:] = jnp.zeros((half, half), F32)
    eliminate(rest[...], out, half)
    out[half:, :half] = -dot(out[half:, half:], corner[...])
    out[...] = out[...] * across[...]


def first_factor(blocks, order):
    columns = blocks[0].shape[1]
    half = like((columns // 2, columns // 2))
    return whole(
        functools.partial(first_factor_kernel, order),
        [half, half, half, like((1, columns))],
        *blocks,
        scratch=[pltpu.VMEM((columns, columns), F32)],
        flops=6 * 10**9,
    )


def second_factor(halves):
    columns = halves[3].shape[1]
    return whole(second_factor_kernel, like((columns, columns)), *halves, flops=6 * 10**9)


def next_head(head):
    count = lax.axis_size("rows")
    return lax.ppermute(head, "rows", [(i + 1, i) for i in range(count - 1)])


def band_kernel(field, after, diag_tiles, upper_tiles, *refs):
    earlier, (part, image, matrix) = refs[:-3], refs[-3:]
    band = after.shape[0]
    tiles = field.shape[0] // band
    values = lambda x: x.astype(F32)
    for t in range(tiles):
        at = slice(t * band, (t + 1) * band)
        following = after[...] if t == tiles - 1 else field[(t + 1) * band : (t + 2) * band]
        image[at] = 0.5 * dot_three(diag_tiles[at], values(field[at])) + dot_three(
            upper_tiles[at], values(following)
        )
    if field.dtype == BF16:
        matrix[...] = dot_two(field[...], image[...], TN)
    else:
        matrix[...] = dot_three(field[...], image[...], TN)
    size = matrix.shape[0] // lax.axis_size("node")
    for ref in earlier:
        part[:-size] = ref[...]
    part[-size:] = matrix[pl.ds(pl.multiple_of(lax.axis_index("node") * size, 8), size), :]


def band_slice(field, after, diag_tiles, upper_tiles, *earlier):
    rows, columns = field.shape
    size = columns // lax.axis_size("node")
    return whole(
        band_kernel,
        like((size * (1 + sum(x.shape[0] // size for x in earlier)), columns)),
        field,
        after,
        diag_tiles,
        upper_tiles,
        *earlier,
        scratch=[pltpu.VMEM((rows, columns), F32), pltpu.VMEM((columns, columns), F32)],
    )


def last_kernel(field, factor, out):
    if field.dtype == BF16:
        out[...] = dot_two(field[...], factor[...], NT)
    else:
        out[...] = dot_three(field[...], factor[...], NT)


def projected_kernel(order, *refs):
    blocks, factors, (out, matrix) = refs[: -2 - ITERS], refs[-2 - ITERS : -2], refs[-2:]
    node = lax.axis_index("node")
    size = blocks[0].shape[0] // ITERS
    for k, factor in enumerate(factors):
        for step, block in enumerate(blocks):
            at = pl.multiple_of((node ^ step) * size, 8)
            matrix[pl.ds(at, size), :] = block[k * size : (k + 1) * size]
        value = dot_three(dot_three(factor[...], matrix[...]), factor[...], NT)
        out[k] = (value + value.T) * (1.0 / order)


def after(value, *others):
    return lax.optimization_barrier((value,) + others)[0]


def per_device(subspace, inverse, weights, diag_tiles, upper_tiles):
    order = float(subspace.shape[0] * lax.axis_size("rows"))
    band = upper_tiles.shape[1]
    coupling = upper_tiles[-band:]
    partners = lax.axis_size("node") - 1
    columns = subspace.shape[1]
    factors, parts = [], ()
    for iteration in range(ITERS):
        if iteration == 0:
            base, out_a, out_b, inverse = start(subspace, weights, coupling, inverse)
        else:
            base, out_a, out_b = solve(field, factor, weights, coupling, inverse)
        got_a, got_b = core_swap(out_a), link_swap(out_b)
        own, *others = correct(
            weights, base, got_a, got_b, coupling, inverse, TERM_TYPES[iteration]
        )
        piece = tree_sum([own] + [x.astype(F32) for x in node_spread(others)])
        piece = piece.astype(FIELD_TYPES[iteration])
        field, head, part = gram_slice([piece] + node_spread([piece] * partners), band)
        part = part + core_swap(part)
        following = next_head(after(head, part))
        total = chip_sum(part)
        gathered = [total] + node_spread([total] * partners)
        pair = band_slice(field, after(following, total), diag_tiles, upper_tiles, *parts)
        parts = (pair,)
        halves = first_factor(gathered, order)
        if iteration == ITERS - 1:
            pair = pair + core_swap(after(pair, *gathered))
            pair = after(pair, *halves)
            pair = chip_sum(pair)
        factor = second_factor(halves)
        factors.append(factor)
    pair = after(pair, factor)
    spread = [pair] + node_spread([pair] * partners)
    orthonormal = whole(last_kernel, jax.ShapeDtypeStruct(subspace.shape, F32), field, factor)
    projected = whole(
        functools.partial(projected_kernel, order),
        jax.ShapeDtypeStruct((ITERS, columns, columns), F32),
        *spread,
        *factors,
        scratch=[pltpu.VMEM((columns, columns), F32)],
    )
    return orthonormal, projected


def solution(mesh):
    placed = (
        P("rows", None),
        P("node", None, "rows", None),
        P("node", None),
        P("rows", None),
        P("rows", None),
    )
    return jax.shard_map(
        per_device, mesh=mesh, in_specs=placed, out_specs=(P("rows", None), P()), check_vma=False
    )
```

```python
import functools

import jax
import jax.numpy as jnp
from jax import lax
from jax.experimental import pallas as pl
from jax.experimental.pallas import tpu as pltpu
from jax.sharding import PartitionSpec as P


ITERS = 2
GROUP = 8
GRANT = 16 * 2**20
TERM_TYPES = (jnp.float32, jnp.bfloat16)
FIELD_TYPES = (jnp.float32, jnp.bfloat16)

precise = lax.Precision.HIGHEST
F32 = jnp.float32
BF16 = jnp.bfloat16


def dot(left, right):
    return jnp.dot(left, right, precision=precise, preferred_element_type=F32)


def dot_tn(left, right):
    dims = (((0,), (0,)), ((), ()))
    return lax.dot_general(left, right, dims, precision=precise, preferred_element_type=F32)


def halves_of(value):
    high = value.astype(BF16)
    return high, (value - high.astype(F32)).astype(BF16)


def dot_three(left, right, dims=(((1,), (0,)), ((), ()))):
    times = lambda a, b: lax.dot_general(a, b, dims, preferred_element_type=F32)
    (a, b), (c, d) = halves_of(left), halves_of(right)
    return times(a, c) + (times(a, d) + times(b, c))


def dot_two(left, right, dims=(((1,), (0,)), ((), ()))):
    times = lambda a, b: lax.dot_general(a, b, dims, preferred_element_type=F32)
    c, d = halves_of(right)
    return times(left, c) + times(left, d)


NT = (((1,), (1,)), ((), ()))
TN = (((0,), (0,)), ((), ()))


def like(shape, dtype=F32):
    return pltpu.VMEM(shape, dtype)


def halves_of(value):
    high = value.astype(BF16)
    return high, (value - high.astype(F32)).astype(BF16)


def dot_three(left, right, dims=(((1,), (0,)), ((), ()))):
    times = lambda a, b: lax.dot_general(a, b, dims, preferred_element_type=F32)
    (a, b), (c, d) = halves_of(left), halves_of(right)
    return times(a, c) + (times(a, d) + times(b, c))


def dot_two(left, right, dims=(((1,), (0,)), ((), ()))):
    times = lambda a, b: lax.dot_general(a, b, dims, preferred_element_type=F32)
    c, d = halves_of(right)
    return times(left, c) + times(left, d)


NT = (((1,), (1,)), ((), ()))
TN = (((0,), (0,)), ((), ()))


def local(value):
    return pltpu.with_memory_space_constraint(value, pltpu.VMEM)


def whole(kernel, out_shape, *operands, scratch=(), flops=10**8):
    size = sum(x.size * x.dtype.itemsize for x in operands)
    vmem = pl.BlockSpec(memory_space=pltpu.VMEM)
    return pl.pallas_call(
        kernel,
        out_shape=out_shape,
        in_specs=[vmem for _ in operands],
        out_specs=jax.tree.map(lambda _: vmem, out_shape),
        scratch_shapes=list(scratch),
        cost_estimate=pl.CostEstimate(flops=flops, bytes_accessed=size, transcendentals=0),
        compiler_params=pltpu.CompilerParams(vmem_limit_bytes=GRANT),
    )(*[local(x) for x in operands])


def node_swap(block, step):
    count = lax.axis_size("node")
    return lax.ppermute(block, "node", [(i, i ^ step) for i in range(count)])


def core_swap(block):
    count = lax.axis_size("rows")
    return lax.ppermute(block, "rows", [(i, i ^ 1) for i in range(count)])


def link_swap(block):
    count = lax.axis_size("rows")
    pairs = [(i, i + 1) for i in range(1, count - 1, 2)]
    return lax.ppermute(block, "rows", pairs + [(b, a) for a, b in pairs])


def node_spread(blocks):
    return [node_swap(block, step + 1) for step, block in enumerate(blocks)]


def tree_sum(blocks):
    while len(blocks) > 1:
        odd = blocks[len(blocks) // 2 * 2 :]
        blocks = [a + b for a, b in zip(blocks[::2], blocks[1::2])] + odd
    return blocks[0]


def chip_sum(block):
    count = lax.axis_size("rows")
    chips = count // 2
    if chips <= 4:
        steps = range(1, chips)
        routes = [[(i, i ^ (2 * s)) for i in range(count)] for s in steps]
        return tree_sum([block] + [lax.ppermute(block, "rows", route) for route in routes])
    step = 2
    while step < count:
        block = block + lax.ppermute(block, "rows", [(i, i ^ step) for i in range(count)])
        step *= 2
    return block


def emit_messages(is_even, first, last, out_a, out_b):
    out_a[...] = jnp.where(is_even, last, first)
    out_b[...] = jnp.where(is_even, first, last)


def emit_messages(real, imag, coupling, tip, out_a, out_b):
    band = coupling.shape[0]
    is_even = lax.rem(lax.axis_index("rows"), 2) == 0
    last = jnp.concatenate([real[-band:], imag[-band:]], 1).astype(BF16)
    last = dot_tn(coupling, last.astype(F32)).astype(BF16)
    out_a[...] = jnp.where(is_even, last, tip)
    out_b[...] = jnp.where(is_even, tip, last)


def tip_of(real, imag, band):
    return jnp.concatenate([real[:band], imag[:band]], 1).astype(BF16)


def combine(weights, real, imag):
    return weights[:, 0:1] * real - weights[:, 1:2] * imag


def start_kernel(weights, source, vectors, coupling, base, out_a, out_b, inverse, tip, arrived):
    rows = vectors.shape[0]
    band = coupling.shape[0]
    tile = 2 * band if rows % (2 * band) == 0 else band
    spans = [pl.ds(at, tile) for at in range(0, rows, tile)]
    copies = [
        pltpu.make_async_copy(source.at[:, :, span], inverse.at[:, :, span], arrived.at[i])
        for i, span in enumerate(spans)
    ]
    for copy in copies:
        copy.start()
    for i, span in enumerate(spans):
        copies[i].wait()
        real = jnp.dot(inverse[0, 0, span], vectors[...], preferred_element_type=F32)
        imag = jnp.dot(inverse[0, 1, span], vectors[...], preferred_element_type=F32)
        base[span] = combine(weights, real, imag)
        if i == 0:
            tip[...] = tip_of(real, imag, band)
    emit_messages(real, imag, coupling[...], tip[...], out_a, out_b)


def start(vectors, weights, coupling, inverse):
    rows, columns = vectors.shape
    band = coupling.shape[1]
    message = like((band, 2 * columns), BF16)
    vmem = pl.BlockSpec(memory_space=pltpu.VMEM)
    return pl.pallas_call(
        start_kernel,
        in_specs=[vmem, pl.BlockSpec(memory_space=pltpu.HBM), vmem, vmem],
        out_specs=[vmem] * 4,
        out_shape=[like((rows, columns)), message, message, like(inverse.shape, BF16)],
        scratch_shapes=[
            pltpu.VMEM((band, 2 * columns), BF16),
            pltpu.SemaphoreType.DMA((rows // band,)),
        ],
        cost_estimate=pl.CostEstimate(
            flops=4 * rows * rows * columns, bytes_accessed=inverse.size * 2, transcendentals=0
        ),
        compiler_params=pltpu.CompilerParams(vmem_limit_bytes=GRANT),
        name="start",
    )(local(weights), pltpu.with_memory_space_constraint(inverse, pltpu.HBM), local(vectors), local(coupling))


def solve_kernel(weights, field, factor, coupling, inverse, base, out_a, out_b, tip, current):
    band = coupling.shape[0]
    rows = field.shape[0]
    current[...] = dot_three(field[...], factor[...], NT).astype(BF16)
    tile = 2 * band if rows % (2 * band) == 0 else band
    for at in range(0, rows, tile):
        real = jnp.dot(inverse[0, 0, at : at + tile], current[...], preferred_element_type=F32)
        imag = jnp.dot(inverse[0, 1, at : at + tile], current[...], preferred_element_type=F32)
        base[at : at + tile] = combine(weights, real, imag)
        if at == 0:
            tip[...] = tip_of(real, imag, band)
    emit_messages(real, imag, coupling[...], tip[...], out_a, out_b)


def solve(field, factor, weights, coupling, inverse):
    rows, columns = field.shape
    band = coupling.shape[1]
    message = like((band, 2 * columns), BF16)
    return whole(
        solve_kernel,
        [like((rows, columns)), message, message],
        weights,
        field,
        factor,
        coupling,
        inverse,
        scratch=[pltpu.VMEM((band, 2 * columns), BF16), pltpu.VMEM((rows, columns), BF16)],
        flops=4 * rows * rows * columns,
    )


def correct_kernel(weights, base, got_a, got_b, coupling, inverse, own, *refs):
    sends, term = refs[:-1], refs[-1]
    band = coupling.shape[1]
    rows, columns = base.shape
    node = lax.axis_index("node")
    is_even = lax.rem(lax.axis_index("rows"), 2) == 0
    above = jnp.where(is_even, got_b[...], got_a[...])
    from_next = jnp.where(is_even, got_a[...], got_b[...])
    below = dot(coupling[...], from_next.astype(F32)).astype(BF16)
    total = base[...]
    for edge, columns_at in ((above, 0), (below, rows - band)):
        real, imag = edge[:, :columns].astype(F32), edge[:, columns:].astype(F32)
        part = slice(columns_at, columns_at + band)
        total = total + dot_two(inverse[0, 0, :, part], combine(weights, real, imag))
        total = total - dot_two(inverse[0, 1, :, part], weights[:, 0:1] * imag + weights[:, 1:2] * real)
    term[...] = total
    size = own.shape[0]
    for s, out in enumerate((own,) + sends):
        where = pl.multiple_of((node ^ s) * size, 8)
        out[...] = term[pl.ds(where, size), :].astype(out.dtype)


def correct(weights, base, got_a, got_b, coupling, inverse, kind):
    rows, columns = base.shape
    band = coupling.shape[1]
    count = lax.axis_size("node")
    size = rows // count
    outs = [like((size, columns))] + [like((size, columns), kind)] * (count - 1)
    return whole(
        correct_kernel,
        outs,
        weights,
        base,
        got_a,
        got_b,
        coupling,
        inverse,
        scratch=[pltpu.VMEM((rows, columns), F32)],
        flops=16 * rows * band * columns,
    )


def place(blocks, out):
    node = lax.axis_index("node")
    size = blocks[0].shape[0]
    for step, block in enumerate(blocks):
        out[pl.ds(pl.multiple_of((node ^ step) * size, 8), size), :] = block[...]


def gram_kernel(*refs):
    *blocks, field, head, part, matrix = refs
    place(blocks, field)
    head[...] = field[: head.shape[0]]
    if field.dtype == BF16:
        matrix[...] = lax.dot_general(field[...], field[...], TN, preferred_element_type=F32)
    else:
        matrix[...] = dot_tn(field[...], field[...])
    size = part.shape[0]
    part[...] = matrix[pl.ds(pl.multiple_of(lax.axis_index("node") * size, 8), size), :]


def gram_slice(blocks, band):
    rows, columns = blocks[0].shape
    count = len(blocks)
    kind = blocks[0].dtype
    outs = [
        like((rows * count, columns), kind),
        like((band, columns), kind),
        like((columns // count, columns)),
    ]
    scratch = [pltpu.VMEM((columns, columns), F32)]
    return whole(gram_kernel, outs, *blocks, scratch=scratch)


def eliminate(block, out, base):
    count = block.shape[0]
    full = (GROUP, count)
    lane = lax.broadcasted_iota(jnp.int32, full, 1)
    span = range(GROUP)
    tiles = [block[t * GROUP : (t + 1) * GROUP] for t in range(count // GROUP)]
    for t, tile in enumerate(tiles):
        k = t * GROUP
        tile = tiles[t]
        rows = [jnp.broadcast_to(tile[i : i + 1], full) for i in span]
        pivot = [[jnp.broadcast_to(rows[i][:, k + j : k + j + 1], full) for j in range(i + 1)] for i in span]
        scale = []
        low = [[None] * GROUP for _ in span]
        for j in span:
            scale.append(lax.rsqrt(pivot[j][j]))
            for i in range(j + 1, GROUP):
                low[i][j] = pivot[i][j] * scale[j]
            for i in range(j + 1, GROUP):
                for m in range(j + 1, i + 1):
                    pivot[i][m] = pivot[i][m] - low[i][j] * low[m][j]
        inv = [[None] * GROUP for _ in span]
        for j in span:
            inv[j][j] = scale[j]
            for i in range(j + 1, GROUP):
                total = low[i][j] * inv[j][j]
                for m in range(j + 1, i):
                    total = total + low[i][m] * inv[m][j]
                inv[i][j] = -total * scale[i]
        inside = (lane >= k) & (lane < k + GROUP)
        rows = [jnp.where(inside, jnp.where(lane == k + i, 1.0, 0.0), rows[i]) for i in span]
        done = []
        for i in span:
            total = inv[i][0] * rows[0]
            for j in range(1, i + 1):
                total = total + inv[i][j] * rows[j]
            done.append(total)
            at = base + k + i
            out[at : at + 1, base : base + count] = jnp.where(lane < k + GROUP, total, 0.0)[:1]
        if t + 1 < len(tiles):
            back = []
            for j in span:
                total = inv[j][j] * done[j]
                for i in range(j + 1, GROUP):
                    total = total + inv[i][j] * done[i]
                back.append(total)
            for u in range(t + 1, len(tiles)):
                old = tiles[u]
                new = jnp.where(inside, 0.0, old)
                for j in span:
                    new = new - old[:, k + j : k + j + 1] * back[j]
                tiles[u] = new


def first_factor_kernel(order, *refs):
    *blocks, top, corner, rest, across, matrix = refs
    place(blocks, matrix)
    count = matrix.shape[0]
    half = count // 2
    values = matrix[...] * (1.0 / order)
    eye = lax.broadcasted_iota(jnp.int32, (count, count), 0) == lax.broadcasted_iota(
        jnp.int32, (count, count), 1
    )
    diagonal = jnp.where(eye, values, 0.0)
    scale = lax.rsqrt(jnp.sum(diagonal, 0, keepdims=True))
    down = lax.rsqrt(jnp.sum(diagonal, 1, keepdims=True))
    across[...] = scale
    values = values * scale * down
    eliminate(values[:half, :half], top, 0)
    beside = dot(top[...], values[:half, half:])
    corner[...] = dot_tn(beside, top[...])
    rest[...] = values[half:, half:] - dot_tn(beside, beside)


def second_factor_kernel(top, corner, rest, across, out):
    half = top.shape[0]
    out[:half, :half] = top[...]
    out[:half, half:] = jnp.zeros((half, half), F32)
    eliminate(rest[...], out, half)
    out[half:, :half] = -dot(out[half:, half:], corner[...])
    out[...] = out[...] * across[...]


def first_factor(blocks, order):
    columns = blocks[0].shape[1]
    half = like((columns // 2, columns // 2))
    return whole(
        functools.partial(first_factor_kernel, order),
        [half, half, half, like((1, columns))],
        *blocks,
        scratch=[pltpu.VMEM((columns, columns), F32)],
        flops=6 * 10**9,
    )


def second_factor(halves):
    columns = halves[3].shape[1]
    return whole(second_factor_kernel, like((columns, columns)), *halves, flops=6 * 10**9)


def next_head(head):
    count = lax.axis_size("rows")
    return lax.ppermute(head, "rows", [(i + 1, i) for i in range(count - 1)])


def band_kernel(field, after, diag_tiles, upper_tiles, *refs):
    earlier, (part, image, matrix) = refs[:-3], refs[-3:]
    band = after.shape[0]
    tiles = field.shape[0] // band
    values = lambda x: x.astype(F32)
    for t in range(tiles):
        at = slice(t * band, (t + 1) * band)
        following = after[...] if t == tiles - 1 else field[(t + 1) * band : (t + 2) * band]
        image[at] = 0.5 * dot_three(diag_tiles[at], values(field[at])) + dot_three(
            upper_tiles[at], values(following)
        )
    if field.dtype == BF16:
        matrix[...] = dot_two(field[...], image[...], TN)
    else:
        matrix[...] = dot_three(field[...], image[...], TN)
    size = matrix.shape[0] // lax.axis_size("node")
    for ref in earlier:
        part[:-size] = ref[...]
    part[-size:] = matrix[pl.ds(pl.multiple_of(lax.axis_index("node") * size, 8), size), :]


def band_slice(field, after, diag_tiles, upper_tiles, *earlier):
    rows, columns = field.shape
    size = columns // lax.axis_size("node")
    return whole(
        band_kernel,
        like((size * (1 + sum(x.shape[0] // size for x in earlier)), columns)),
        field,
        after,
        diag_tiles,
        upper_tiles,
        *earlier,
        scratch=[pltpu.VMEM((rows, columns), F32), pltpu.VMEM((columns, columns), F32)],
    )


def last_kernel(field, factor, out):
    if field.dtype == BF16:
        out[...] = dot_two(field[...], factor[...], NT)
    else:
        out[...] = dot_three(field[...], factor[...], NT)


def projected_kernel(order, *refs):
    blocks, factors, (out, matrix) = refs[: -2 - ITERS], refs[-2 - ITERS : -2], refs[-2:]
    node = lax.axis_index("node")
    size = blocks[0].shape[0] // ITERS
    for k, factor in enumerate(factors):
        for step, block in enumerate(blocks):
            at = pl.multiple_of((node ^ step) * size, 8)
            matrix[pl.ds(at, size), :] = block[k * size : (k + 1) * size]
        value = dot_three(dot_three(factor[...], matrix[...]), factor[...], NT)
        out[k] = (value + value.T) * (1.0 / order)


def after(value, *others):
    return lax.optimization_barrier((value,) + others)[0]


def per_device(subspace, inverse, weights, diag_tiles, upper_tiles):
    order = float(subspace.shape[0] * lax.axis_size("rows"))
    band = upper_tiles.shape[1]
    coupling = upper_tiles[-band:]
    partners = lax.axis_size("node") - 1
    columns = subspace.shape[1]
    factors, parts = [], ()
    for iteration in range(ITERS):
        if iteration == 0:
            base, out_a, out_b, inverse = start(subspace, weights, coupling, inverse)
        else:
            base, out_a, out_b = solve(field, factor, weights, coupling, inverse)
        got_a, got_b = core_swap(out_a), link_swap(out_b)
        own, *others = correct(
            weights, base, got_a, got_b, coupling, inverse, TERM_TYPES[iteration]
        )
        piece = tree_sum([own] + [x.astype(F32) for x in node_spread(others)])
        piece = piece.astype(FIELD_TYPES[iteration])
        field, head, part = gram_slice([piece] + node_spread([piece] * partners), band)
        part = part + core_swap(part)
        following = next_head(after(head, part))
        total = chip_sum(part)
        gathered = [total] + node_spread([total] * partners)
        pair = band_slice(field, after(following, total), diag_tiles, upper_tiles, *parts)
        parts = (pair,)
        halves = first_factor(gathered, order)
        if iteration == ITERS - 1:
            pair = pair + core_swap(after(pair, *gathered))
            pair = after(pair, *halves)
            pair = chip_sum(pair)
        factor = second_factor(halves)
        factors.append(factor)
    pair = after(pair, factor)
    spread = [pair] + node_spread([pair] * partners)
    orthonormal = whole(last_kernel, jax.ShapeDtypeStruct(subspace.shape, F32), field, factor)
    projected = whole(
        functools.partial(projected_kernel, order),
        jax.ShapeDtypeStruct((ITERS, columns, columns), F32),
        *spread,
        *factors,
        scratch=[pltpu.VMEM((columns, columns), F32)],
    )
    return orthonormal, projected


def solution(mesh):
    placed = (
        P("rows", None),
        P("node", None, "rows", None),
        P("node", None),
        P("rows", None),
        P("rows", None),
    )
    return jax.shard_map(
        per_device, mesh=mesh, in_specs=placed, out_specs=(P("rows", None), P()), check_vma=False
    )
```

```python
import functools

import jax
import jax.numpy as jnp
from jax import lax
from jax.experimental import pallas as pl
from jax.experimental.pallas import tpu as pltpu
from jax.sharding import PartitionSpec as P


ITERS = 2
GROUP = 8
GRANT = 16 * 2**20

precise = lax.Precision.HIGHEST
F32 = jnp.float32
BF16 = jnp.bfloat16


def dot(left, right):
    return jnp.dot(left, right, precision=precise, preferred_element_type=F32)


def dot_tn(left, right):
    dims = (((0,), (0,)), ((), ()))
    return lax.dot_general(left, right, dims, precision=precise, preferred_element_type=F32)


def halves_of(value):
    high = value.astype(BF16)
    return high, (value - high.astype(F32)).astype(BF16)


def dot_three(left, right, dims=(((1,), (0,)), ((), ()))):
    times = lambda a, b: lax.dot_general(a, b, dims, preferred_element_type=F32)
    (a, b), (c, d) = halves_of(left), halves_of(right)
    return times(a, c) + (times(a, d) + times(b, c))


def dot_two(left, right, dims=(((1,), (0,)), ((), ()))):
    times = lambda a, b: lax.dot_general(a, b, dims, preferred_element_type=F32)
    c, d = halves_of(right)
    return times(left, c) + times(left, d)


NT = (((1,), (1,)), ((), ()))
TN = (((0,), (0,)), ((), ()))


def like(shape, dtype=F32):
    return pltpu.VMEM(shape, dtype)


def halves_of(value):
    high = value.astype(BF16)
    return high, (value - high.astype(F32)).astype(BF16)


def dot_three(left, right, dims=(((1,), (0,)), ((), ()))):
    times = lambda a, b: lax.dot_general(a, b, dims, preferred_element_type=F32)
    (a, b), (c, d) = halves_of(left), halves_of(right)
    return times(a, c) + (times(a, d) + times(b, c))


def dot_two(left, right, dims=(((1,), (0,)), ((), ()))):
    times = lambda a, b: lax.dot_general(a, b, dims, preferred_element_type=F32)
    c, d = halves_of(right)
    return times(left, c) + times(left, d)


NT = (((1,), (1,)), ((), ()))
TN = (((0,), (0,)), ((), ()))


def local(value):
    return pltpu.with_memory_space_constraint(value, pltpu.VMEM)


def whole(kernel, out_shape, *operands, scratch=(), flops=10**8):
    size = sum(x.size * x.dtype.itemsize for x in operands)
    vmem = pl.BlockSpec(memory_space=pltpu.VMEM)
    return pl.pallas_call(
        kernel,
        out_shape=out_shape,
        in_specs=[vmem for _ in operands],
        out_specs=jax.tree.map(lambda _: vmem, out_shape),
        scratch_shapes=list(scratch),
        cost_estimate=pl.CostEstimate(flops=flops, bytes_accessed=size, transcendentals=0),
        compiler_params=pltpu.CompilerParams(vmem_limit_bytes=GRANT),
    )(*[local(x) for x in operands])


def node_swap(block, step):
    count = lax.axis_size("node")
    return lax.ppermute(block, "node", [(i, i ^ step) for i in range(count)])


def core_swap(block):
    count = lax.axis_size("rows")
    return lax.ppermute(block, "rows", [(i, i ^ 1) for i in range(count)])


def link_swap(block):
    count = lax.axis_size("rows")
    pairs = [(i, i + 1) for i in range(1, count - 1, 2)]
    return lax.ppermute(block, "rows", pairs + [(b, a) for a, b in pairs])


def node_spread(blocks):
    return [node_swap(block, step + 1) for step, block in enumerate(blocks)]


def tree_sum(blocks):
    while len(blocks) > 1:
        odd = blocks[len(blocks) // 2 * 2 :]
        blocks = [a + b for a, b in zip(blocks[::2], blocks[1::2])] + odd
    return blocks[0]


def chip_sum(block):
    count = lax.axis_size("rows")
    chips = count // 2
    if chips <= 4:
        steps = range(1, chips)
        routes = [[(i, i ^ (2 * s)) for i in range(count)] for s in steps]
        return tree_sum([block] + [lax.ppermute(block, "rows", route) for route in routes])
    step = 2
    while step < count:
        block = block + lax.ppermute(block, "rows", [(i, i ^ step) for i in range(count)])
        step *= 2
    return block


def emit_messages(is_even, first, last, out_a, out_b):
    out_a[...] = jnp.where(is_even, last, first)
    out_b[...] = jnp.where(is_even, first, last)


def emit_messages(real, imag, coupling, tip, out_a, out_b):
    band = coupling.shape[0]
    is_even = lax.rem(lax.axis_index("rows"), 2) == 0
    last = jnp.concatenate([real[-band:], imag[-band:]], 1).astype(BF16)
    last = dot_tn(coupling, last.astype(F32)).astype(BF16)
    out_a[...] = jnp.where(is_even, last, tip)
    out_b[...] = jnp.where(is_even, tip, last)


def tip_of(real, imag, band):
    return jnp.concatenate([real[:band], imag[:band]], 1).astype(BF16)


def combine(weights, real, imag):
    return weights[:, 0:1] * real - weights[:, 1:2] * imag


def start_kernel(weights_at, source, vectors_at, upper_at, *refs):
    base, out_a, out_b, inverse, coupling, weights, vectors, tip, arrived = refs
    rows = vectors.shape[0]
    band = coupling.shape[0]
    tile = 2 * band if rows % (2 * band) == 0 else band
    spans = [pl.ds(at, tile) for at in range(0, rows, tile)]
    pairs = [(vectors_at, vectors), (weights_at, weights)]
    pairs += [(source.at[:, :, span], inverse.at[:, :, span]) for span in spans]
    pairs += [(upper_at.at[pl.ds(rows - band, band)], coupling)]
    copies = [pltpu.make_async_copy(*pair, arrived.at[i]) for i, pair in enumerate(pairs)]
    for copy in copies:
        copy.start()
    for copy in copies[:2]:
        copy.wait()
    for i, span in enumerate(spans):
        copies[2 + i].wait()
        real = jnp.dot(inverse[0, 0, span], vectors[...], preferred_element_type=F32)
        imag = jnp.dot(inverse[0, 1, span], vectors[...], preferred_element_type=F32)
        base[span] = combine(weights, real, imag)
        if i == 0:
            tip[...] = tip_of(real, imag, band)
    copies[-1].wait()
    emit_messages(real, imag, coupling[...], tip[...], out_a, out_b)


def start(vectors, weights, upper_tiles, inverse):
    rows, columns = vectors.shape
    band = upper_tiles.shape[1]
    message = like((band, 2 * columns), BF16)
    outs = [like((rows, columns)), message, message]
    outs += [like(inverse.shape, BF16), like((band, band)), like(weights.shape)]
    far = lambda x: pltpu.with_memory_space_constraint(x, pltpu.HBM)
    return pl.pallas_call(
        start_kernel,
        in_specs=[pl.BlockSpec(memory_space=pltpu.HBM)] * 4,
        out_specs=[pl.BlockSpec(memory_space=pltpu.VMEM)] * len(outs),
        out_shape=outs,
        scratch_shapes=[
            pltpu.VMEM(vectors.shape, BF16),
            pltpu.VMEM((band, 2 * columns), BF16),
            pltpu.SemaphoreType.DMA((rows // band + 3,)),
        ],
        cost_estimate=pl.CostEstimate(
            flops=4 * rows * rows * columns, bytes_accessed=inverse.size * 2, transcendentals=0
        ),
        compiler_params=pltpu.CompilerParams(vmem_limit_bytes=GRANT),
        name="start",
    )(far(weights), far(inverse), far(vectors), far(upper_tiles))


def solve_kernel(weights, field, low, factor, coupling, inverse, base, out_a, out_b, tip, current):
    band = coupling.shape[0]
    rows = field.shape[0]
    high, rest = halves_of(factor[...])
    times = lambda a, b: lax.dot_general(a, b, NT, preferred_element_type=F32)
    result = times(field[...], high) + (times(field[...], rest) + times(low[...], high))
    current[...] = result.astype(BF16)
    tile = 2 * band if rows % (2 * band) == 0 else band
    for at in range(0, rows, tile):
        real = jnp.dot(inverse[0, 0, at : at + tile], current[...], preferred_element_type=F32)
        imag = jnp.dot(inverse[0, 1, at : at + tile], current[...], preferred_element_type=F32)
        base[at : at + tile] = combine(weights, real, imag)
        if at == 0:
            tip[...] = tip_of(real, imag, band)
    emit_messages(real, imag, coupling[...], tip[...], out_a, out_b)


def solve(field, low, factor, weights, coupling, inverse):
    rows, columns = field.shape
    band = coupling.shape[1]
    message = like((band, 2 * columns), BF16)
    return whole(
        solve_kernel,
        [like((rows, columns)), message, message],
        weights,
        field,
        low,
        factor,
        coupling,
        inverse,
        scratch=[pltpu.VMEM((band, 2 * columns), BF16), pltpu.VMEM((rows, columns), BF16)],
        flops=4 * rows * rows * columns,
    )


def correct_kernel(weights, base, got_a, got_b, coupling, inverse, own, *refs):
    sends, term = refs[:-1], refs[-1]
    band = coupling.shape[1]
    rows, columns = base.shape
    node = lax.axis_index("node")
    is_even = lax.rem(lax.axis_index("rows"), 2) == 0
    above = jnp.where(is_even, got_b[...], got_a[...])
    from_next = jnp.where(is_even, got_a[...], got_b[...])
    below = dot(coupling[...], from_next.astype(F32)).astype(BF16)
    total = base[...]
    for edge, columns_at in ((above, 0), (below, rows - band)):
        real, imag = edge[:, :columns].astype(F32), edge[:, columns:].astype(F32)
        part = slice(columns_at, columns_at + band)
        total = total + dot_two(inverse[0, 0, :, part], combine(weights, real, imag))
        total = total - dot_two(inverse[0, 1, :, part], weights[:, 0:1] * imag + weights[:, 1:2] * real)
    term[...] = total
    size = own.shape[0]
    steps = lax.axis_size("node")
    for s, out in enumerate((own,) + sends):
        where = pl.multiple_of((node ^ (s if s < steps else s - steps + 1)) * size, 8)
        value = term[pl.ds(where, size), :]
        if s >= steps:
            value = value - value.astype(BF16).astype(F32)
        out[...] = value.astype(out.dtype)


def correct(weights, base, got_a, got_b, coupling, inverse, parts):
    rows, columns = base.shape
    band = coupling.shape[1]
    count = lax.axis_size("node")
    size = rows // count
    outs = [like((size, columns))] + [like((size, columns), BF16)] * (parts * (count - 1))
    return whole(
        correct_kernel,
        outs,
        weights,
        base,
        got_a,
        got_b,
        coupling,
        inverse,
        scratch=[pltpu.VMEM((rows, columns), F32)],
        flops=16 * rows * band * columns,
    )


def place(blocks, out):
    node = lax.axis_index("node")
    size = blocks[0].shape[0]
    for step, block in enumerate(blocks):
        out[pl.ds(pl.multiple_of((node ^ step) * size, 8), size), :] = block[...]


def gram_kernel(*refs):
    *blocks, field, head, part, matrix = refs
    place(blocks, field)
    head[...] = field[: head.shape[0]]
    matrix[...] = lax.dot_general(field[...], field[...], TN, preferred_element_type=F32)
    size = part.shape[0]
    part[...] = matrix[pl.ds(pl.multiple_of(lax.axis_index("node") * size, 8), size), :]


def gram_slice(blocks, band):
    rows, columns = blocks[0].shape
    count = len(blocks)
    outs = [
        like((rows * count, columns), BF16),
        like((band, columns), BF16),
        like((columns // count, columns)),
    ]
    scratch = [pltpu.VMEM((columns, columns), F32)]
    return whole(gram_kernel, outs, *blocks, scratch=scratch)


def join_kernel(*refs):
    place(refs[:-1], refs[-1])


def join(blocks):
    rows, columns = blocks[0].shape
    return whole(join_kernel, like((rows * len(blocks), columns), BF16), *blocks)


def eliminate(block, out, base):
    count = block.shape[0]
    full = (GROUP, count)
    lane = lax.broadcasted_iota(jnp.int32, full, 1)
    span = range(GROUP)
    tiles = [block[t * GROUP : (t + 1) * GROUP] for t in range(count // GROUP)]
    for t, tile in enumerate(tiles):
        k = t * GROUP
        tile = tiles[t]
        rows = [jnp.broadcast_to(tile[i : i + 1], full) for i in span]
        pivot = [[jnp.broadcast_to(rows[i][:, k + j : k + j + 1], full) for j in range(i + 1)] for i in span]
        scale = []
        low = [[None] * GROUP for _ in span]
        for j in span:
            scale.append(lax.rsqrt(pivot[j][j]))
            for i in range(j + 1, GROUP):
                low[i][j] = pivot[i][j] * scale[j]
            for i in range(j + 1, GROUP):
                for m in range(j + 1, i + 1):
                    pivot[i][m] = pivot[i][m] - low[i][j] * low[m][j]
        inv = [[None] * GROUP for _ in span]
        for j in span:
            inv[j][j] = scale[j]
            for i in range(j + 1, GROUP):
                total = low[i][j] * inv[j][j]
                for m in range(j + 1, i):
                    total = total + low[i][m] * inv[m][j]
                inv[i][j] = -total * scale[i]
        inside = (lane >= k) & (lane < k + GROUP)
        rows = [jnp.where(inside, jnp.where(lane == k + i, 1.0, 0.0), rows[i]) for i in span]
        done = []
        for i in span:
            total = inv[i][0] * rows[0]
            for j in range(1, i + 1):
                total = total + inv[i][j] * rows[j]
            done.append(total)
            at = base + k + i
            out[at : at + 1, base : base + count] = jnp.where(lane < k + GROUP, total, 0.0)[:1]
        if t + 1 < len(tiles):
            back = []
            for j in span:
                total = inv[j][j] * done[j]
                for i in range(j + 1, GROUP):
                    total = total + inv[i][j] * done[i]
                back.append(total)
            for u in range(t + 1, len(tiles)):
                old = tiles[u]
                new = jnp.where(inside, 0.0, old)
                for j in span:
                    new = new - old[:, k + j : k + j + 1] * back[j]
                tiles[u] = new


def first_factor_kernel(order, *refs):
    *blocks, top, corner, rest, across, matrix = refs
    place(blocks, matrix)
    count = matrix.shape[0]
    half = count // 2
    values = matrix[...] * (1.0 / order)
    eye = lax.broadcasted_iota(jnp.int32, (count, count), 0) == lax.broadcasted_iota(
        jnp.int32, (count, count), 1
    )
    diagonal = jnp.where(eye, values, 0.0)
    scale = lax.rsqrt(jnp.sum(diagonal, 0, keepdims=True))
    down = lax.rsqrt(jnp.sum(diagonal, 1, keepdims=True))
    across[...] = scale
    values = values * scale * down
    eliminate(values[:half, :half], top, 0)
    beside = dot(top[...], values[:half, half:])
    corner[...] = dot_tn(beside, top[...])
    rest[...] = values[half:, half:] - dot_tn(beside, beside)


def second_factor_kernel(top, corner, rest, across, out):
    half = top.shape[0]
    out[:half, :half] = top[...]
    out[:half, half:] = jnp.zeros((half, half), F32)
    eliminate(rest[...], out, half)
    out[half:, :half] = -dot(out[half:, half:], corner[...])
    out[...] = out[...] * across[...]


def first_factor(blocks, order):
    columns = blocks[0].shape[1]
    half = like((columns // 2, columns // 2))
    return whole(
        functools.partial(first_factor_kernel, order),
        [half, half, half, like((1, columns))],
        *blocks,
        scratch=[pltpu.VMEM((columns, columns), F32)],
        flops=6 * 10**9,
    )


def second_factor(halves):
    columns = halves[3].shape[1]
    return whole(second_factor_kernel, like((columns, columns)), *halves, flops=6 * 10**9)


def next_head(head):
    count = lax.axis_size("rows")
    return lax.ppermute(head, "rows", [(i + 1, i) for i in range(count - 1)])


def band_kernel(extra, field, after, diag_tiles, upper_tiles, *refs):
    low, earlier, (part, image, matrix) = refs[:extra], refs[extra:-3], refs[-3:]
    band = after.shape[0]
    tiles = field.shape[0] // band

    def values(at):
        total = field[at].astype(F32)
        return total + low[0][at].astype(F32) if low else total

    for t in range(tiles):
        at = slice(t * band, (t + 1) * band)
        following = slice((t + 1) * band, (t + 2) * band)
        following = after[...].astype(F32) if t == tiles - 1 else values(following)
        image[at] = 0.5 * dot_three(diag_tiles[at], values(at)) + dot_three(upper_tiles[at], following)
    matrix[...] = dot_two(field[...], image[...], TN)
    if low:
        matrix[...] += lax.dot_general(
            low[0][...], image[...].astype(BF16), TN, preferred_element_type=F32
        )
    size = matrix.shape[0] // lax.axis_size("node")
    for ref in earlier:
        part[:-size] = ref[...]
    part[-size:] = matrix[pl.ds(pl.multiple_of(lax.axis_index("node") * size, 8), size), :]


def band_slice(field, low, after, diag_tiles, upper_tiles, earlier):
    rows, columns = field.shape
    size = columns // lax.axis_size("node")
    return whole(
        functools.partial(band_kernel, len(low)),
        like((size * (1 + sum(x.shape[0] // size for x in earlier)), columns)),
        field,
        after,
        diag_tiles,
        upper_tiles,
        *low,
        *earlier,
        scratch=[pltpu.VMEM((rows, columns), F32), pltpu.VMEM((columns, columns), F32)],
    )


def last_kernel(field, factor, out):
    out[...] = dot_two(field[...], factor[...], NT)


def projected_kernel(order, *refs):
    blocks, factors, (out, matrix) = refs[: -2 - ITERS], refs[-2 - ITERS : -2], refs[-2:]
    node = lax.axis_index("node")
    size = blocks[0].shape[0] // ITERS
    for k, factor in enumerate(factors):
        for step, block in enumerate(blocks):
            at = pl.multiple_of((node ^ step) * size, 8)
            matrix[pl.ds(at, size), :] = block[k * size : (k + 1) * size]
        value = dot_three(dot_three(factor[...], matrix[...]), factor[...], NT)
        out[k] = (value + value.T) * (1.0 / order)


def after(value, *others):
    return lax.optimization_barrier((value,) + others)[0]


def per_device(subspace, inverse, weights, diag_tiles, upper_tiles):
    order = float(subspace.shape[0] * lax.axis_size("rows"))
    band = upper_tiles.shape[1]
    partners = lax.axis_size("node") - 1
    columns = subspace.shape[1]
    factors, earlier = [], ()
    for iteration in range(ITERS):
        final = iteration == ITERS - 1
        if iteration == 0:
            base, out_a, out_b, inverse, coupling, weights = start(
                subspace, weights, upper_tiles, inverse
            )
        else:
            base, out_a, out_b = solve(field, low[0], factor, weights, coupling, inverse)
        got_a, got_b = core_swap(out_a), link_swap(out_b)
        own, *terms = correct(
            weights, base, got_a, got_b, coupling, inverse, 1 if final else 2
        )
        got = node_spread(terms[:partners])
        if not final:
            low_got = node_spread(terms[partners:])
        total = tree_sum([own] + [x.astype(F32) for x in got])
        piece = total.astype(BF16)
        blocks = [piece] + node_spread([piece] * partners)
        low = ()
        if not final:
            total, sent = lax.optimization_barrier((total, piece))
            total = total + tree_sum([x.astype(F32) for x in low_got])
            low_piece = (total - sent.astype(F32)).astype(BF16)
            low = (join([low_piece] + node_spread([low_piece] * partners)),)
        field, head, part = gram_slice(blocks, band)
        part = part + core_swap(part)
        following = next_head(after(head, part))
        total = chip_sum(part)
        gathered = [total] + node_spread([total] * partners)
        pair = band_slice(field, low, after(following, total), diag_tiles, upper_tiles, earlier)
        earlier = (pair,)
        halves = first_factor(gathered, order)
        if final:
            pair = pair + core_swap(pair)
            pair = chip_sum(after(pair, *gathered))
            pair = after(pair, *halves)
            spread = [pair] + node_spread([pair] * partners)
        factor = second_factor(halves)
        factors.append(factor)
    orthonormal = whole(last_kernel, jax.ShapeDtypeStruct(subspace.shape, F32), field, factor)
    projected = whole(
        functools.partial(projected_kernel, order),
        jax.ShapeDtypeStruct((ITERS, columns, columns), F32),
        *spread,
        *factors,
        scratch=[pltpu.VMEM((columns, columns), F32)],
    )
    return orthonormal, projected


def solution(mesh):
    placed = (
        P("rows", None),
        P("node", None, "rows", None),
        P("node", None),
        P("rows", None),
        P("rows", None),
    )
    return jax.shard_map(
        per_device, mesh=mesh, in_specs=placed, out_specs=(P("rows", None), P()), check_vma=False
    )
```

```python
import functools

import jax
import jax.numpy as jnp
from jax import lax
from jax.experimental import pallas as pl
from jax.experimental.pallas import tpu as pltpu
from jax.sharding import PartitionSpec as P


ITERS = 2
GROUP = 8
GRANT = 16 * 2**20

precise = lax.Precision.HIGHEST
F32 = jnp.float32
BF16 = jnp.bfloat16


def dot(left, right):
    return jnp.dot(left, right, precision=precise, preferred_element_type=F32)


def dot_tn(left, right):
    dims = (((0,), (0,)), ((), ()))
    return lax.dot_general(left, right, dims, precision=precise, preferred_element_type=F32)


def halves_of(value):
    high = value.astype(BF16)
    return high, (value - high.astype(F32)).astype(BF16)


def dot_three(left, right, dims=(((1,), (0,)), ((), ()))):
    times = lambda a, b: lax.dot_general(a, b, dims, preferred_element_type=F32)
    (a, b), (c, d) = halves_of(left), halves_of(right)
    return times(a, c) + (times(a, d) + times(b, c))


def dot_two(left, right, dims=(((1,), (0,)), ((), ()))):
    times = lambda a, b: lax.dot_general(a, b, dims, preferred_element_type=F32)
    c, d = halves_of(right)
    return times(left, c) + times(left, d)


NT = (((1,), (1,)), ((), ()))
TN = (((0,), (0,)), ((), ()))


def like(shape, dtype=F32):
    return pltpu.VMEM(shape, dtype)


def halves_of(value):
    high = value.astype(BF16)
    return high, (value - high.astype(F32)).astype(BF16)


def dot_three(left, right, dims=(((1,), (0,)), ((), ()))):
    times = lambda a, b: lax.dot_general(a, b, dims, preferred_element_type=F32)
    (a, b), (c, d) = halves_of(left), halves_of(right)
    return times(a, c) + (times(a, d) + times(b, c))


def dot_two(left, right, dims=(((1,), (0,)), ((), ()))):
    times = lambda a, b: lax.dot_general(a, b, dims, preferred_element_type=F32)
    c, d = halves_of(right)
    return times(left, c) + times(left, d)


NT = (((1,), (1,)), ((), ()))
TN = (((0,), (0,)), ((), ()))


def local(value):
    return pltpu.with_memory_space_constraint(value, pltpu.VMEM)


def whole(kernel, out_shape, *operands, scratch=(), flops=10**8):
    size = sum(x.size * x.dtype.itemsize for x in operands)
    vmem = pl.BlockSpec(memory_space=pltpu.VMEM)
    return pl.pallas_call(
        kernel,
        out_shape=out_shape,
        in_specs=[vmem for _ in operands],
        out_specs=jax.tree.map(lambda _: vmem, out_shape),
        scratch_shapes=list(scratch),
        cost_estimate=pl.CostEstimate(flops=flops, bytes_accessed=size, transcendentals=0),
        compiler_params=pltpu.CompilerParams(vmem_limit_bytes=GRANT),
    )(*[local(x) for x in operands])


def node_swap(block, step):
    count = lax.axis_size("node")
    return lax.ppermute(block, "node", [(i, i ^ step) for i in range(count)])


def core_swap(block):
    count = lax.axis_size("rows")
    return lax.ppermute(block, "rows", [(i, i ^ 1) for i in range(count)])


def link_swap(block):
    count = lax.axis_size("rows")
    pairs = [(i, i + 1) for i in range(1, count - 1, 2)]
    return lax.ppermute(block, "rows", pairs + [(b, a) for a, b in pairs])


def node_spread(blocks):
    return [node_swap(block, step + 1) for step, block in enumerate(blocks)]


def tree_sum(blocks):
    while len(blocks) > 1:
        odd = blocks[len(blocks) // 2 * 2 :]
        blocks = [a + b for a, b in zip(blocks[::2], blocks[1::2])] + odd
    return blocks[0]


def chip_sum(block):
    count = lax.axis_size("rows")
    chips = count // 2
    if chips <= 4:
        steps = range(1, chips)
        routes = [[(i, i ^ (2 * s)) for i in range(count)] for s in steps]
        return tree_sum([block] + [lax.ppermute(block, "rows", route) for route in routes])
    step = 2
    while step < count:
        block = block + lax.ppermute(block, "rows", [(i, i ^ step) for i in range(count)])
        step *= 2
    return block


def emit_messages(is_even, first, last, out_a, out_b):
    out_a[...] = jnp.where(is_even, last, first)
    out_b[...] = jnp.where(is_even, first, last)


def emit_messages(real, imag, coupling, tip, out_a, out_b):
    band = coupling.shape[0]
    is_even = lax.rem(lax.axis_index("rows"), 2) == 0
    last = jnp.concatenate([real[-band:], imag[-band:]], 1).astype(BF16)
    last = dot_tn(coupling, last.astype(F32)).astype(BF16)
    out_a[...] = jnp.where(is_even, last, tip)
    out_b[...] = jnp.where(is_even, tip, last)


def tip_of(real, imag, band):
    return jnp.concatenate([real[:band], imag[:band]], 1).astype(BF16)


def combine(weights, real, imag):
    return weights[:, 0:1] * real - weights[:, 1:2] * imag


def start_kernel(weights_at, source, vectors_at, upper_at, *refs):
    base, out_a, out_b, inverse, coupling, weights, vectors, tip, arrived = refs
    rows = vectors.shape[0]
    band = coupling.shape[0]
    tile = 2 * band if rows % (2 * band) == 0 else band
    spans = [pl.ds(at, tile) for at in range(0, rows, tile)]
    pairs = [(vectors_at, vectors), (weights_at, weights)]
    pairs += [(source.at[:, :, span], inverse.at[:, :, span]) for span in spans]
    pairs += [(upper_at.at[pl.ds(rows - band, band)], coupling)]
    copies = [pltpu.make_async_copy(*pair, arrived.at[i]) for i, pair in enumerate(pairs)]
    for copy in copies:
        copy.start()
    for copy in copies[:2]:
        copy.wait()
    for i, span in enumerate(spans):
        copies[2 + i].wait()
        real = jnp.dot(inverse[0, 0, span], vectors[...], preferred_element_type=F32)
        imag = jnp.dot(inverse[0, 1, span], vectors[...], preferred_element_type=F32)
        base[span] = combine(weights, real, imag)
        if i == 0:
            tip[...] = tip_of(real, imag, band)
    copies[-1].wait()
    emit_messages(real, imag, coupling[...], tip[...], out_a, out_b)


def start(vectors, weights, upper_tiles, inverse):
    rows, columns = vectors.shape
    band = upper_tiles.shape[1]
    message = like((band, 2 * columns), BF16)
    outs = [like((rows, columns)), message, message]
    outs += [like(inverse.shape, BF16), like((band, band)), like(weights.shape)]
    far = lambda x: pltpu.with_memory_space_constraint(x, pltpu.HBM)
    return pl.pallas_call(
        start_kernel,
        in_specs=[pl.BlockSpec(memory_space=pltpu.HBM)] * 4,
        out_specs=[pl.BlockSpec(memory_space=pltpu.VMEM)] * len(outs),
        out_shape=outs,
        scratch_shapes=[
            pltpu.VMEM(vectors.shape, BF16),
            pltpu.VMEM((band, 2 * columns), BF16),
            pltpu.SemaphoreType.DMA((rows // band + 3,)),
        ],
        cost_estimate=pl.CostEstimate(
            flops=4 * rows * rows * columns, bytes_accessed=inverse.size * 2, transcendentals=0
        ),
        compiler_params=pltpu.CompilerParams(vmem_limit_bytes=GRANT),
        name="start",
    )(far(weights), far(inverse), far(vectors), far(upper_tiles))


def solve_kernel(weights, field, low, factor, coupling, inverse, base, out_a, out_b, tip, current):
    band = coupling.shape[0]
    rows = field.shape[0]
    current[...] = refined(field[...], low[...], factor[...]).astype(BF16)
    tile = 2 * band if rows % (2 * band) == 0 else band
    for at in range(0, rows, tile):
        real = jnp.dot(inverse[0, 0, at : at + tile], current[...], preferred_element_type=F32)
        imag = jnp.dot(inverse[0, 1, at : at + tile], current[...], preferred_element_type=F32)
        base[at : at + tile] = combine(weights, real, imag)
        if at == 0:
            tip[...] = tip_of(real, imag, band)
    emit_messages(real, imag, coupling[...], tip[...], out_a, out_b)


def solve(field, low, factor, weights, coupling, inverse):
    rows, columns = field.shape
    band = coupling.shape[1]
    message = like((band, 2 * columns), BF16)
    return whole(
        solve_kernel,
        [like((rows, columns)), message, message],
        weights,
        field,
        low,
        factor,
        coupling,
        inverse,
        scratch=[pltpu.VMEM((band, 2 * columns), BF16), pltpu.VMEM((rows, columns), BF16)],
        flops=4 * rows * rows * columns,
    )


def correct_kernel(weights, base, got_a, got_b, coupling, inverse, own, *refs):
    sends, term = refs[:-1], refs[-1]
    band = coupling.shape[1]
    rows, columns = base.shape
    node = lax.axis_index("node")
    is_even = lax.rem(lax.axis_index("rows"), 2) == 0
    above = jnp.where(is_even, got_b[...], got_a[...])
    from_next = jnp.where(is_even, got_a[...], got_b[...])
    below = dot(coupling[...], from_next.astype(F32)).astype(BF16)
    total = base[...]
    for edge, columns_at in ((above, 0), (below, rows - band)):
        real, imag = edge[:, :columns].astype(F32), edge[:, columns:].astype(F32)
        part = slice(columns_at, columns_at + band)
        total = total + dot_two(inverse[0, 0, :, part], combine(weights, real, imag))
        total = total - dot_two(inverse[0, 1, :, part], weights[:, 0:1] * imag + weights[:, 1:2] * real)
    term[...] = total
    size = own.shape[0]
    steps = lax.axis_size("node")
    for s, out in enumerate((own,) + sends):
        where = pl.multiple_of((node ^ (s if s < steps else s - steps + 1)) * size, 8)
        value = term[pl.ds(where, size), :]
        if s >= steps:
            value = value - value.astype(BF16).astype(F32)
        out[...] = value.astype(out.dtype)


def correct(weights, base, got_a, got_b, coupling, inverse, parts):
    rows, columns = base.shape
    band = coupling.shape[1]
    count = lax.axis_size("node")
    size = rows // count
    outs = [like((size, columns))] + [like((size, columns), BF16)] * (parts * (count - 1))
    return whole(
        correct_kernel,
        outs,
        weights,
        base,
        got_a,
        got_b,
        coupling,
        inverse,
        scratch=[pltpu.VMEM((rows, columns), F32)],
        flops=16 * rows * band * columns,
    )


def place(blocks, out):
    node = lax.axis_index("node")
    size = blocks[0].shape[0]
    for step, block in enumerate(blocks):
        out[pl.ds(pl.multiple_of((node ^ step) * size, 8), size), :] = block[...]


def gram_kernel(*refs):
    *blocks, field, head, part, matrix = refs
    place(blocks, field)
    head[...] = field[: head.shape[0]]
    matrix[...] = lax.dot_general(field[...], field[...], TN, preferred_element_type=F32)
    size = part.shape[0]
    part[...] = matrix[pl.ds(pl.multiple_of(lax.axis_index("node") * size, 8), size), :]


def gram_slice(blocks, band):
    rows, columns = blocks[0].shape
    count = len(blocks)
    outs = [
        like((rows * count, columns), BF16),
        like((band, columns), BF16),
        like((columns // count, columns)),
    ]
    scratch = [pltpu.VMEM((columns, columns), F32)]
    return whole(gram_kernel, outs, *blocks, scratch=scratch)


def join_kernel(*refs):
    place(refs[:-1], refs[-1])


def join(blocks):
    rows, columns = blocks[0].shape
    return whole(join_kernel, like((rows * len(blocks), columns), BF16), *blocks)


def eliminate(block, out, base, spread):
    count = block.shape[0]
    full = (GROUP, count)
    lane = lax.broadcasted_iota(jnp.int32, full, 1)
    span = range(GROUP)
    tiles = [block[t * GROUP : (t + 1) * GROUP] for t in range(count // GROUP)]
    room = GROUP * (GROUP + 1)
    for t in range(len(tiles)):
        k = t * GROUP
        tile = tiles[t]
        slot = (t % 2) * room
        spread[slot : slot + GROUP] = tile
        for j in span:
            at = slot + GROUP * (j + 1)
            spread[at : at + GROUP] = jnp.broadcast_to(tile[:, k + j : k + j + 1], full)
        across = lambda row: spread[pl.ds(slot + row, GROUP, stride=0), :]
        rows = [across(i) for i in span]
        pivot = [[across(GROUP * (j + 1) + i) for j in range(i + 1)] for i in span]
        scale = []
        low = [[None] * GROUP for _ in span]
        for j in span:
            scale.append(lax.rsqrt(pivot[j][j]))
            for i in range(j + 1, GROUP):
                low[i][j] = pivot[i][j] * scale[j]
            for i in range(j + 1, GROUP):
                for m in range(j + 1, i + 1):
                    pivot[i][m] = pivot[i][m] - low[i][j] * low[m][j]
        inv = [[None] * GROUP for _ in span]
        for j in span:
            inv[j][j] = scale[j]
            for i in range(j + 1, GROUP):
                total = low[i][j] * inv[j][j]
                for m in range(j + 1, i):
                    total = total + low[i][m] * inv[m][j]
                inv[i][j] = -total * scale[i]
        inside = (lane >= k) & (lane < k + GROUP)
        rows = [jnp.where(inside, jnp.where(lane == k + i, 1.0, 0.0), rows[i]) for i in span]
        done = []
        for i in span:
            total = inv[i][0] * rows[0]
            for j in range(1, i + 1):
                total = total + inv[i][j] * rows[j]
            done.append(total)
            at = base + k + i
            out[at : at + 1, base : base + count] = jnp.where(lane < k + GROUP, total, 0.0)[:1]
        if t + 1 < len(tiles):
            back = []
            for j in span:
                total = inv[j][j] * done[j]
                for i in range(j + 1, GROUP):
                    total = total + inv[i][j] * done[i]
                back.append(total)
            for u in range(t + 1, len(tiles)):
                old = tiles[u]
                new = jnp.where(inside, 0.0, old)
                for j in span:
                    new = new - old[:, k + j : k + j + 1] * back[j]
                tiles[u] = new


def first_factor_kernel(order, *refs):
    *blocks, top, corner, rest, across, matrix, spread = refs
    place(blocks, matrix)
    count = matrix.shape[0]
    half = count // 2
    values = matrix[...] * (1.0 / order)
    eye = lax.broadcasted_iota(jnp.int32, (count, count), 0) == lax.broadcasted_iota(
        jnp.int32, (count, count), 1
    )
    diagonal = jnp.where(eye, values, 0.0)
    scale = lax.rsqrt(jnp.sum(diagonal, 0, keepdims=True))
    down = lax.rsqrt(jnp.sum(diagonal, 1, keepdims=True))
    across[...] = scale
    values = values * scale * down
    eliminate(values[:half, :half], top, 0, spread)
    beside = dot(top[...], values[:half, half:])
    corner[...] = dot_tn(beside, top[...])
    rest[...] = values[half:, half:] - dot_tn(beside, beside)


def second_factor_kernel(top, corner, rest, across, out, spread):
    half = top.shape[0]
    out[:half, :half] = top[...]
    out[:half, half:] = jnp.zeros((half, half), F32)
    eliminate(rest[...], out, half, spread)
    out[half:, :half] = -dot(out[half:, half:], corner[...])
    out[...] = out[...] * across[...]


def spread_room(columns):
    return pltpu.VMEM((2 * GROUP * (GROUP + 1), columns // 2), F32)


def first_factor(blocks, order):
    columns = blocks[0].shape[1]
    half = like((columns // 2, columns // 2))
    return whole(
        functools.partial(first_factor_kernel, order),
        [half, half, half, like((1, columns))],
        *blocks,
        scratch=[pltpu.VMEM((columns, columns), F32), spread_room(columns)],
        flops=6 * 10**9,
    )


def second_factor(halves):
    columns = halves[3].shape[1]
    return whole(
        second_factor_kernel,
        like((columns, columns)),
        *halves,
        scratch=[spread_room(columns)],
        flops=6 * 10**9,
    )


def next_head(head):
    count = lax.axis_size("rows")
    return lax.ppermute(head, "rows", [(i + 1, i) for i in range(count - 1)])


def band_kernel(field, low, after, diag_tiles, upper_tiles, part, image, matrix):
    band = after.shape[0]
    tiles = field.shape[0] // band

    def values(at):
        return field[at].astype(F32) + low[at].astype(F32)

    for t in range(tiles):
        at = slice(t * band, (t + 1) * band)
        following = slice((t + 1) * band, (t + 2) * band)
        following = after[...].astype(F32) if t == tiles - 1 else values(following)
        image[at] = 0.5 * dot_three(diag_tiles[at], values(at)) + dot_three(upper_tiles[at], following)
    matrix[...] = dot_two(field[...], image[...], TN)
    matrix[...] += lax.dot_general(
        low[...], image[...].astype(BF16), TN, preferred_element_type=F32
    )
    size = part.shape[0]
    part[...] = matrix[pl.ds(pl.multiple_of(lax.axis_index("node") * size, 8), size), :]


def band_slice(field, low, after, diag_tiles, upper_tiles):
    rows, columns = field.shape
    return whole(
        band_kernel,
        like((columns // lax.axis_size("node"), columns)),
        field,
        low,
        after,
        diag_tiles,
        upper_tiles,
        scratch=[pltpu.VMEM((rows, columns), F32), pltpu.VMEM((columns, columns), F32)],
    )


def refined(field, low, factor):
    high, rest = halves_of(factor)
    times = lambda a, b: lax.dot_general(a, b, NT, preferred_element_type=F32)
    return times(field, high) + (times(field, rest) + times(low, high))


def last_kernel(field, low, factor, out):
    out[...] = refined(field[...], low[...], factor[...])


def projected_kernel(order, *refs):
    blocks, factors, (out, matrix) = refs[: -2 - ITERS], refs[-2 - ITERS : -2], refs[-2:]
    node = lax.axis_index("node")
    size = blocks[0].shape[0] // ITERS
    for k, factor in enumerate(factors):
        for step, block in enumerate(blocks):
            at = pl.multiple_of((node ^ step) * size, 8)
            matrix[pl.ds(at, size), :] = block[k * size : (k + 1) * size]
        value = dot_three(dot_three(factor[...], matrix[...]), factor[...], NT)
        out[k] = (value + value.T) * (1.0 / order)


def after(value, *others):
    return lax.optimization_barrier((value,) + others)[0]


def per_device(subspace, inverse, weights, diag_tiles, upper_tiles):
    order = float(subspace.shape[0] * lax.axis_size("rows"))
    band = upper_tiles.shape[1]
    partners = lax.axis_size("node") - 1
    columns = subspace.shape[1]
    factors, pairs = [], []
    for iteration in range(ITERS):
        final = iteration == ITERS - 1
        if iteration == 0:
            base, out_a, out_b, inverse, coupling, weights = start(
                subspace, weights, upper_tiles, inverse
            )
        else:
            base, out_a, out_b = solve(field, low, factor, weights, coupling, inverse)
        got_b = link_swap(out_b)
        got_a = core_swap(out_a)
        own, *terms = correct(
            weights, base, got_a, got_b, coupling, inverse, 1 if final else 2
        )
        got = node_spread(terms[:partners])
        if not final:
            low_got = node_spread(terms[partners:])
        total = tree_sum([own] + [x.astype(F32) for x in got])
        piece = total.astype(BF16)
        blocks = [piece] + node_spread([piece] * partners)
        total, sent = lax.optimization_barrier((total, piece))
        if not final:
            total = total + tree_sum([x.astype(F32) for x in low_got])
        low_piece = (total - sent.astype(F32)).astype(BF16)
        low = join([low_piece] + node_spread([low_piece] * partners))
        field, head, part = gram_slice(blocks, band)
        part = part + core_swap(part)
        following = next_head(after(head, part))
        total = chip_sum(part)
        gathered = [total] + node_spread([total] * partners)
        pair = band_slice(field, low, after(following, total), diag_tiles, upper_tiles)
        halves = first_factor(gathered, order)
        pair = pair + core_swap(pair)
        pairs.append(chip_sum(after(pair, *gathered)))
        if final:
            pair = after(jnp.concatenate(pairs, 0), *halves)
            spread = [pair] + node_spread([pair] * partners)
        factor = second_factor(halves)
        factors.append(factor)
    orthonormal = whole(last_kernel, jax.ShapeDtypeStruct(subspace.shape, F32), field, low, factor)
    projected = whole(
        functools.partial(projected_kernel, order),
        jax.ShapeDtypeStruct((ITERS, columns, columns), F32),
        *spread,
        *factors,
        scratch=[pltpu.VMEM((columns, columns), F32)],
    )
    return orthonormal, projected


def solution(mesh):
    placed = (
        P("rows", None),
        P("node", None, "rows", None),
        P("node", None),
        P("rows", None),
        P("rows", None),
    )
    return jax.shard_map(
        per_device, mesh=mesh, in_specs=placed, out_specs=(P("rows", None), P()), check_vma=False
    )
```

```python
import functools

import jax
import jax.numpy as jnp
from jax import lax
from jax.experimental import pallas as pl
from jax.experimental.pallas import tpu as pltpu
from jax.sharding import PartitionSpec as P


ITERS = 2
GROUP = 8
GRANT = 16 * 2**20

precise = lax.Precision.HIGHEST
F32 = jnp.float32
BF16 = jnp.bfloat16


def dot(left, right):
    return jnp.dot(left, right, precision=precise, preferred_element_type=F32)


def dot_tn(left, right):
    dims = (((0,), (0,)), ((), ()))
    return lax.dot_general(left, right, dims, precision=precise, preferred_element_type=F32)


def halves_of(value):
    high = value.astype(BF16)
    return high, (value - high.astype(F32)).astype(BF16)


def dot_three(left, right, dims=(((1,), (0,)), ((), ()))):
    times = lambda a, b: lax.dot_general(a, b, dims, preferred_element_type=F32)
    (a, b), (c, d) = halves_of(left), halves_of(right)
    return times(a, c) + (times(a, d) + times(b, c))


def dot_two(left, right, dims=(((1,), (0,)), ((), ()))):
    times = lambda a, b: lax.dot_general(a, b, dims, preferred_element_type=F32)
    c, d = halves_of(right)
    return times(left, c) + times(left, d)


NT = (((1,), (1,)), ((), ()))
TN = (((0,), (0,)), ((), ()))


def like(shape, dtype=F32):
    return pltpu.VMEM(shape, dtype)


def halves_of(value):
    high = value.astype(BF16)
    return high, (value - high.astype(F32)).astype(BF16)


def dot_three(left, right, dims=(((1,), (0,)), ((), ()))):
    times = lambda a, b: lax.dot_general(a, b, dims, preferred_element_type=F32)
    (a, b), (c, d) = halves_of(left), halves_of(right)
    return times(a, c) + (times(a, d) + times(b, c))


def dot_two(left, right, dims=(((1,), (0,)), ((), ()))):
    times = lambda a, b: lax.dot_general(a, b, dims, preferred_element_type=F32)
    c, d = halves_of(right)
    return times(left, c) + times(left, d)


NT = (((1,), (1,)), ((), ()))
TN = (((0,), (0,)), ((), ()))


def local(value):
    return pltpu.with_memory_space_constraint(value, pltpu.VMEM)


def whole(kernel, out_shape, *operands, scratch=(), flops=10**8):
    size = sum(x.size * x.dtype.itemsize for x in operands)
    vmem = pl.BlockSpec(memory_space=pltpu.VMEM)
    return pl.pallas_call(
        kernel,
        out_shape=out_shape,
        in_specs=[vmem for _ in operands],
        out_specs=jax.tree.map(lambda _: vmem, out_shape),
        scratch_shapes=list(scratch),
        cost_estimate=pl.CostEstimate(flops=flops, bytes_accessed=size, transcendentals=0),
        compiler_params=pltpu.CompilerParams(vmem_limit_bytes=GRANT),
    )(*[local(x) for x in operands])


def node_swap(block, step):
    count = lax.axis_size("node")
    return lax.ppermute(block, "node", [(i, i ^ step) for i in range(count)])


def core_swap(block):
    count = lax.axis_size("rows")
    return lax.ppermute(block, "rows", [(i, i ^ 1) for i in range(count)])


def link_swap(block):
    count = lax.axis_size("rows")
    pairs = [(i, i + 1) for i in range(1, count - 1, 2)]
    return lax.ppermute(block, "rows", pairs + [(b, a) for a, b in pairs])


def node_spread(blocks):
    return [node_swap(block, step + 1) for step, block in enumerate(blocks)]


def tree_sum(blocks):
    while len(blocks) > 1:
        odd = blocks[len(blocks) // 2 * 2 :]
        blocks = [a + b for a, b in zip(blocks[::2], blocks[1::2])] + odd
    return blocks[0]


def chip_sum(block):
    count = lax.axis_size("rows")
    chips = count // 2
    if chips <= 4:
        steps = range(1, chips)
        routes = [[(i, i ^ (2 * s)) for i in range(count)] for s in steps]
        return tree_sum([block] + [lax.ppermute(block, "rows", route) for route in routes])
    step = 2
    while step < count:
        block = block + lax.ppermute(block, "rows", [(i, i ^ step) for i in range(count)])
        step *= 2
    return block


def combine(weights, real, imag):
    return weights[:, 0:1] * real - weights[:, 1:2] * imag


def emit_messages(vectors, top, bottom, coupling, out_a, out_b):
    is_even = lax.rem(lax.axis_index("rows"), 2) == 0
    times = lambda block: jnp.dot(block, vectors, preferred_element_type=F32)
    both = lambda rows: jnp.concatenate([times(rows[0]), times(rows[1])], 1).astype(BF16)
    first, last = both(top), both(bottom)
    last = dot_tn(coupling, last.astype(F32)).astype(BF16)
    out_a[...] = jnp.where(is_even, last, first)
    out_b[...] = jnp.where(is_even, first, last)


def start_kernel(source, vectors_at, upper_at, *refs):
    out_a, out_b, coupling, vectors, ends, arrived = refs
    rows = vectors.shape[0]
    band = coupling.shape[0]
    pairs = [
        (vectors_at, vectors),
        (source.at[0, :, pl.ds(0, band)], ends.at[0]),
        (source.at[0, :, pl.ds(rows - band, band)], ends.at[1]),
        (upper_at.at[pl.ds(rows - band, band)], coupling),
    ]
    copies = [pltpu.make_async_copy(*pair, arrived.at[i]) for i, pair in enumerate(pairs)]
    for copy in copies:
        copy.start()
    for copy in copies:
        copy.wait()
    emit_messages(vectors[...], ends.at[0], ends.at[1], coupling[...], out_a, out_b)


def from_hbm(kernel, outs, scratch, copies, *operands):
    far = lambda x: pltpu.with_memory_space_constraint(x, pltpu.HBM)
    kinds = [pltpu.HBM if is_far else pltpu.VMEM for _, is_far in operands]
    return pl.pallas_call(
        kernel,
        in_specs=[pl.BlockSpec(memory_space=kind) for kind in kinds],
        out_specs=[pl.BlockSpec(memory_space=pltpu.VMEM)] * len(outs),
        out_shape=outs,
        scratch_shapes=scratch + [pltpu.SemaphoreType.DMA((copies,))],
        cost_estimate=pl.CostEstimate(flops=10**8, bytes_accessed=10**6, transcendentals=0),
        compiler_params=pltpu.CompilerParams(vmem_limit_bytes=GRANT),
    )(*[far(x) if is_far else local(x) for x, is_far in operands])


def start(vectors, upper_tiles, inverse):
    rows, columns = vectors.shape
    band = upper_tiles.shape[1]
    message = like((band, 2 * columns), BF16)
    outs = [message, message, like((band, band)), like(vectors.shape, BF16)]
    scratch = [pltpu.VMEM((2, 2, band, rows), BF16)]
    operands = [(inverse, True), (vectors, True), (upper_tiles, True)]
    return from_hbm(start_kernel, outs, scratch, 4, *operands)


def tile_of(rows, band):
    return 2 * band if rows % (2 * band) == 0 else band


def near_edge(weights, got, coupling, inverse, on_chip):
    rows, columns = inverse.shape[2], got.shape[1] // 2
    band = coupling.shape[0]
    is_even = lax.rem(lax.axis_index("rows"), 2) == 0
    is_next = is_even if on_chip else jnp.logical_not(is_even)
    below = dot(coupling[...], got[...].astype(F32)).astype(BF16)
    edge = jnp.where(is_next, below, got[...]).astype(F32)
    real, imag = edge[:, :columns], edge[:, columns:]
    at = pl.multiple_of(jnp.where(is_next, rows - band, 0), band)
    left = dot_two(inverse[0, 0, :, pl.ds(at, band)], combine(weights, real, imag))
    right = weights[:, 0:1] * imag + weights[:, 1:2] * real
    return left - dot_two(inverse[0, 1, :, pl.ds(at, band)], right)


def products(weights, vectors, inverse, span):
    real = jnp.dot(inverse[0, 0, span], vectors[...], preferred_element_type=F32)
    imag = jnp.dot(inverse[0, 1, span], vectors[...], preferred_element_type=F32)
    return combine(weights, real, imag)


def start_base_kernel(weights_at, source, vectors, coupling, got, base, inverse, weights, arrived):
    rows = vectors.shape[0]
    tile = tile_of(rows, coupling.shape[0])
    spans = [pl.ds(at, tile) for at in range(0, rows, tile)]
    pairs = [(weights_at, weights)]
    pairs += [(source.at[:, :, span], inverse.at[:, :, span]) for span in spans]
    copies = [pltpu.make_async_copy(*pair, arrived.at[i]) for i, pair in enumerate(pairs)]
    for copy in copies:
        copy.start()
    copies[0].wait()
    for copy, span in zip(copies[1:], spans):
        copy.wait()
        base[span] = products(weights, vectors, inverse, span)
    base[...] += near_edge(weights, got, coupling, inverse, True)


def start_base(weights, inverse, vectors, coupling, got):
    rows, columns = vectors.shape
    outs = [like((rows, columns)), like(inverse.shape, BF16), like(weights.shape)]
    operands = [(weights, True), (inverse, True), (vectors, False), (coupling, False), (got, False)]
    return from_hbm(start_base_kernel, outs, [], rows // coupling.shape[0] + 1, *operands)


def refined(field, low, factor):
    high, rest = halves_of(factor)
    times = lambda a, b: lax.dot_general(a, b, NT, preferred_element_type=F32)
    return times(field, high) + (times(field, rest) + times(low, high))


def solve_kernel(field, low, factor, coupling, inverse, out_a, out_b, current):
    band = coupling.shape[0]
    current[...] = refined(field[...], low[...], factor[...]).astype(BF16)
    top, bottom = inverse.at[0, :, :band], inverse.at[0, :, -band:]
    emit_messages(current[...], top, bottom, coupling[...], out_a, out_b)


def solve(field, low, factor, coupling, inverse):
    rows, columns = field.shape
    message = like((coupling.shape[0], 2 * columns), BF16)
    outs = [message, message, like((rows, columns), BF16)]
    return whole(solve_kernel, outs, field, low, factor, coupling, inverse)


def base_kernel(weights, vectors, coupling, inverse, got, base):
    rows = vectors.shape[0]
    tile = tile_of(rows, coupling.shape[0])
    for at in range(0, rows, tile):
        span = pl.ds(at, tile)
        base[span] = products(weights, vectors, inverse, span)
    base[...] += near_edge(weights, got, coupling, inverse, True)


def solve_base(weights, vectors, coupling, inverse, got):
    return whole(base_kernel, like(vectors.shape), weights, vectors, coupling, inverse, got)


def correct_kernel(weights, base, got, coupling, inverse, own, *refs):
    sends, term = refs[:-1], refs[-1]
    node = lax.axis_index("node")
    term[...] = base[...] + near_edge(weights, got, coupling, inverse, False)
    size = own.shape[0]
    steps = lax.axis_size("node")
    for s, out in enumerate((own,) + sends):
        where = pl.multiple_of((node ^ (s if s < steps else s - steps + 1)) * size, 8)
        value = term[pl.ds(where, size), :]
        if s >= steps:
            value = value - value.astype(BF16).astype(F32)
        out[...] = value.astype(out.dtype)


def correct(weights, base, got, coupling, inverse, parts):
    rows, columns = base.shape
    count = lax.axis_size("node")
    size = rows // count
    outs = [like((size, columns))] + [like((size, columns), BF16)] * (parts * (count - 1))
    scratch = [pltpu.VMEM((rows, columns), F32)]
    return whole(correct_kernel, outs, weights, base, got, coupling, inverse, scratch=scratch)


def place(blocks, out):
    node = lax.axis_index("node")
    size = blocks[0].shape[0]
    for step, block in enumerate(blocks):
        out[pl.ds(pl.multiple_of((node ^ step) * size, 8), size), :] = block[...]


def gram_kernel(*refs):
    *blocks, field, head, part, matrix = refs
    place(blocks, field)
    head[...] = field[: head.shape[0]]
    matrix[...] = lax.dot_general(field[...], field[...], TN, preferred_element_type=F32)
    size = part.shape[0]
    part[...] = matrix[pl.ds(pl.multiple_of(lax.axis_index("node") * size, 8), size), :]


def gram_slice(blocks, band):
    rows, columns = blocks[0].shape
    count = len(blocks)
    outs = [
        like((rows * count, columns), BF16),
        like((band, columns), BF16),
        like((columns // count, columns)),
    ]
    scratch = [pltpu.VMEM((columns, columns), F32)]
    return whole(gram_kernel, outs, *blocks, scratch=scratch)


def join_kernel(*refs):
    place(refs[:-1], refs[-1])


def join(blocks):
    rows, columns = blocks[0].shape
    return whole(join_kernel, like((rows * len(blocks), columns), BF16), *blocks)


def eliminate(block, out, base, spread):
    count = block.shape[0]
    full = (GROUP, count)
    lane = lax.broadcasted_iota(jnp.int32, full, 1)
    span = range(GROUP)
    tiles = [block[t * GROUP : (t + 1) * GROUP] for t in range(count // GROUP)]
    room = GROUP * (GROUP + 1)
    for t in range(len(tiles)):
        k = t * GROUP
        tile = tiles[t]
        slot = (t % 2) * room
        spread[slot : slot + GROUP] = tile
        for j in span:
            at = slot + GROUP * (j + 1)
            spread[at : at + GROUP] = jnp.broadcast_to(tile[:, k + j : k + j + 1], full)
        across = lambda row: spread[pl.ds(slot + row, GROUP, stride=0), :]
        rows = [across(i) for i in span]
        pivot = [[across(GROUP * (j + 1) + i) for j in range(i + 1)] for i in span]
        scale = []
        low = [[None] * GROUP for _ in span]
        for j in span:
            scale.append(lax.rsqrt(pivot[j][j]))
            for i in range(j + 1, GROUP):
                low[i][j] = pivot[i][j] * scale[j]
            for i in range(j + 1, GROUP):
                for m in range(j + 1, i + 1):
                    pivot[i][m] = pivot[i][m] - low[i][j] * low[m][j]
        inv = [[None] * GROUP for _ in span]
        for j in span:
            inv[j][j] = scale[j]
            for i in range(j + 1, GROUP):
                total = low[i][j] * inv[j][j]
                for m in range(j + 1, i):
                    total = total + low[i][m] * inv[m][j]
                inv[i][j] = -total * scale[i]
        inside = (lane >= k) & (lane < k + GROUP)
        rows = [jnp.where(inside, jnp.where(lane == k + i, 1.0, 0.0), rows[i]) for i in span]
        done = []
        for i in span:
            total = inv[i][0] * rows[0]
            for j in range(1, i + 1):
                total = total + inv[i][j] * rows[j]
            done.append(total)
            at = base + k + i
            out[at : at + 1, base : base + count] = jnp.where(lane < k + GROUP, total, 0.0)[:1]
        if t + 1 < len(tiles):
            back = []
            for j in span:
                total = inv[j][j] * done[j]
                for i in range(j + 1, GROUP):
                    total = total + inv[i][j] * done[i]
                back.append(total)
            for u in range(t + 1, len(tiles)):
                old = tiles[u]
                new = jnp.where(inside, 0.0, old)
                for j in span:
                    new = new - old[:, k + j : k + j + 1] * back[j]
                tiles[u] = new


def first_factor_kernel(order, *refs):
    *blocks, top, corner, rest, across, matrix, spread = refs
    place(blocks, matrix)
    count = matrix.shape[0]
    half = count // 2
    values = matrix[...] * (1.0 / order)
    eye = lax.broadcasted_iota(jnp.int32, (count, count), 0) == lax.broadcasted_iota(
        jnp.int32, (count, count), 1
    )
    diagonal = jnp.where(eye, values, 0.0)
    scale = lax.rsqrt(jnp.sum(diagonal, 0, keepdims=True))
    down = lax.rsqrt(jnp.sum(diagonal, 1, keepdims=True))
    across[...] = scale
    values = values * scale * down
    eliminate(values[:half, :half], top, 0, spread)
    beside = dot(top[...], values[:half, half:])
    corner[...] = dot_tn(beside, top[...])
    rest[...] = values[half:, half:] - dot_tn(beside, beside)


def second_factor_kernel(top, corner, rest, across, out, spread):
    half = top.shape[0]
    out[:half, :half] = top[...]
    out[:half, half:] = jnp.zeros((half, half), F32)
    eliminate(rest[...], out, half, spread)
    out[half:, :half] = -dot(out[half:, half:], corner[...])
    out[...] = out[...] * across[...]


def spread_room(columns):
    return pltpu.VMEM((2 * GROUP * (GROUP + 1), columns // 2), F32)


def first_factor(blocks, order):
    columns = blocks[0].shape[1]
    half = like((columns // 2, columns // 2))
    return whole(
        functools.partial(first_factor_kernel, order),
        [half, half, half, like((1, columns))],
        *blocks,
        scratch=[pltpu.VMEM((columns, columns), F32), spread_room(columns)],
        flops=6 * 10**9,
    )


def second_factor(halves):
    columns = halves[3].shape[1]
    return whole(
        second_factor_kernel,
        like((columns, columns)),
        *halves,
        scratch=[spread_room(columns)],
        flops=6 * 10**9,
    )


def next_head(head):
    count = lax.axis_size("rows")
    return lax.ppermute(head, "rows", [(i + 1, i) for i in range(count - 1)])


def band_kernel(field, low, after, diag_tiles, upper_tiles, part, image, matrix):
    band = after.shape[0]
    tiles = field.shape[0] // band

    def values(at):
        return field[at].astype(F32) + low[at].astype(F32)

    for t in range(tiles):
        at = slice(t * band, (t + 1) * band)
        following = slice((t + 1) * band, (t + 2) * band)
        following = after[...].astype(F32) if t == tiles - 1 else values(following)
        image[at] = 0.5 * dot_three(diag_tiles[at], values(at)) + dot_three(upper_tiles[at], following)
    matrix[...] = dot_two(field[...], image[...], TN)
    matrix[...] += lax.dot_general(
        low[...], image[...].astype(BF16), TN, preferred_element_type=F32
    )
    size = part.shape[0]
    part[...] = matrix[pl.ds(pl.multiple_of(lax.axis_index("node") * size, 8), size), :]


def band_slice(field, low, after, diag_tiles, upper_tiles):
    rows, columns = field.shape
    return whole(
        band_kernel,
        like((columns // lax.axis_size("node"), columns)),
        field,
        low,
        after,
        diag_tiles,
        upper_tiles,
        scratch=[pltpu.VMEM((rows, columns), F32), pltpu.VMEM((columns, columns), F32)],
    )


def last_kernel(field, low, factor, out):
    out[...] = refined(field[...], low[...], factor[...])


def projected_kernel(order, *refs):
    blocks, factors, (out, matrix) = refs[: -2 - ITERS], refs[-2 - ITERS : -2], refs[-2:]
    node = lax.axis_index("node")
    size = blocks[0].shape[0] // ITERS
    for k, factor in enumerate(factors):
        for step, block in enumerate(blocks):
            at = pl.multiple_of((node ^ step) * size, 8)
            matrix[pl.ds(at, size), :] = block[k * size : (k + 1) * size]
        value = dot_three(dot_three(factor[...], matrix[...]), factor[...], NT)
        out[k] = (value + value.T) * (1.0 / order)


def after(value, *others):
    return lax.optimization_barrier((value,) + others)[0]


def per_device(subspace, inverse, weights, diag_tiles, upper_tiles):
    order = float(subspace.shape[0] * lax.axis_size("rows"))
    band = upper_tiles.shape[1]
    partners = lax.axis_size("node") - 1
    columns = subspace.shape[1]
    factors, pairs = [], []
    for iteration in range(ITERS):
        final = iteration == ITERS - 1
        if iteration == 0:
            out_a, out_b, coupling, vectors = start(subspace, upper_tiles, inverse)
        else:
            out_a, out_b, vectors = solve(field, low, factor, coupling, inverse)
        got_b = link_swap(out_b)
        got_a = core_swap(out_a)
        if iteration == 0:
            base, inverse, weights = start_base(weights, inverse, vectors, coupling, got_a)
        else:
            base = solve_base(weights, vectors, coupling, inverse, got_a)
        own, *terms = correct(weights, base, got_b, coupling, inverse, 1 if final else 2)
        got = node_spread(terms[:partners])
        if not final:
            low_got = node_spread(terms[partners:])
        total = tree_sum([own] + [x.astype(F32) for x in got])
        piece = total.astype(BF16)
        blocks = [piece] + node_spread([piece] * partners)
        total, sent = lax.optimization_barrier((total, piece))
        if not final:
            total = total + tree_sum([x.astype(F32) for x in low_got])
        low_piece = (total - sent.astype(F32)).astype(BF16)
        low = join([low_piece] + node_spread([low_piece] * partners))
        field, head, part = gram_slice(blocks, band)
        part = part + core_swap(part)
        following = next_head(after(head, part))
        total = chip_sum(part)
        gathered = [total] + node_spread([total] * partners)
        pair = band_slice(field, low, after(following, total), diag_tiles, upper_tiles)
        halves = first_factor(gathered, order)
        pair = pair + core_swap(pair)
        pairs.append(chip_sum(after(pair, *gathered)))
        if final:
            pair = after(jnp.concatenate(pairs, 0), *halves)
            spread = [pair] + node_spread([pair] * partners)
        factor = second_factor(halves)
        factors.append(factor)
    orthonormal = whole(last_kernel, jax.ShapeDtypeStruct(subspace.shape, F32), field, low, factor)
    projected = whole(
        functools.partial(projected_kernel, order),
        jax.ShapeDtypeStruct((ITERS, columns, columns), F32),
        *spread,
        *factors,
        scratch=[pltpu.VMEM((columns, columns), F32)],
    )
    return orthonormal, projected


def solution(mesh):
    placed = (
        P("rows", None),
        P("node", None, "rows", None),
        P("node", None),
        P("rows", None),
        P("rows", None),
    )
    return jax.shard_map(
        per_device, mesh=mesh, in_specs=placed, out_specs=(P("rows", None), P()), check_vma=False
    )
```

```python
import functools

import jax
import jax.numpy as jnp
from jax import lax
from jax.experimental import pallas as pl
from jax.experimental.pallas import tpu as pltpu
from jax.sharding import PartitionSpec as P


ITERS = 2
GROUP = 8
GRANT = 16 * 2**20

precise = lax.Precision.HIGHEST
F32 = jnp.float32
BF16 = jnp.bfloat16


def dot(left, right):
    return jnp.dot(left, right, precision=precise, preferred_element_type=F32)


def dot_tn(left, right):
    dims = (((0,), (0,)), ((), ()))
    return lax.dot_general(left, right, dims, precision=precise, preferred_element_type=F32)


def halves_of(value):
    high = value.astype(BF16)
    return high, (value - high.astype(F32)).astype(BF16)


def dot_three(left, right, dims=(((1,), (0,)), ((), ()))):
    times = lambda a, b: lax.dot_general(a, b, dims, preferred_element_type=F32)
    (a, b), (c, d) = halves_of(left), halves_of(right)
    return times(a, c) + (times(a, d) + times(b, c))


def dot_two(left, right, dims=(((1,), (0,)), ((), ()))):
    times = lambda a, b: lax.dot_general(a, b, dims, preferred_element_type=F32)
    c, d = halves_of(right)
    return times(left, c) + times(left, d)


NT = (((1,), (1,)), ((), ()))
TN = (((0,), (0,)), ((), ()))


def like(shape, dtype=F32):
    return pltpu.VMEM(shape, dtype)


def halves_of(value):
    high = value.astype(BF16)
    return high, (value - high.astype(F32)).astype(BF16)


def dot_three(left, right, dims=(((1,), (0,)), ((), ()))):
    times = lambda a, b: lax.dot_general(a, b, dims, preferred_element_type=F32)
    (a, b), (c, d) = halves_of(left), halves_of(right)
    return times(a, c) + (times(a, d) + times(b, c))


def dot_two(left, right, dims=(((1,), (0,)), ((), ()))):
    times = lambda a, b: lax.dot_general(a, b, dims, preferred_element_type=F32)
    c, d = halves_of(right)
    return times(left, c) + times(left, d)


NT = (((1,), (1,)), ((), ()))
TN = (((0,), (0,)), ((), ()))


def local(value):
    return pltpu.with_memory_space_constraint(value, pltpu.VMEM)


def whole(kernel, out_shape, *operands, scratch=(), flops=10**8):
    size = sum(x.size * x.dtype.itemsize for x in operands)
    vmem = pl.BlockSpec(memory_space=pltpu.VMEM)
    return pl.pallas_call(
        kernel,
        out_shape=out_shape,
        in_specs=[vmem for _ in operands],
        out_specs=jax.tree.map(lambda _: vmem, out_shape),
        scratch_shapes=list(scratch),
        cost_estimate=pl.CostEstimate(flops=flops, bytes_accessed=size, transcendentals=0),
        compiler_params=pltpu.CompilerParams(vmem_limit_bytes=GRANT),
    )(*[local(x) for x in operands])


def node_swap(block, step):
    count = lax.axis_size("node")
    return lax.ppermute(block, "node", [(i, i ^ step) for i in range(count)])


def core_swap(block):
    count = lax.axis_size("rows")
    return lax.ppermute(block, "rows", [(i, i ^ 1) for i in range(count)])


def link_swap(block):
    count = lax.axis_size("rows")
    pairs = [(i, i + 1) for i in range(1, count - 1, 2)]
    return lax.ppermute(block, "rows", pairs + [(b, a) for a, b in pairs])


def node_spread(blocks):
    return [node_swap(block, step + 1) for step, block in enumerate(blocks)]


def tree_sum(blocks):
    while len(blocks) > 1:
        odd = blocks[len(blocks) // 2 * 2 :]
        blocks = [a + b for a, b in zip(blocks[::2], blocks[1::2])] + odd
    return blocks[0]


def chip_sum(block):
    count = lax.axis_size("rows")
    chips = count // 2
    if chips <= 4:
        steps = range(1, chips)
        routes = [[(i, i ^ (2 * s)) for i in range(count)] for s in steps]
        return tree_sum([block] + [lax.ppermute(block, "rows", route) for route in routes])
    step = 2
    while step < count:
        block = block + lax.ppermute(block, "rows", [(i, i ^ step) for i in range(count)])
        step *= 2
    return block


def combine(weights, real, imag):
    return weights[:, 0:1] * real - weights[:, 1:2] * imag


def emit_messages(vectors, top, bottom, coupling, out_a, out_b):
    is_even = lax.rem(lax.axis_index("rows"), 2) == 0
    times = lambda block: jnp.dot(block, vectors, preferred_element_type=F32)
    both = lambda rows: jnp.concatenate([times(rows[0]), times(rows[1])], 1).astype(BF16)
    first, last = both(top), both(bottom)
    last = dot_tn(coupling, last.astype(F32)).astype(BF16)
    out_a[...] = jnp.where(is_even, last, first)
    out_b[...] = jnp.where(is_even, first, last)


def start_kernel(source, vectors_at, upper_at, *refs):
    out_a, out_b, coupling, vectors, ends, arrived = refs
    rows = vectors.shape[0]
    band = coupling.shape[0]
    pairs = [
        (vectors_at, vectors),
        (source.at[0, :, pl.ds(0, band)], ends.at[0]),
        (source.at[0, :, pl.ds(rows - band, band)], ends.at[1]),
        (upper_at.at[pl.ds(rows - band, band)], coupling),
    ]
    copies = [pltpu.make_async_copy(*pair, arrived.at[i]) for i, pair in enumerate(pairs)]
    for copy in copies:
        copy.start()
    for copy in copies:
        copy.wait()
    emit_messages(vectors[...], ends.at[0], ends.at[1], coupling[...], out_a, out_b)


def from_hbm(kernel, outs, scratch, copies, *operands):
    far = lambda x: pltpu.with_memory_space_constraint(x, pltpu.HBM)
    kinds = [pltpu.HBM if is_far else pltpu.VMEM for _, is_far in operands]
    return pl.pallas_call(
        kernel,
        in_specs=[pl.BlockSpec(memory_space=kind) for kind in kinds],
        out_specs=[pl.BlockSpec(memory_space=pltpu.VMEM)] * len(outs),
        out_shape=outs,
        scratch_shapes=scratch + [pltpu.SemaphoreType.DMA((copies,))],
        cost_estimate=pl.CostEstimate(flops=10**8, bytes_accessed=10**6, transcendentals=0),
        compiler_params=pltpu.CompilerParams(vmem_limit_bytes=GRANT),
    )(*[far(x) if is_far else local(x) for x, is_far in operands])


def start(vectors, upper_tiles, inverse):
    rows, columns = vectors.shape
    band = upper_tiles.shape[1]
    message = like((band, 2 * columns), BF16)
    outs = [message, message, like((band, band)), like(vectors.shape, BF16)]
    scratch = [pltpu.VMEM((2, 2, band, rows), BF16)]
    operands = [(inverse, True), (vectors, True), (upper_tiles, True)]
    return from_hbm(start_kernel, outs, scratch, 4, *operands)


def tile_of(rows, band):
    return 2 * band if rows % (2 * band) == 0 else band


def near_edge(weights, got, coupling, inverse, on_chip, factor=None):
    rows, columns = inverse.shape[2], got.shape[1] // 2
    band = coupling.shape[0]
    is_even = lax.rem(lax.axis_index("rows"), 2) == 0
    is_next = is_even if on_chip else jnp.logical_not(is_even)
    if factor is None:
        below = dot(coupling[...], got[...].astype(F32)).astype(BF16)
        edge = jnp.where(is_next, below, got[...]).astype(F32)
        real, imag = edge[:, :columns], edge[:, columns:]
    else:
        turned = [dot_three(got[:, at : at + columns], factor, NT) for at in (0, columns)]
        real, imag = [jnp.where(is_next, dot_three(coupling[...], x), x) for x in turned]
    at = pl.multiple_of(jnp.where(is_next, rows - band, 0), band)
    left = dot_two(inverse[0, 0, :, pl.ds(at, band)], combine(weights, real, imag))
    right = weights[:, 0:1] * imag + weights[:, 1:2] * real
    return left - dot_two(inverse[0, 1, :, pl.ds(at, band)], right)


def products(weights, vectors, inverse, span):
    real = jnp.dot(inverse[0, 0, span], vectors[...], preferred_element_type=F32)
    imag = jnp.dot(inverse[0, 1, span], vectors[...], preferred_element_type=F32)
    return combine(weights, real, imag)


def start_base_kernel(weights_at, source, vectors, coupling, got, base, inverse, weights, arrived):
    rows = vectors.shape[0]
    tile = tile_of(rows, coupling.shape[0])
    spans = [pl.ds(at, tile) for at in range(0, rows, tile)]
    pairs = [(weights_at, weights)]
    pairs += [(source.at[:, :, span], inverse.at[:, :, span]) for span in spans]
    copies = [pltpu.make_async_copy(*pair, arrived.at[i]) for i, pair in enumerate(pairs)]
    for copy in copies:
        copy.start()
    copies[0].wait()
    for copy, span in zip(copies[1:], spans):
        copy.wait()
        base[span] = products(weights, vectors, inverse, span)
    base[...] += near_edge(weights, got, coupling, inverse, True)


def start_base(weights, inverse, vectors, coupling, got):
    rows, columns = vectors.shape
    outs = [like((rows, columns)), like(inverse.shape, BF16), like(weights.shape)]
    operands = [(weights, True), (inverse, True), (vectors, False), (coupling, False), (got, False)]
    return from_hbm(start_base_kernel, outs, [], rows // coupling.shape[0] + 1, *operands)


def refined(field, low, factor):
    high, rest = halves_of(factor)
    times = lambda a, b: lax.dot_general(a, b, NT, preferred_element_type=F32)
    return times(field, high) + (times(field, rest) + times(low, high))


def tips_kernel(field, low, coupling, inverse, out_a, out_b):
    band = coupling.shape[0]
    is_even = lax.rem(lax.axis_index("rows"), 2) == 0

    def both(at):
        times = lambda part, x: jnp.dot(
            inverse[0, part, at : at + band], x, preferred_element_type=F32
        )
        of = lambda part: times(part, field[...]) + times(part, low[...])
        return jnp.concatenate([of(0), of(1)], 1)

    first = both(0)
    last = dot_tn(coupling[...], both(field.shape[0] - band))
    out_a[...] = jnp.where(is_even, last, first)
    out_b[...] = jnp.where(is_even, first, last)


def tips(field, low, coupling, inverse):
    message = like((coupling.shape[0], 2 * field.shape[1]))
    return whole(tips_kernel, [message, message], field, low, coupling, inverse)


def emit_term(term, own, sends):
    node = lax.axis_index("node")
    size = own.shape[0]
    steps = lax.axis_size("node")
    for s, out in enumerate((own,) + sends):
        where = pl.multiple_of((node ^ (s if s < steps else s - steps + 1)) * size, 8)
        value = term[pl.ds(where, size), :]
        if s >= steps:
            value = value - value.astype(BF16).astype(F32)
        out[...] = value.astype(out.dtype)


def solve_kernel(weights, field, low, factor, coupling, inverse, got_a, got_b, own, *refs):
    sends, (current, term) = refs[:-2], refs[-2:]
    current[...] = refined(field[...], low[...], factor[...]).astype(BF16)
    rows = field.shape[0]
    tile = tile_of(rows, coupling.shape[0])
    for at in range(0, rows, tile):
        span = pl.ds(at, tile)
        term[span] = products(weights, current, inverse, span)
    term[...] += near_edge(weights, got_a, coupling, inverse, True, factor[...])
    term[...] += near_edge(weights, got_b, coupling, inverse, False, factor[...])
    emit_term(term, own, sends)


def blocks_of(rows, columns, parts):
    count = lax.axis_size("node")
    size = rows // count
    return [like((size, columns))] + [like((size, columns), BF16)] * (parts * (count - 1))


def solve(weights, field, low, factor, coupling, inverse, got_a, got_b, parts):
    rows, columns = field.shape
    return whole(
        solve_kernel,
        blocks_of(rows, columns, parts),
        weights,
        field,
        low,
        factor,
        coupling,
        inverse,
        got_a,
        got_b,
        scratch=[pltpu.VMEM((rows, columns), BF16), pltpu.VMEM((rows, columns), F32)],
    )


def correct_kernel(weights, base, got, coupling, inverse, own, *refs):
    sends, term = refs[:-1], refs[-1]
    term[...] = base[...] + near_edge(weights, got, coupling, inverse, False)
    emit_term(term, own, sends)


def correct(weights, base, got, coupling, inverse, parts):
    rows, columns = base.shape
    outs = blocks_of(rows, columns, parts)
    scratch = [pltpu.VMEM((rows, columns), F32)]
    return whole(correct_kernel, outs, weights, base, got, coupling, inverse, scratch=scratch)


def place(blocks, out):
    node = lax.axis_index("node")
    size = blocks[0].shape[0]
    for step, block in enumerate(blocks):
        out[pl.ds(pl.multiple_of((node ^ step) * size, 8), size), :] = block[...]


def gram_kernel(*refs):
    *blocks, field, head, part, matrix = refs
    place(blocks, field)
    head[...] = field[: head.shape[0]]
    matrix[...] = lax.dot_general(field[...], field[...], TN, preferred_element_type=F32)
    size = part.shape[0]
    part[...] = matrix[pl.ds(pl.multiple_of(lax.axis_index("node") * size, 8), size), :]


def gram_slice(blocks, band):
    rows, columns = blocks[0].shape
    count = len(blocks)
    outs = [
        like((rows * count, columns), BF16),
        like((band, columns), BF16),
        like((columns // count, columns)),
    ]
    scratch = [pltpu.VMEM((columns, columns), F32)]
    return whole(gram_kernel, outs, *blocks, scratch=scratch)


def join_kernel(*refs):
    place(refs[:-1], refs[-1])


def join(blocks):
    rows, columns = blocks[0].shape
    return whole(join_kernel, like((rows * len(blocks), columns), BF16), *blocks)


def eliminate(block, out, base, spread):
    count = block.shape[0]
    full = (GROUP, count)
    lane = lax.broadcasted_iota(jnp.int32, full, 1)
    span = range(GROUP)
    tiles = [block[t * GROUP : (t + 1) * GROUP] for t in range(count // GROUP)]
    room = GROUP * (GROUP + 1)
    for t in range(len(tiles)):
        k = t * GROUP
        tile = tiles[t]
        slot = (t % 2) * room
        spread[slot : slot + GROUP] = tile
        for j in span:
            at = slot + GROUP * (j + 1)
            spread[at : at + GROUP] = jnp.broadcast_to(tile[:, k + j : k + j + 1], full)
        across = lambda row: spread[pl.ds(slot + row, GROUP, stride=0), :]
        rows = [across(i) for i in span]
        pivot = [[across(GROUP * (j + 1) + i) for j in range(i + 1)] for i in span]
        scale = []
        low = [[None] * GROUP for _ in span]
        for j in span:
            scale.append(lax.rsqrt(pivot[j][j]))
            for i in range(j + 1, GROUP):
                low[i][j] = pivot[i][j] * scale[j]
            for i in range(j + 1, GROUP):
                for m in range(j + 1, i + 1):
                    pivot[i][m] = pivot[i][m] - low[i][j] * low[m][j]
        inv = [[None] * GROUP for _ in span]
        for j in span:
            inv[j][j] = scale[j]
            for i in range(j + 1, GROUP):
                total = low[i][j] * inv[j][j]
                for m in range(j + 1, i):
                    total = total + low[i][m] * inv[m][j]
                inv[i][j] = -total * scale[i]
        inside = (lane >= k) & (lane < k + GROUP)
        rows = [jnp.where(inside, jnp.where(lane == k + i, 1.0, 0.0), rows[i]) for i in span]
        done = []
        for i in span:
            total = inv[i][0] * rows[0]
            for j in range(1, i + 1):
                total = total + inv[i][j] * rows[j]
            done.append(total)
            at = base + k + i
            out[at : at + 1, base : base + count] = jnp.where(lane < k + GROUP, total, 0.0)[:1]
        if t + 1 < len(tiles):
            back = []
            for j in span:
                total = inv[j][j] * done[j]
                for i in range(j + 1, GROUP):
                    total = total + inv[i][j] * done[i]
                back.append(total)
            for u in range(t + 1, len(tiles)):
                old = tiles[u]
                new = jnp.where(inside, 0.0, old)
                for j in span:
                    new = new - old[:, k + j : k + j + 1] * back[j]
                tiles[u] = new


def first_factor_kernel(order, *refs):
    *blocks, top, corner, rest, across, matrix, spread = refs
    place(blocks, matrix)
    count = matrix.shape[0]
    half = count // 2
    values = matrix[...] * (1.0 / order)
    eye = lax.broadcasted_iota(jnp.int32, (count, count), 0) == lax.broadcasted_iota(
        jnp.int32, (count, count), 1
    )
    diagonal = jnp.where(eye, values, 0.0)
    scale = lax.rsqrt(jnp.sum(diagonal, 0, keepdims=True))
    down = lax.rsqrt(jnp.sum(diagonal, 1, keepdims=True))
    across[...] = scale
    values = values * scale * down
    eliminate(values[:half, :half], top, 0, spread)
    beside = dot(top[...], values[:half, half:])
    corner[...] = dot_tn(beside, top[...])
    rest[...] = values[half:, half:] - dot_tn(beside, beside)


def second_factor_kernel(top, corner, rest, across, out, spread):
    half = top.shape[0]
    out[:half, :half] = top[...]
    out[:half, half:] = jnp.zeros((half, half), F32)
    eliminate(rest[...], out, half, spread)
    out[half:, :half] = -dot(out[half:, half:], corner[...])
    out[...] = out[...] * across[...]


def spread_room(columns):
    return pltpu.VMEM((2 * GROUP * (GROUP + 1), columns // 2), F32)


def first_factor(blocks, order):
    columns = blocks[0].shape[1]
    half = like((columns // 2, columns // 2))
    return whole(
        functools.partial(first_factor_kernel, order),
        [half, half, half, like((1, columns))],
        *blocks,
        scratch=[pltpu.VMEM((columns, columns), F32), spread_room(columns)],
        flops=6 * 10**9,
    )


def second_factor(halves):
    columns = halves[3].shape[1]
    return whole(
        second_factor_kernel,
        like((columns, columns)),
        *halves,
        scratch=[spread_room(columns)],
        flops=6 * 10**9,
    )


def next_head(head):
    count = lax.axis_size("rows")
    return lax.ppermute(head, "rows", [(i + 1, i) for i in range(count - 1)])


def band_kernel(field, low, after, diag_tiles, upper_tiles, part, image, matrix):
    band = after.shape[0]
    tiles = field.shape[0] // band

    def values(at):
        return field[at].astype(F32) + low[at].astype(F32)

    for t in range(tiles):
        at = slice(t * band, (t + 1) * band)
        following = slice((t + 1) * band, (t + 2) * band)
        following = after[...].astype(F32) if t == tiles - 1 else values(following)
        image[at] = 0.5 * dot_three(diag_tiles[at], values(at)) + dot_three(upper_tiles[at], following)
    matrix[...] = dot_two(field[...], image[...], TN)
    matrix[...] += lax.dot_general(
        low[...], image[...].astype(BF16), TN, preferred_element_type=F32
    )
    size = part.shape[0]
    part[...] = matrix[pl.ds(pl.multiple_of(lax.axis_index("node") * size, 8), size), :]


def band_slice(field, low, after, diag_tiles, upper_tiles):
    rows, columns = field.shape
    return whole(
        band_kernel,
        like((columns // lax.axis_size("node"), columns)),
        field,
        low,
        after,
        diag_tiles,
        upper_tiles,
        scratch=[pltpu.VMEM((rows, columns), F32), pltpu.VMEM((columns, columns), F32)],
    )


def finish_kernel(order, field, low, *refs):
    blocks, factors = refs[: -6 - ITERS], refs[-6 - ITERS : -6]
    vectors_at, projected_at, vectors, projected, matrix, sent = refs[-6:]
    rows = field.shape[0]
    tile = rows // 3 if rows % 48 == 0 else rows
    copies = []

    def send(source, target):
        copies.append(pltpu.make_async_copy(source, target, sent.at[len(copies)]))
        copies[-1].start()

    for at in range(0, rows, tile):
        span = pl.ds(at, tile)
        vectors[span] = refined(field[span], low[span], factors[-1][...])
        send(vectors.at[span], vectors_at.at[span])
    node = lax.axis_index("node")
    size = blocks[0].shape[0] // ITERS
    for k, factor in enumerate(factors):
        for step, block in enumerate(blocks):
            at = pl.multiple_of((node ^ step) * size, 8)
            matrix[pl.ds(at, size), :] = block[k * size : (k + 1) * size]
        value = dot_three(dot_three(factor[...], matrix[...]), factor[...], NT)
        projected[k] = (value + value.T) * (1.0 / order)
        send(projected.at[k], projected_at.at[k])
    for copy in copies:
        copy.wait()


def finish(field, low, blocks, factors, order):
    rows, columns = field.shape
    operands = [field, low, *blocks, *factors]
    vmem = pl.BlockSpec(memory_space=pltpu.VMEM)
    shapes = [(rows, columns), (ITERS, columns, columns)]
    return pl.pallas_call(
        functools.partial(finish_kernel, order),
        in_specs=[vmem for _ in operands],
        out_specs=[pl.BlockSpec(memory_space=pltpu.HBM)] * 2,
        out_shape=[jax.ShapeDtypeStruct(x, F32) for x in shapes],
        scratch_shapes=[pltpu.VMEM(x, F32) for x in shapes]
        + [pltpu.VMEM((columns, columns), F32), pltpu.SemaphoreType.DMA((3 + ITERS,))],
        cost_estimate=pl.CostEstimate(flops=10**9, bytes_accessed=10**6, transcendentals=0),
        compiler_params=pltpu.CompilerParams(vmem_limit_bytes=GRANT),
        name="finish",
    )(*[local(x) for x in operands])


def after(value, *others):
    return lax.optimization_barrier((value,) + others)[0]


def per_device(subspace, inverse, weights, diag_tiles, upper_tiles):
    order = float(subspace.shape[0] * lax.axis_size("rows"))
    band = upper_tiles.shape[1]
    partners = lax.axis_size("node") - 1
    factors, pairs = [], []
    for iteration in range(ITERS):
        final = iteration == ITERS - 1
        parts = 1 if final else 2
        if iteration == 0:
            out_a, out_b, coupling, vectors = start(subspace, upper_tiles, inverse)
            got_b = link_swap(out_b)
            got_a = core_swap(out_a)
            base, inverse, weights = start_base(weights, inverse, vectors, coupling, got_a)
            own, *terms = correct(weights, base, got_b, coupling, inverse, parts)
        else:
            own, *terms = solve(
                weights, field, low, factor, coupling, inverse, got_a, got_b, parts
            )
        got = node_spread(terms[:partners])
        if not final:
            low_got = node_spread(terms[partners:])
        total = tree_sum([own] + [x.astype(F32) for x in got])
        piece = total.astype(BF16)
        blocks = [piece] + node_spread([piece] * partners)
        total, sent = lax.optimization_barrier((total, piece))
        if not final:
            total = total + tree_sum([x.astype(F32) for x in low_got])
        low_piece = (total - sent.astype(F32)).astype(BF16)
        low = join([low_piece] + node_spread([low_piece] * partners))
        field, head, part = gram_slice(blocks, band)
        part = part + core_swap(part)
        following = next_head(after(head, part))
        total = chip_sum(part)
        gathered = [total] + node_spread([total] * partners)
        pair = band_slice(field, low, after(following, total), diag_tiles, upper_tiles)
        if not final:
            out_a, out_b = tips(field, low, coupling, inverse)
            got_b = link_swap(out_b)
            got_a = core_swap(out_a)
        halves = first_factor(gathered, order)
        pair = pair + core_swap(pair)
        pairs.append(chip_sum(after(pair, *gathered)))
        if final:
            pair = after(jnp.concatenate(pairs, 0), *halves)
            spread = [pair] + node_spread([pair] * partners)
        factor = second_factor(halves)
        factors.append(factor)
    orthonormal, projected = finish(field, low, spread, factors, order)
    return orthonormal, projected


def solution(mesh):
    placed = (
        P("rows", None),
        P("node", None, "rows", None),
        P("node", None),
        P("rows", None),
        P("rows", None),
    )
    return jax.shard_map(
        per_device, mesh=mesh, in_specs=placed, out_specs=(P("rows", None), P()), check_vma=False
    )
```

```python
import functools

import jax
import jax.numpy as jnp
from jax import lax
from jax.experimental import pallas as pl
from jax.experimental.pallas import tpu as pltpu
from jax.sharding import PartitionSpec as P


ITERS = 2
GROUP = 8
GRANT = 16 * 2**20

precise = lax.Precision.HIGHEST
F32 = jnp.float32
BF16 = jnp.bfloat16


def dot(left, right):
    return jnp.dot(left, right, precision=precise, preferred_element_type=F32)


def dot_tn(left, right):
    dims = (((0,), (0,)), ((), ()))
    return lax.dot_general(left, right, dims, precision=precise, preferred_element_type=F32)


def halves_of(value):
    high = value.astype(BF16)
    return high, (value - high.astype(F32)).astype(BF16)


def dot_three(left, right, dims=(((1,), (0,)), ((), ()))):
    times = lambda a, b: lax.dot_general(a, b, dims, preferred_element_type=F32)
    (a, b), (c, d) = halves_of(left), halves_of(right)
    return times(a, c) + (times(a, d) + times(b, c))


def dot_two(left, right, dims=(((1,), (0,)), ((), ()))):
    times = lambda a, b: lax.dot_general(a, b, dims, preferred_element_type=F32)
    c, d = halves_of(right)
    return times(left, c) + times(left, d)


NT = (((1,), (1,)), ((), ()))
TN = (((0,), (0,)), ((), ()))


def like(shape, dtype=F32):
    return pltpu.VMEM(shape, dtype)


def halves_of(value):
    high = value.astype(BF16)
    return high, (value - high.astype(F32)).astype(BF16)


def dot_three(left, right, dims=(((1,), (0,)), ((), ()))):
    times = lambda a, b: lax.dot_general(a, b, dims, preferred_element_type=F32)
    (a, b), (c, d) = halves_of(left), halves_of(right)
    return times(a, c) + (times(a, d) + times(b, c))


def dot_two(left, right, dims=(((1,), (0,)), ((), ()))):
    times = lambda a, b: lax.dot_general(a, b, dims, preferred_element_type=F32)
    c, d = halves_of(right)
    return times(left, c) + times(left, d)


NT = (((1,), (1,)), ((), ()))
TN = (((0,), (0,)), ((), ()))


def local(value):
    return pltpu.with_memory_space_constraint(value, pltpu.VMEM)


def whole(kernel, out_shape, *operands, scratch=(), flops=10**8):
    size = sum(x.size * x.dtype.itemsize for x in operands)
    vmem = pl.BlockSpec(memory_space=pltpu.VMEM)
    return pl.pallas_call(
        kernel,
        out_shape=out_shape,
        in_specs=[vmem for _ in operands],
        out_specs=jax.tree.map(lambda _: vmem, out_shape),
        scratch_shapes=list(scratch),
        cost_estimate=pl.CostEstimate(flops=flops, bytes_accessed=size, transcendentals=0),
        compiler_params=pltpu.CompilerParams(vmem_limit_bytes=GRANT),
    )(*[local(x) for x in operands])


def node_swap(block, step):
    count = lax.axis_size("node")
    return lax.ppermute(block, "node", [(i, i ^ step) for i in range(count)])


def core_swap(block):
    count = lax.axis_size("rows")
    return lax.ppermute(block, "rows", [(i, i ^ 1) for i in range(count)])


def link_swap(block):
    count = lax.axis_size("rows")
    pairs = [(i, i + 1) for i in range(1, count - 1, 2)]
    return lax.ppermute(block, "rows", pairs + [(b, a) for a, b in pairs])


def node_spread(blocks):
    return [node_swap(block, step + 1) for step, block in enumerate(blocks)]


def tree_sum(blocks):
    while len(blocks) > 1:
        odd = blocks[len(blocks) // 2 * 2 :]
        blocks = [a + b for a, b in zip(blocks[::2], blocks[1::2])] + odd
    return blocks[0]


def chip_sum(block):
    count = lax.axis_size("rows")
    chips = count // 2
    if chips <= 4:
        steps = range(1, chips)
        routes = [[(i, i ^ (2 * s)) for i in range(count)] for s in steps]
        return tree_sum([block] + [lax.ppermute(block, "rows", route) for route in routes])
    step = 2
    while step < count:
        block = block + lax.ppermute(block, "rows", [(i, i ^ step) for i in range(count)])
        step *= 2
    return block


def combine(weights, real, imag):
    return weights[:, 0:1] * real - weights[:, 1:2] * imag


def emit_messages(vectors, top, bottom, coupling, out_a, out_b):
    is_even = lax.rem(lax.axis_index("rows"), 2) == 0
    times = lambda block: jnp.dot(block, vectors, preferred_element_type=F32)
    both = lambda rows: jnp.concatenate([times(rows[0]), times(rows[1])], 1).astype(BF16)
    first, last = both(top), both(bottom)
    last = dot_tn(coupling, last.astype(F32)).astype(BF16)
    out_a[...] = jnp.where(is_even, last, first)
    out_b[...] = jnp.where(is_even, first, last)


def start_kernel(source, vectors_at, upper_at, *refs):
    out_a, out_b, coupling, vectors, ends, arrived = refs
    rows = vectors.shape[0]
    band = coupling.shape[0]
    half = rows // 2
    pairs = [(vectors_at.at[pl.ds(at, half)], vectors.at[pl.ds(at, half)]) for at in (0, half)]
    for end, at in ((0, 0), (1, rows - band)):
        pairs += [(source.at[0, c, pl.ds(at, band)], ends.at[end, c]) for c in range(2)]
    pairs.append((upper_at.at[pl.ds(rows - band, band)], coupling))
    copies = [pltpu.make_async_copy(*pair, arrived.at[i]) for i, pair in enumerate(pairs)]
    for copy in copies:
        copy.start()
    for copy in copies:
        copy.wait()
    emit_messages(vectors[...], ends.at[0], ends.at[1], coupling[...], out_a, out_b)


def from_hbm(kernel, outs, scratch, copies, *operands):
    far = lambda x: pltpu.with_memory_space_constraint(x, pltpu.HBM)
    kinds = [pltpu.HBM if is_far else pltpu.VMEM for _, is_far in operands]
    return pl.pallas_call(
        kernel,
        in_specs=[pl.BlockSpec(memory_space=kind) for kind in kinds],
        out_specs=[pl.BlockSpec(memory_space=pltpu.VMEM)] * len(outs),
        out_shape=outs,
        scratch_shapes=scratch + [pltpu.SemaphoreType.DMA((copies,))],
        cost_estimate=pl.CostEstimate(flops=10**8, bytes_accessed=10**6, transcendentals=0),
        compiler_params=pltpu.CompilerParams(vmem_limit_bytes=GRANT),
    )(*[far(x) if is_far else local(x) for x, is_far in operands])


def start(vectors, upper_tiles, inverse):
    rows, columns = vectors.shape
    band = upper_tiles.shape[1]
    message = like((band, 2 * columns), BF16)
    outs = [message, message, like((band, band)), like(vectors.shape, BF16)]
    scratch = [pltpu.VMEM((2, 2, band, rows), BF16)]
    operands = [(inverse, True), (vectors, True), (upper_tiles, True)]
    return from_hbm(start_kernel, outs, scratch, 7, *operands)


def tile_of(rows, band):
    return 2 * band if rows % (2 * band) == 0 else band


def edge_of(weights, got, coupling, rows, on_chip, factor=None):
    columns = got.shape[1] // 2
    band = coupling.shape[0]
    is_even = lax.rem(lax.axis_index("rows"), 2) == 0
    is_next = is_even if on_chip else jnp.logical_not(is_even)
    if factor is None:
        below = dot(coupling[...], got[...].astype(F32)).astype(BF16)
        edge = jnp.where(is_next, below, got[...]).astype(F32)
    else:
        turned = jnp.concatenate([got[:, :columns], got[:, columns:]], 0)
        turned = dot_three(turned, factor, NT)
        edge = jnp.concatenate([turned[:band], turned[band:]], 1)
        edge = jnp.where(is_next, dot_three(coupling[...], edge), edge)
    real, imag = edge[:, :columns], edge[:, columns:]
    at = pl.multiple_of(jnp.where(is_next, rows - band, 0), band)
    under = weights[:, 0:1] * imag + weights[:, 1:2] * real
    return at, jnp.concatenate([combine(weights, real, imag), -under], 0)


def edge_terms(edges, inverse, span, band):
    left = [inverse[0, c, span, pl.ds(at, band)] for at, _ in edges for c in range(2)]
    high, rest = halves_of(jnp.concatenate([edge for _, edge in edges], 0))
    left = jnp.concatenate(left, 1)
    times = lambda right: jnp.dot(left, right, preferred_element_type=F32)
    return times(high) + times(rest)


def products(weights, vectors, inverse, span):
    real = jnp.dot(inverse[0, 0, span], vectors[...], preferred_element_type=F32)
    imag = jnp.dot(inverse[0, 1, span], vectors[...], preferred_element_type=F32)
    return combine(weights, real, imag)


def start_base_kernel(weights_at, source, vectors, coupling, got, base, inverse, weights, arrived):
    rows = vectors.shape[0]
    tile = tile_of(rows, coupling.shape[0])
    spans = [pl.ds(at, tile) for at in range(0, rows, tile)]
    pairs = [(weights_at, weights)]
    pairs += [(source.at[:, :, span], inverse.at[:, :, span]) for span in spans]
    copies = [pltpu.make_async_copy(*pair, arrived.at[i]) for i, pair in enumerate(pairs)]
    for copy in copies:
        copy.start()
    copies[0].wait()
    band = coupling.shape[0]
    edges = [edge_of(weights, got, coupling, rows, True)]
    for copy, span in zip(copies[1:], spans):
        copy.wait()
        term = products(weights, vectors, inverse, span)
        base[span] = term + edge_terms(edges, inverse, span, band)


def start_base(weights, inverse, vectors, coupling, got):
    rows, columns = vectors.shape
    outs = [like((rows, columns)), like(inverse.shape, BF16), like(weights.shape)]
    operands = [(weights, True), (inverse, True), (vectors, False), (coupling, False), (got, False)]
    return from_hbm(start_base_kernel, outs, [], rows // coupling.shape[0] + 1, *operands)


def refined(field, low, factor):
    high, rest = halves_of(factor)
    times = lambda a, b: lax.dot_general(a, b, NT, preferred_element_type=F32)
    return times(field, high) + (times(field, rest) + times(low, high))


def tips_kernel(field, low, coupling, inverse, out_a, out_b):
    band = coupling.shape[0]
    is_even = lax.rem(lax.axis_index("rows"), 2) == 0

    def both(at):
        times = lambda part, x: jnp.dot(
            inverse[0, part, at : at + band], x, preferred_element_type=F32
        )
        of = lambda part: times(part, field[...]) + times(part, low[...])
        return jnp.concatenate([of(0), of(1)], 1)

    first = both(0)
    last = dot_tn(coupling[...], both(field.shape[0] - band))
    out_a[...] = jnp.where(is_even, last, first)
    out_b[...] = jnp.where(is_even, first, last)


def tips(field, low, coupling, inverse):
    message = like((coupling.shape[0], 2 * field.shape[1]))
    return whole(tips_kernel, [message, message], field, low, coupling, inverse)


def emit_term(term, own, sends):
    node = lax.axis_index("node")
    size = own.shape[0]
    steps = lax.axis_size("node")
    for s, out in enumerate((own,) + sends):
        where = pl.multiple_of((node ^ (s if s < steps else s - steps + 1)) * size, 8)
        value = term[pl.ds(where, size), :]
        if s >= steps:
            value = value - value.astype(BF16).astype(F32)
        out[...] = value.astype(out.dtype)


def solve_kernel(weights, field, low, factor, coupling, inverse, got_a, got_b, own, *refs):
    sends, (current, term) = refs[:-2], refs[-2:]
    current[...] = refined(field[...], low[...], factor[...]).astype(BF16)
    rows = field.shape[0]
    band = coupling.shape[0]
    tile = tile_of(rows, band)
    edges = [
        edge_of(weights, got, coupling, rows, on_chip, factor[...])
        for got, on_chip in ((got_a, True), (got_b, False))
    ]
    for at in range(0, rows, tile):
        span = pl.ds(at, tile)
        part = products(weights, current, inverse, span)
        term[span] = part + edge_terms(edges, inverse, span, band)
    emit_term(term, own, sends)


def blocks_of(rows, columns, parts):
    count = lax.axis_size("node")
    size = rows // count
    return [like((size, columns))] + [like((size, columns), BF16)] * (parts * (count - 1))


def solve(weights, field, low, factor, coupling, inverse, got_a, got_b, parts):
    rows, columns = field.shape
    return whole(
        solve_kernel,
        blocks_of(rows, columns, parts),
        weights,
        field,
        low,
        factor,
        coupling,
        inverse,
        got_a,
        got_b,
        scratch=[pltpu.VMEM((rows, columns), BF16), pltpu.VMEM((rows, columns), F32)],
    )


def correct_kernel(weights, base, got, coupling, inverse, own, *refs):
    sends, term = refs[:-1], refs[-1]
    rows = base.shape[0]
    band = coupling.shape[0]
    tile = tile_of(rows, band)
    edges = [edge_of(weights, got, coupling, rows, False)]
    for at in range(0, rows, tile):
        span = pl.ds(at, tile)
        term[span] = base[span] + edge_terms(edges, inverse, span, band)
    emit_term(term, own, sends)


def correct(weights, base, got, coupling, inverse, parts):
    rows, columns = base.shape
    outs = blocks_of(rows, columns, parts)
    scratch = [pltpu.VMEM((rows, columns), F32)]
    return whole(correct_kernel, outs, weights, base, got, coupling, inverse, scratch=scratch)


def place(blocks, out):
    node = lax.axis_index("node")
    size = blocks[0].shape[0]
    for step, block in enumerate(blocks):
        out[pl.ds(pl.multiple_of((node ^ step) * size, 8), size), :] = block[...]


def gram_kernel(*refs):
    *blocks, field, head, part, matrix = refs
    place(blocks, field)
    head[...] = field[: head.shape[0]]
    matrix[...] = lax.dot_general(field[...], field[...], TN, preferred_element_type=F32)
    size = part.shape[0]
    part[...] = matrix[pl.ds(pl.multiple_of(lax.axis_index("node") * size, 8), size), :]


def gram_slice(blocks, band):
    rows, columns = blocks[0].shape
    count = len(blocks)
    outs = [
        like((rows * count, columns), BF16),
        like((band, columns), BF16),
        like((columns // count, columns)),
    ]
    scratch = [pltpu.VMEM((columns, columns), F32)]
    return whole(gram_kernel, outs, *blocks, scratch=scratch)


def join_kernel(*refs):
    place(refs[:-1], refs[-1])


def join(blocks):
    rows, columns = blocks[0].shape
    return whole(join_kernel, like((rows * len(blocks), columns), BF16), *blocks)


def eliminate(block, out, base, spread):
    count = block.shape[0]
    full = (GROUP, count)
    lane = lax.broadcasted_iota(jnp.int32, full, 1)
    span = range(GROUP)
    tiles = [block[t * GROUP : (t + 1) * GROUP] for t in range(count // GROUP)]
    room = GROUP * (GROUP + 1)
    for t in range(len(tiles)):
        k = t * GROUP
        tile = tiles[t]
        slot = (t % 2) * room
        spread[slot : slot + GROUP] = tile
        for j in span:
            at = slot + GROUP * (j + 1)
            spread[at : at + GROUP] = jnp.broadcast_to(tile[:, k + j : k + j + 1], full)
        across = lambda row: spread[pl.ds(slot + row, GROUP, stride=0), :]
        rows = [across(i) for i in span]
        pivot = [[across(GROUP * (j + 1) + i) for j in range(i + 1)] for i in span]
        low = [[None] * GROUP for _ in span]
        inverse = [None] * GROUP
        pivots = [None] * GROUP
        for j in range(0, GROUP, 2):
            lead, side = pivot[j][j], pivot[j + 1][j]
            determinant = lead * pivot[j + 1][j + 1] - side * side
            inverse[j] = 1.0 / lead
            inverse[j + 1] = lead * (1.0 / determinant)
            pivots[j] = lead
            pivots[j + 1] = determinant * inverse[j]
            low[j + 1][j] = side * inverse[j]
            second = [None] * GROUP
            for i in range(j + 2, GROUP):
                low[i][j] = pivot[i][j] * inverse[j]
                second[i] = pivot[i][j + 1] - low[i][j] * side
                low[i][j + 1] = second[i] * inverse[j + 1]
            for i in range(j + 2, GROUP):
                for m in range(j + 2, i + 1):
                    pivot[i][m] = pivot[i][m] - low[i][j] * pivot[m][j] - low[i][j + 1] * second[m]
        inv = [[None] * GROUP for _ in span]
        for j in span:
            for i in range(j + 1, GROUP):
                total = low[i][j]
                for m in range(j + 1, i):
                    total = total + low[i][m] * inv[m][j]
                inv[i][j] = -total
        inside = (lane >= k) & (lane < k + GROUP)
        rows = [jnp.where(inside, jnp.where(lane == k + i, 1.0, 0.0), rows[i]) for i in span]
        done = []
        for i in span:
            total = rows[i]
            for j in range(i):
                total = total + inv[i][j] * rows[j]
            done.append(total)
            at = base + k + i
            row = jnp.where(lane < k + GROUP, total * lax.rsqrt(pivots[i]), 0.0)
            out[at : at + 1, base : base + count] = row[:1]
        if t + 1 < len(tiles):
            scaled = [done[i] * inverse[i] for i in span]
            back = []
            for j in span:
                total = scaled[j]
                for i in range(j + 1, GROUP):
                    total = total + inv[i][j] * scaled[i]
                back.append(total)
            for u in range(t + 1, len(tiles)):
                old = tiles[u]
                new = jnp.where(inside, 0.0, old)
                for j in span:
                    new = new - old[:, k + j : k + j + 1] * back[j]
                tiles[u] = new


def first_factor_kernel(order, *refs):
    *blocks, top, corner, rest, across, matrix, spread = refs
    place(blocks, matrix)
    count = matrix.shape[0]
    half = count // 2
    values = matrix[...] * (1.0 / order)
    eye = lax.broadcasted_iota(jnp.int32, (count, count), 0) == lax.broadcasted_iota(
        jnp.int32, (count, count), 1
    )
    diagonal = jnp.where(eye, values, 0.0)
    scale = lax.rsqrt(jnp.sum(diagonal, 0, keepdims=True))
    down = lax.rsqrt(jnp.sum(diagonal, 1, keepdims=True))
    across[...] = scale
    values = values * scale * down
    eliminate(values[:half, :half], top, 0, spread)
    beside = dot(top[...], values[:half, half:])
    corner[...] = dot_tn(beside, top[...])
    rest[...] = values[half:, half:] - dot_tn(beside, beside)


def second_factor_kernel(top, corner, rest, across, out, spread):
    half = top.shape[0]
    out[:half, :half] = top[...]
    out[:half, half:] = jnp.zeros((half, half), F32)
    eliminate(rest[...], out, half, spread)
    out[half:, :half] = -dot(out[half:, half:], corner[...])
    out[...] = out[...] * across[...]


def spread_room(columns):
    return pltpu.VMEM((2 * GROUP * (GROUP + 1), columns // 2), F32)


def first_factor(blocks, order):
    columns = blocks[0].shape[1]
    half = like((columns // 2, columns // 2))
    return whole(
        functools.partial(first_factor_kernel, order),
        [half, half, half, like((1, columns))],
        *blocks,
        scratch=[pltpu.VMEM((columns, columns), F32), spread_room(columns)],
        flops=6 * 10**9,
    )


def second_factor(halves):
    columns = halves[3].shape[1]
    return whole(
        second_factor_kernel,
        like((columns, columns)),
        *halves,
        scratch=[spread_room(columns)],
        flops=6 * 10**9,
    )


def next_head(head):
    count = lax.axis_size("rows")
    return lax.ppermute(head, "rows", [(i + 1, i) for i in range(count - 1)])


def band_kernel(field, low, after, diag_tiles, upper_tiles, part, image, matrix):
    band = after.shape[0]
    tiles = field.shape[0] // band

    def values(at):
        return field[at].astype(F32) + low[at].astype(F32)

    for t in range(tiles):
        at = slice(t * band, (t + 1) * band)
        following = slice((t + 1) * band, (t + 2) * band)
        following = after[...].astype(F32) if t == tiles - 1 else values(following)
        image[at] = 0.5 * dot_three(diag_tiles[at], values(at)) + dot_three(upper_tiles[at], following)
    matrix[...] = dot_two(field[...], image[...], TN)
    matrix[...] += lax.dot_general(
        low[...], image[...].astype(BF16), TN, preferred_element_type=F32
    )
    size = part.shape[0]
    part[...] = matrix[pl.ds(pl.multiple_of(lax.axis_index("node") * size, 8), size), :]


def band_slice(field, low, after, diag_tiles, upper_tiles):
    rows, columns = field.shape
    return whole(
        band_kernel,
        like((columns // lax.axis_size("node"), columns)),
        field,
        low,
        after,
        diag_tiles,
        upper_tiles,
        scratch=[pltpu.VMEM((rows, columns), F32), pltpu.VMEM((columns, columns), F32)],
    )


def finish_kernel(order, field, low, *refs):
    blocks, factors = refs[: -6 - ITERS], refs[-6 - ITERS : -6]
    vectors_at, projected_at, vectors, projected, matrix, sent = refs[-6:]
    rows = field.shape[0]
    tile = rows // 3 if rows % 48 == 0 else rows
    copies = []

    def send(source, target):
        copies.append(pltpu.make_async_copy(source, target, sent.at[len(copies)]))
        copies[-1].start()

    for at in range(0, rows, tile):
        span = pl.ds(at, tile)
        vectors[span] = refined(field[span], low[span], factors[-1][...])
        send(vectors.at[span], vectors_at.at[span])
    node = lax.axis_index("node")
    size = blocks[0].shape[0] // ITERS
    for k, factor in enumerate(factors):
        for step, block in enumerate(blocks):
            at = pl.multiple_of((node ^ step) * size, 8)
            matrix[pl.ds(at, size), :] = block[k * size : (k + 1) * size]
        value = dot_three(dot_three(factor[...], matrix[...]), factor[...], NT)
        projected[k] = (value + value.T) * (1.0 / order)
        send(projected.at[k], projected_at.at[k])
    for copy in copies:
        copy.wait()


def finish(field, low, blocks, factors, order):
    rows, columns = field.shape
    operands = [field, low, *blocks, *factors]
    vmem = pl.BlockSpec(memory_space=pltpu.VMEM)
    shapes = [(rows, columns), (ITERS, columns, columns)]
    return pl.pallas_call(
        functools.partial(finish_kernel, order),
        in_specs=[vmem for _ in operands],
        out_specs=[pl.BlockSpec(memory_space=pltpu.HBM)] * 2,
        out_shape=[jax.ShapeDtypeStruct(x, F32) for x in shapes],
        scratch_shapes=[pltpu.VMEM(x, F32) for x in shapes]
        + [pltpu.VMEM((columns, columns), F32), pltpu.SemaphoreType.DMA((3 + ITERS,))],
        cost_estimate=pl.CostEstimate(flops=10**9, bytes_accessed=10**6, transcendentals=0),
        compiler_params=pltpu.CompilerParams(vmem_limit_bytes=GRANT),
        name="finish",
    )(*[local(x) for x in operands])


def after(value, *others):
    return lax.optimization_barrier((value,) + others)[0]


def per_device(subspace, inverse, weights, diag_tiles, upper_tiles):
    order = float(subspace.shape[0] * lax.axis_size("rows"))
    band = upper_tiles.shape[1]
    partners = lax.axis_size("node") - 1
    factors, pairs = [], []
    for iteration in range(ITERS):
        final = iteration == ITERS - 1
        parts = 1 if final else 2
        if iteration == 0:
            out_a, out_b, coupling, vectors = start(subspace, upper_tiles, inverse)
            got_b = link_swap(out_b)
            got_a = core_swap(out_a)
            base, inverse, weights = start_base(weights, inverse, vectors, coupling, got_a)
            own, *terms = correct(weights, base, got_b, coupling, inverse, parts)
        else:
            own, *terms = solve(
                weights, field, low, factor, coupling, inverse, got_a, got_b, parts
            )
        got = node_spread(terms[:partners])
        if not final:
            low_got = node_spread(terms[partners:])
        total = tree_sum([own] + [x.astype(F32) for x in got])
        piece = total.astype(BF16)
        blocks = [piece] + node_spread([piece] * partners)
        total, sent = lax.optimization_barrier((total, piece))
        if not final:
            total = total + tree_sum([x.astype(F32) for x in low_got])
        low_piece = (total - sent.astype(F32)).astype(BF16)
        low = join([low_piece] + node_spread([low_piece] * partners))
        field, head, part = gram_slice(blocks, band)
        part = part + core_swap(part)
        following = next_head(after(head, part))
        total = chip_sum(part)
        gathered = [total] + node_spread([total] * partners)
        pair = band_slice(field, low, after(following, total), diag_tiles, upper_tiles)
        if not final:
            out_a, out_b = tips(field, low, coupling, inverse)
            got_b = link_swap(out_b)
            got_a = core_swap(out_a)
        halves = first_factor(gathered, order)
        pair = pair + core_swap(pair)
        pairs.append(chip_sum(after(pair, *gathered)))
        if final:
            pair = after(jnp.concatenate(pairs, 0), *halves)
            spread = [pair] + node_spread([pair] * partners)
        factor = second_factor(halves)
        factors.append(factor)
    orthonormal, projected = finish(field, low, spread, factors, order)
    return orthonormal, projected


def solution(mesh):
    placed = (
        P("rows", None),
        P("node", None, "rows", None),
        P("node", None),
        P("rows", None),
        P("rows", None),
    )
    return jax.shard_map(
        per_device, mesh=mesh, in_specs=placed, out_specs=(P("rows", None), P()), check_vma=False
    )
```

```python
import functools

import jax
import jax.numpy as jnp
from jax import lax
from jax.experimental import pallas as pl
from jax.experimental.pallas import tpu as pltpu
from jax.sharding import PartitionSpec as P


ITERS = 2
GROUP = 8
GRANT = 16 * 2**20

precise = lax.Precision.HIGHEST
F32 = jnp.float32
BF16 = jnp.bfloat16


def dot(left, right):
    return jnp.dot(left, right, precision=precise, preferred_element_type=F32)


def dot_tn(left, right):
    dims = (((0,), (0,)), ((), ()))
    return lax.dot_general(left, right, dims, precision=precise, preferred_element_type=F32)


def halves_of(value):
    high = value.astype(BF16)
    return high, (value - high.astype(F32)).astype(BF16)


def dot_three(left, right, dims=(((1,), (0,)), ((), ()))):
    times = lambda a, b: lax.dot_general(a, b, dims, preferred_element_type=F32)
    (a, b), (c, d) = halves_of(left), halves_of(right)
    return times(a, c) + (times(a, d) + times(b, c))


def dot_two(left, right, dims=(((1,), (0,)), ((), ()))):
    times = lambda a, b: lax.dot_general(a, b, dims, preferred_element_type=F32)
    c, d = halves_of(right)
    return times(left, c) + times(left, d)


NT = (((1,), (1,)), ((), ()))
TN = (((0,), (0,)), ((), ()))


def like(shape, dtype=F32):
    return pltpu.VMEM(shape, dtype)


def halves_of(value):
    high = value.astype(BF16)
    return high, (value - high.astype(F32)).astype(BF16)


def dot_three(left, right, dims=(((1,), (0,)), ((), ()))):
    times = lambda a, b: lax.dot_general(a, b, dims, preferred_element_type=F32)
    (a, b), (c, d) = halves_of(left), halves_of(right)
    return times(a, c) + (times(a, d) + times(b, c))


def dot_two(left, right, dims=(((1,), (0,)), ((), ()))):
    times = lambda a, b: lax.dot_general(a, b, dims, preferred_element_type=F32)
    c, d = halves_of(right)
    return times(left, c) + times(left, d)


NT = (((1,), (1,)), ((), ()))
TN = (((0,), (0,)), ((), ()))


def local(value):
    return pltpu.with_memory_space_constraint(value, pltpu.VMEM)


def whole(kernel, out_shape, *operands, scratch=(), flops=10**8):
    size = sum(x.size * x.dtype.itemsize for x in operands)
    vmem = pl.BlockSpec(memory_space=pltpu.VMEM)
    return pl.pallas_call(
        kernel,
        out_shape=out_shape,
        in_specs=[vmem for _ in operands],
        out_specs=jax.tree.map(lambda _: vmem, out_shape),
        scratch_shapes=list(scratch),
        cost_estimate=pl.CostEstimate(flops=flops, bytes_accessed=size, transcendentals=0),
        compiler_params=pltpu.CompilerParams(vmem_limit_bytes=GRANT),
    )(*[local(x) for x in operands])


def node_swap(block, step):
    count = lax.axis_size("node")
    return lax.ppermute(block, "node", [(i, i ^ step) for i in range(count)])


def core_swap(block):
    count = lax.axis_size("rows")
    return lax.ppermute(block, "rows", [(i, i ^ 1) for i in range(count)])


def link_swap(block):
    count = lax.axis_size("rows")
    pairs = [(i, i + 1) for i in range(1, count - 1, 2)]
    return lax.ppermute(block, "rows", pairs + [(b, a) for a, b in pairs])


def node_spread(blocks):
    return [node_swap(block, step + 1) for step, block in enumerate(blocks)]


def tree_sum(blocks):
    while len(blocks) > 1:
        odd = blocks[len(blocks) // 2 * 2 :]
        blocks = [a + b for a, b in zip(blocks[::2], blocks[1::2])] + odd
    return blocks[0]


def chip_sum(block):
    count = lax.axis_size("rows")
    chips = count // 2
    if chips <= 4:
        steps = range(1, chips)
        routes = [[(i, i ^ (2 * s)) for i in range(count)] for s in steps]
        return tree_sum([block] + [lax.ppermute(block, "rows", route) for route in routes])
    step = 2
    while step < count:
        block = block + lax.ppermute(block, "rows", [(i, i ^ step) for i in range(count)])
        step *= 2
    return block


def combine(weights, real, imag):
    return weights[:, 0:1] * real - weights[:, 1:2] * imag


def end_products(vectors, block):
    times = lambda part: jnp.dot(block[part], vectors, preferred_element_type=F32)
    return jnp.concatenate([times(0), times(1)], 1).astype(BF16)


def emit_messages(first, last, coupling, out_a, out_b):
    is_even = lax.rem(lax.axis_index("rows"), 2) == 0
    last = dot_tn(coupling, last.astype(F32)).astype(BF16)
    out_a[...] = jnp.where(is_even, last, first)
    out_b[...] = jnp.where(is_even, first, last)


def start_kernel(source, vectors_at, upper_at, *refs):
    out_a, out_b, coupling, vectors, ends, arrived = refs
    rows = vectors.shape[0]
    band = coupling.shape[0]
    half = rows // 2
    pairs = [(vectors_at.at[pl.ds(at, half)], vectors.at[pl.ds(at, half)]) for at in (0, half)]
    for end, at in ((0, 0), (1, rows - band)):
        pairs += [(source.at[0, c, pl.ds(at, band)], ends.at[end, c]) for c in range(2)]
    pairs.append((upper_at.at[pl.ds(rows - band, band)], coupling))
    copies = [pltpu.make_async_copy(*pair, arrived.at[i]) for i, pair in enumerate(pairs)]
    for copy in copies:
        copy.start()
    for copy in copies[:4]:
        copy.wait()
    first = end_products(vectors[...], ends.at[0])
    for copy in copies[4:]:
        copy.wait()
    last = end_products(vectors[...], ends.at[1])
    emit_messages(first, last, coupling[...], out_a, out_b)


def from_hbm(kernel, outs, scratch, copies, *operands):
    far = lambda x: pltpu.with_memory_space_constraint(x, pltpu.HBM)
    kinds = [pltpu.HBM if is_far else pltpu.VMEM for _, is_far in operands]
    return pl.pallas_call(
        kernel,
        in_specs=[pl.BlockSpec(memory_space=kind) for kind in kinds],
        out_specs=[pl.BlockSpec(memory_space=pltpu.VMEM)] * len(outs),
        out_shape=outs,
        scratch_shapes=scratch + [pltpu.SemaphoreType.DMA((copies,))],
        cost_estimate=pl.CostEstimate(flops=10**8, bytes_accessed=10**6, transcendentals=0),
        compiler_params=pltpu.CompilerParams(vmem_limit_bytes=GRANT),
    )(*[far(x) if is_far else local(x) for x, is_far in operands])


def start(vectors, upper_tiles, inverse):
    rows, columns = vectors.shape
    band = upper_tiles.shape[1]
    message = like((band, 2 * columns), BF16)
    outs = [message, message, like((band, band)), like(vectors.shape, BF16)]
    scratch = [pltpu.VMEM((2, 2, band, rows), BF16)]
    operands = [(inverse, True), (vectors, True), (upper_tiles, True)]
    return from_hbm(start_kernel, outs, scratch, 7, *operands)


def tile_of(rows, band):
    return 2 * band if rows % (2 * band) == 0 else band


def edge_of(weights, got, coupling, rows, on_chip, factor=None):
    columns = got.shape[1] // 2
    band = coupling.shape[0]
    is_even = lax.rem(lax.axis_index("rows"), 2) == 0
    is_next = is_even if on_chip else jnp.logical_not(is_even)
    if factor is None:
        below = dot(coupling[...], got[...].astype(F32)).astype(BF16)
        edge = jnp.where(is_next, below, got[...]).astype(F32)
    else:
        turned = jnp.concatenate([got[:, :columns], got[:, columns:]], 0)
        turned = dot_three(turned, factor, NT)
        edge = jnp.concatenate([turned[:band], turned[band:]], 1)
        edge = jnp.where(is_next, dot_three(coupling[...], edge), edge)
    real, imag = edge[:, :columns], edge[:, columns:]
    at = pl.multiple_of(jnp.where(is_next, rows - band, 0), band)
    under = weights[:, 0:1] * imag + weights[:, 1:2] * real
    return at, jnp.concatenate([combine(weights, real, imag), -under], 0)


def edge_terms(edges, inverse, span, band):
    left = [inverse[0, c, span, pl.ds(at, band)] for at, _ in edges for c in range(2)]
    high, rest = halves_of(jnp.concatenate([edge for _, edge in edges], 0))
    left = jnp.concatenate(left, 1)
    times = lambda right: jnp.dot(left, right, preferred_element_type=F32)
    return times(high) + times(rest)


def products(weights, vectors, inverse, span):
    real = jnp.dot(inverse[0, 0, span], vectors[...], preferred_element_type=F32)
    imag = jnp.dot(inverse[0, 1, span], vectors[...], preferred_element_type=F32)
    return combine(weights, real, imag)


def start_base_kernel(weights_at, source, vectors, coupling, got, base, inverse, weights, arrived):
    rows = vectors.shape[0]
    tile = tile_of(rows, coupling.shape[0])
    spans = [pl.ds(at, tile) for at in range(0, rows, tile)]
    pairs = [(weights_at, weights)]
    pairs += [(source.at[:, :, span], inverse.at[:, :, span]) for span in spans]
    copies = [pltpu.make_async_copy(*pair, arrived.at[i]) for i, pair in enumerate(pairs)]
    for copy in copies:
        copy.start()
    copies[0].wait()
    band = coupling.shape[0]
    edges = [edge_of(weights, got, coupling, rows, True)]
    for copy, span in zip(copies[1:], spans):
        copy.wait()
        term = products(weights, vectors, inverse, span)
        base[span] = term + edge_terms(edges, inverse, span, band)


def start_base(weights, inverse, vectors, coupling, got):
    rows, columns = vectors.shape
    outs = [like((rows, columns)), like(inverse.shape, BF16), like(weights.shape)]
    operands = [(weights, True), (inverse, True), (vectors, False), (coupling, False), (got, False)]
    return from_hbm(start_base_kernel, outs, [], rows // coupling.shape[0] + 1, *operands)


def refined(field, low, factor):
    high, rest = halves_of(factor)
    times = lambda a, b: lax.dot_general(a, b, NT, preferred_element_type=F32)
    return times(field, high) + (times(field, rest) + times(low, high))


def tips_kernel(field, low, coupling, inverse, out_a, out_b):
    band = coupling.shape[0]
    is_even = lax.rem(lax.axis_index("rows"), 2) == 0

    def both(at):
        times = lambda part, x: jnp.dot(
            inverse[0, part, at : at + band], x, preferred_element_type=F32
        )
        of = lambda part: times(part, field[...]) + times(part, low[...])
        return jnp.concatenate([of(0), of(1)], 1)

    first = both(0)
    last = dot_tn(coupling[...], both(field.shape[0] - band))
    out_a[...] = jnp.where(is_even, last, first)
    out_b[...] = jnp.where(is_even, first, last)


def tips(field, low, coupling, inverse):
    message = like((coupling.shape[0], 2 * field.shape[1]))
    return whole(tips_kernel, [message, message], field, low, coupling, inverse)


def emit_term(term, own, sends):
    node = lax.axis_index("node")
    size = own.shape[0]
    steps = lax.axis_size("node")
    for s, out in enumerate((own,) + sends):
        where = pl.multiple_of((node ^ (s if s < steps else s - steps + 1)) * size, 8)
        value = term[pl.ds(where, size), :]
        if s >= steps:
            value = value - value.astype(BF16).astype(F32)
        out[...] = value.astype(out.dtype)


def solve_kernel(weights, field, low, factor, coupling, inverse, got_a, got_b, own, *refs):
    sends, (current, term) = refs[:-2], refs[-2:]
    current[...] = refined(field[...], low[...], factor[...]).astype(BF16)
    rows = field.shape[0]
    band = coupling.shape[0]
    tile = tile_of(rows, band)
    edges = [
        edge_of(weights, got, coupling, rows, on_chip, factor[...])
        for got, on_chip in ((got_a, True), (got_b, False))
    ]
    for at in range(0, rows, tile):
        span = pl.ds(at, tile)
        part = products(weights, current, inverse, span)
        term[span] = part + edge_terms(edges, inverse, span, band)
    emit_term(term, own, sends)


def blocks_of(rows, columns, parts):
    count = lax.axis_size("node")
    size = rows // count
    return [like((size, columns))] + [like((size, columns), BF16)] * (parts * (count - 1))


def solve(weights, field, low, factor, coupling, inverse, got_a, got_b, parts):
    rows, columns = field.shape
    return whole(
        solve_kernel,
        blocks_of(rows, columns, parts),
        weights,
        field,
        low,
        factor,
        coupling,
        inverse,
        got_a,
        got_b,
        scratch=[pltpu.VMEM((rows, columns), BF16), pltpu.VMEM((rows, columns), F32)],
    )


def correct_kernel(weights, base, got, coupling, inverse, own, *refs):
    sends, term = refs[:-1], refs[-1]
    rows = base.shape[0]
    band = coupling.shape[0]
    tile = tile_of(rows, band)
    edges = [edge_of(weights, got, coupling, rows, False)]
    for at in range(0, rows, tile):
        span = pl.ds(at, tile)
        term[span] = base[span] + edge_terms(edges, inverse, span, band)
    emit_term(term, own, sends)


def correct(weights, base, got, coupling, inverse, parts):
    rows, columns = base.shape
    outs = blocks_of(rows, columns, parts)
    scratch = [pltpu.VMEM((rows, columns), F32)]
    return whole(correct_kernel, outs, weights, base, got, coupling, inverse, scratch=scratch)


def place(blocks, out):
    node = lax.axis_index("node")
    size = blocks[0].shape[0]
    for step, block in enumerate(blocks):
        out[pl.ds(pl.multiple_of((node ^ step) * size, 8), size), :] = block[...]


def gram_kernel(*refs):
    *blocks, field, head, part, matrix = refs
    place(blocks, field)
    head[...] = field[: head.shape[0]]
    matrix[...] = lax.dot_general(field[...], field[...], TN, preferred_element_type=F32)
    size = part.shape[0]
    part[...] = matrix[pl.ds(pl.multiple_of(lax.axis_index("node") * size, 8), size), :]


def gram_slice(blocks, band):
    rows, columns = blocks[0].shape
    count = len(blocks)
    outs = [
        like((rows * count, columns), BF16),
        like((band, columns), BF16),
        like((columns // count, columns)),
    ]
    scratch = [pltpu.VMEM((columns, columns), F32)]
    return whole(gram_kernel, outs, *blocks, scratch=scratch)


def join_kernel(*refs):
    place(refs[:-1], refs[-1])


def join(blocks):
    rows, columns = blocks[0].shape
    return whole(join_kernel, like((rows * len(blocks), columns), BF16), *blocks)


def eliminate(block, out, base, spread):
    count = block.shape[0]
    full = (GROUP, count)
    lane = lax.broadcasted_iota(jnp.int32, full, 1)
    span = range(GROUP)
    tiles = [block[t * GROUP : (t + 1) * GROUP] for t in range(count // GROUP)]
    room = GROUP * (GROUP + 1)
    for t in range(len(tiles)):
        k = t * GROUP
        tile = tiles[t]
        slot = (t % 2) * room
        spread[slot : slot + GROUP] = tile
        for j in span:
            at = slot + GROUP * (j + 1)
            spread[at : at + GROUP] = jnp.broadcast_to(tile[:, k + j : k + j + 1], full)
        across = lambda row: spread[pl.ds(slot + row, GROUP, stride=0), :]
        rows = [across(i) for i in span]
        pivot = [[across(GROUP * (j + 1) + i) for j in range(i + 1)] for i in span]
        low = [[None] * GROUP for _ in span]
        inverse = [None] * GROUP
        pivots = [None] * GROUP
        for j in range(0, GROUP, 2):
            lead, side = pivot[j][j], pivot[j + 1][j]
            determinant = lead * pivot[j + 1][j + 1] - side * side
            inverse[j] = 1.0 / lead
            inverse[j + 1] = lead * (1.0 / determinant)
            pivots[j] = lead
            pivots[j + 1] = determinant * inverse[j]
            low[j + 1][j] = side * inverse[j]
            second = [None] * GROUP
            for i in range(j + 2, GROUP):
                low[i][j] = pivot[i][j] * inverse[j]
                second[i] = pivot[i][j + 1] - low[i][j] * side
                low[i][j + 1] = second[i] * inverse[j + 1]
            for i in range(j + 2, GROUP):
                for m in range(j + 2, i + 1):
                    pivot[i][m] = pivot[i][m] - low[i][j] * pivot[m][j] - low[i][j + 1] * second[m]
        inv = [[None] * GROUP for _ in span]
        for j in span:
            for i in range(j + 1, GROUP):
                total = low[i][j]
                for m in range(j + 1, i):
                    total = total + low[i][m] * inv[m][j]
                inv[i][j] = -total
        inside = (lane >= k) & (lane < k + GROUP)
        rows = [jnp.where(inside, jnp.where(lane == k + i, 1.0, 0.0), rows[i]) for i in span]
        done = []
        for i in span:
            total = rows[i]
            for j in range(i):
                total = total + inv[i][j] * rows[j]
            done.append(total)
            at = base + k + i
            row = jnp.where(lane < k + GROUP, total * lax.rsqrt(pivots[i]), 0.0)
            out[at : at + 1, base : base + count] = row[:1]
        if t + 1 < len(tiles):
            scaled = [done[i] * inverse[i] for i in span]
            back = []
            for j in span:
                total = scaled[j]
                for i in range(j + 1, GROUP):
                    total = total + inv[i][j] * scaled[i]
                back.append(total)
            for u in range(t + 1, len(tiles)):
                old = tiles[u]
                new = jnp.where(inside, 0.0, old)
                for j in span:
                    new = new - old[:, k + j : k + j + 1] * back[j]
                tiles[u] = new


def first_factor_kernel(order, *refs):
    *blocks, top, corner, rest, across, matrix, spread = refs
    place(blocks, matrix)
    count = matrix.shape[0]
    half = count // 2
    values = matrix[...] * (1.0 / order)
    eye = lax.broadcasted_iota(jnp.int32, (count, count), 0) == lax.broadcasted_iota(
        jnp.int32, (count, count), 1
    )
    diagonal = jnp.where(eye, values, 0.0)
    scale = lax.rsqrt(jnp.sum(diagonal, 0, keepdims=True))
    down = lax.rsqrt(jnp.sum(diagonal, 1, keepdims=True))
    across[...] = scale
    values = values * scale * down
    eliminate(values[:half, :half], top, 0, spread)
    beside = dot(top[...], values[:half, half:])
    corner[...] = dot_tn(beside, top[...])
    rest[...] = values[half:, half:] - dot_tn(beside, beside)


def second_factor_kernel(top, corner, rest, across, out, spread):
    half = top.shape[0]
    out[:half, :half] = top[...]
    out[:half, half:] = jnp.zeros((half, half), F32)
    eliminate(rest[...], out, half, spread)
    out[half:, :half] = -dot(out[half:, half:], corner[...])
    out[...] = out[...] * across[...]


def spread_room(columns):
    return pltpu.VMEM((2 * GROUP * (GROUP + 1) + GROUP, columns // 2), F32)


def first_factor(blocks, order):
    columns = blocks[0].shape[1]
    half = like((columns // 2, columns // 2))
    return whole(
        functools.partial(first_factor_kernel, order),
        [half, half, half, like((1, columns))],
        *blocks,
        scratch=[pltpu.VMEM((columns, columns), F32), spread_room(columns)],
        flops=6 * 10**9,
    )


def second_factor(halves):
    columns = halves[3].shape[1]
    return whole(
        second_factor_kernel,
        like((columns, columns)),
        *halves,
        scratch=[spread_room(columns)],
        flops=6 * 10**9,
    )


def next_head(head):
    count = lax.axis_size("rows")
    return lax.ppermute(head, "rows", [(i + 1, i) for i in range(count - 1)])


def band_kernel(field, low, after, diag_tiles, upper_tiles, part, image, matrix):
    band = after.shape[0]
    tiles = field.shape[0] // band

    def values(at):
        return field[at].astype(F32) + low[at].astype(F32)

    for t in range(tiles):
        at = slice(t * band, (t + 1) * band)
        following = slice((t + 1) * band, (t + 2) * band)
        following = after[...].astype(F32) if t == tiles - 1 else values(following)
        image[at] = 0.5 * dot_three(diag_tiles[at], values(at)) + dot_three(upper_tiles[at], following)
    matrix[...] = dot_two(field[...], image[...], TN)
    matrix[...] += lax.dot_general(
        low[...], image[...].astype(BF16), TN, preferred_element_type=F32
    )
    size = part.shape[0]
    part[...] = matrix[pl.ds(pl.multiple_of(lax.axis_index("node") * size, 8), size), :]


def band_slice(field, low, after, diag_tiles, upper_tiles):
    rows, columns = field.shape
    return whole(
        band_kernel,
        like((columns // lax.axis_size("node"), columns)),
        field,
        low,
        after,
        diag_tiles,
        upper_tiles,
        scratch=[pltpu.VMEM((rows, columns), F32), pltpu.VMEM((columns, columns), F32)],
    )


def finish_kernel(order, field, low, *refs):
    blocks, factors = refs[: -6 - ITERS], refs[-6 - ITERS : -6]
    vectors_at, projected_at, vectors, projected, matrix, sent = refs[-6:]
    rows = field.shape[0]
    tile = rows // 3 if rows % 48 == 0 else rows
    copies = []

    def send(source, target):
        copies.append(pltpu.make_async_copy(source, target, sent.at[len(copies)]))
        copies[-1].start()

    for at in range(0, rows, tile):
        span = pl.ds(at, tile)
        vectors[span] = refined(field[span], low[span], factors[-1][...])
        send(vectors.at[span], vectors_at.at[span])
    node = lax.axis_index("node")
    size = blocks[0].shape[0] // ITERS
    for k, factor in enumerate(factors):
        for step, block in enumerate(blocks):
            at = pl.multiple_of((node ^ step) * size, 8)
            matrix[pl.ds(at, size), :] = block[k * size : (k + 1) * size]
        value = dot_three(dot_three(factor[...], matrix[...]), factor[...], NT)
        projected[k] = (value + value.T) * (1.0 / order)
        send(projected.at[k], projected_at.at[k])
    for copy in copies:
        copy.wait()


def finish(field, low, blocks, factors, order):
    rows, columns = field.shape
    operands = [field, low, *blocks, *factors]
    vmem = pl.BlockSpec(memory_space=pltpu.VMEM)
    shapes = [(rows, columns), (ITERS, columns, columns)]
    return pl.pallas_call(
        functools.partial(finish_kernel, order),
        in_specs=[vmem for _ in operands],
        out_specs=[pl.BlockSpec(memory_space=pltpu.HBM)] * 2,
        out_shape=[jax.ShapeDtypeStruct(x, F32) for x in shapes],
        scratch_shapes=[pltpu.VMEM(x, F32) for x in shapes]
        + [pltpu.VMEM((columns, columns), F32), pltpu.SemaphoreType.DMA((3 + ITERS,))],
        cost_estimate=pl.CostEstimate(flops=10**9, bytes_accessed=10**6, transcendentals=0),
        compiler_params=pltpu.CompilerParams(vmem_limit_bytes=GRANT),
        name="finish",
    )(*[local(x) for x in operands])


def after(value, *others):
    return lax.optimization_barrier((value,) + others)[0]


def per_device(subspace, inverse, weights, diag_tiles, upper_tiles):
    order = float(subspace.shape[0] * lax.axis_size("rows"))
    band = upper_tiles.shape[1]
    partners = lax.axis_size("node") - 1
    factors, pairs = [], []
    for iteration in range(ITERS):
        final = iteration == ITERS - 1
        parts = 1 if final else 2
        if iteration == 0:
            out_a, out_b, coupling, vectors = start(subspace, upper_tiles, inverse)
            got_b = link_swap(out_b)
            got_a = core_swap(out_a)
            base, inverse, weights = start_base(weights, inverse, vectors, coupling, got_a)
            own, *terms = correct(weights, base, got_b, coupling, inverse, parts)
        else:
            own, *terms = solve(
                weights, field, low, factor, coupling, inverse, got_a, got_b, parts
            )
        got = node_spread(terms[:partners])
        if not final:
            low_got = node_spread(terms[partners:])
        total = tree_sum([own] + [x.astype(F32) for x in got])
        piece = total.astype(BF16)
        blocks = [piece] + node_spread([piece] * partners)
        total, sent = lax.optimization_barrier((total, piece))
        if not final:
            total = total + tree_sum([x.astype(F32) for x in low_got])
        low_piece = (total - sent.astype(F32)).astype(BF16)
        low = join([low_piece] + node_spread([low_piece] * partners))
        field, head, part = gram_slice(blocks, band)
        part = part + core_swap(part)
        following = next_head(after(head, part))
        total = chip_sum(part)
        gathered = [total] + node_spread([total] * partners)
        pair = band_slice(field, low, after(following, total), diag_tiles, upper_tiles)
        if not final:
            out_a, out_b = tips(field, low, coupling, inverse)
            got_b = link_swap(out_b)
            got_a = core_swap(out_a)
        halves = first_factor(gathered, order)
        pair = pair + core_swap(pair)
        pairs.append(chip_sum(after(pair, *gathered)))
        if final:
            pair = after(jnp.concatenate(pairs, 0), *halves)
            spread = [pair] + node_spread([pair] * partners)
        factor = second_factor(halves)
        factors.append(factor)
    orthonormal, projected = finish(field, low, spread, factors, order)
    return orthonormal, projected


def solution(mesh):
    placed = (
        P("rows", None),
        P("node", None, "rows", None),
        P("node", None),
        P("rows", None),
        P("rows", None),
    )
    return jax.shard_map(
        per_device, mesh=mesh, in_specs=placed, out_specs=(P("rows", None), P()), check_vma=False
    )
```

```python
import functools

import jax
import jax.numpy as jnp
from jax import lax
from jax.experimental import pallas as pl
from jax.experimental.pallas import tpu as pltpu
from jax.sharding import PartitionSpec as P


ITERS = 2
GROUP = 8
GRANT = 16 * 2**20

precise = lax.Precision.HIGHEST
F32 = jnp.float32
BF16 = jnp.bfloat16


def dot(left, right):
    return jnp.dot(left, right, precision=precise, preferred_element_type=F32)


def dot_tn(left, right):
    dims = (((0,), (0,)), ((), ()))
    return lax.dot_general(left, right, dims, precision=precise, preferred_element_type=F32)


def halves_of(value):
    high = value.astype(BF16)
    return high, (value - high.astype(F32)).astype(BF16)


def dot_three(left, right, dims=(((1,), (0,)), ((), ()))):
    times = lambda a, b: lax.dot_general(a, b, dims, preferred_element_type=F32)
    (a, b), (c, d) = halves_of(left), halves_of(right)
    return times(a, c) + (times(a, d) + times(b, c))


def dot_two(left, right, dims=(((1,), (0,)), ((), ()))):
    times = lambda a, b: lax.dot_general(a, b, dims, preferred_element_type=F32)
    c, d = halves_of(right)
    return times(left, c) + times(left, d)


NT = (((1,), (1,)), ((), ()))
TN = (((0,), (0,)), ((), ()))


def like(shape, dtype=F32):
    return pltpu.VMEM(shape, dtype)


def halves_of(value):
    high = value.astype(BF16)
    return high, (value - high.astype(F32)).astype(BF16)


def dot_three(left, right, dims=(((1,), (0,)), ((), ()))):
    times = lambda a, b: lax.dot_general(a, b, dims, preferred_element_type=F32)
    (a, b), (c, d) = halves_of(left), halves_of(right)
    return times(a, c) + (times(a, d) + times(b, c))


def dot_two(left, right, dims=(((1,), (0,)), ((), ()))):
    times = lambda a, b: lax.dot_general(a, b, dims, preferred_element_type=F32)
    c, d = halves_of(right)
    return times(left, c) + times(left, d)


NT = (((1,), (1,)), ((), ()))
TN = (((0,), (0,)), ((), ()))


def local(value):
    return pltpu.with_memory_space_constraint(value, pltpu.VMEM)


def whole(kernel, out_shape, *operands, scratch=(), flops=10**8):
    size = sum(x.size * x.dtype.itemsize for x in operands)
    vmem = pl.BlockSpec(memory_space=pltpu.VMEM)
    return pl.pallas_call(
        kernel,
        out_shape=out_shape,
        in_specs=[vmem for _ in operands],
        out_specs=jax.tree.map(lambda _: vmem, out_shape),
        scratch_shapes=list(scratch),
        cost_estimate=pl.CostEstimate(flops=flops, bytes_accessed=size, transcendentals=0),
        compiler_params=pltpu.CompilerParams(vmem_limit_bytes=GRANT),
    )(*[local(x) for x in operands])


def node_swap(block, step):
    count = lax.axis_size("node")
    return lax.ppermute(block, "node", [(i, i ^ step) for i in range(count)])


def core_swap(block):
    count = lax.axis_size("rows")
    return lax.ppermute(block, "rows", [(i, i ^ 1) for i in range(count)])


def link_swap(block):
    count = lax.axis_size("rows")
    pairs = [(i, i + 1) for i in range(1, count - 1, 2)]
    return lax.ppermute(block, "rows", pairs + [(b, a) for a, b in pairs])


def node_spread(blocks):
    return [node_swap(block, step + 1) for step, block in enumerate(blocks)]


def tree_sum(blocks):
    while len(blocks) > 1:
        odd = blocks[len(blocks) // 2 * 2 :]
        blocks = [a + b for a, b in zip(blocks[::2], blocks[1::2])] + odd
    return blocks[0]


def chip_sum(block):
    count = lax.axis_size("rows")
    chips = count // 2
    if chips <= 4:
        steps = range(1, chips)
        routes = [[(i, i ^ (2 * s)) for i in range(count)] for s in steps]
        return tree_sum([block] + [lax.ppermute(block, "rows", route) for route in routes])
    step = 2
    while step < count:
        block = block + lax.ppermute(block, "rows", [(i, i ^ step) for i in range(count)])
        step *= 2
    return block


def combine(weights, real, imag):
    return weights[:, 0:1] * real - weights[:, 1:2] * imag


def end_products(vectors, block):
    times = lambda part: jnp.dot(block[part], vectors, preferred_element_type=F32)
    return jnp.concatenate([times(0), times(1)], 1).astype(BF16)


def emit_messages(first, last, coupling, out_a, out_b):
    is_even = lax.rem(lax.axis_index("rows"), 2) == 0
    last = dot_tn(coupling, last.astype(F32)).astype(BF16)
    out_a[...] = jnp.where(is_even, last, first)
    out_b[...] = jnp.where(is_even, first, last)


def start_kernel(source, vectors_at, upper_at, *refs):
    out_a, out_b, coupling, vectors, ends, arrived = refs
    rows = vectors.shape[0]
    band = coupling.shape[0]
    half = rows // 2
    pairs = [(vectors_at.at[pl.ds(at, half)], vectors.at[pl.ds(at, half)]) for at in (0, half)]
    for end, at in ((0, 0), (1, rows - band)):
        pairs += [(source.at[0, c, pl.ds(at, band)], ends.at[end, c]) for c in range(2)]
    pairs.append((upper_at.at[pl.ds(rows - band, band)], coupling))
    copies = [pltpu.make_async_copy(*pair, arrived.at[i]) for i, pair in enumerate(pairs)]
    for copy in copies:
        copy.start()
    for copy in copies[:4]:
        copy.wait()
    first = end_products(vectors[...], ends.at[0])
    for copy in copies[4:]:
        copy.wait()
    last = end_products(vectors[...], ends.at[1])
    emit_messages(first, last, coupling[...], out_a, out_b)


def from_hbm(kernel, outs, scratch, copies, *operands):
    far = lambda x: pltpu.with_memory_space_constraint(x, pltpu.HBM)
    kinds = [pltpu.HBM if is_far else pltpu.VMEM for _, is_far in operands]
    return pl.pallas_call(
        kernel,
        in_specs=[pl.BlockSpec(memory_space=kind) for kind in kinds],
        out_specs=[pl.BlockSpec(memory_space=pltpu.VMEM)] * len(outs),
        out_shape=outs,
        scratch_shapes=scratch + [pltpu.SemaphoreType.DMA((copies,))],
        cost_estimate=pl.CostEstimate(flops=10**8, bytes_accessed=10**6, transcendentals=0),
        compiler_params=pltpu.CompilerParams(vmem_limit_bytes=GRANT),
    )(*[far(x) if is_far else local(x) for x, is_far in operands])


def start(vectors, upper_tiles, inverse):
    rows, columns = vectors.shape
    band = upper_tiles.shape[1]
    message = like((band, 2 * columns), BF16)
    outs = [message, message, like((band, band)), like(vectors.shape, BF16)]
    scratch = [pltpu.VMEM((2, 2, band, rows), BF16)]
    operands = [(inverse, True), (vectors, True), (upper_tiles, True)]
    return from_hbm(start_kernel, outs, scratch, 7, *operands)


def tile_of(rows, band):
    return 2 * band if rows % (2 * band) == 0 else band


def edge_of(weights, got, coupling, rows, on_chip, factor=None):
    columns = got.shape[1] // 2
    band = coupling.shape[0]
    is_even = lax.rem(lax.axis_index("rows"), 2) == 0
    is_next = is_even if on_chip else jnp.logical_not(is_even)
    if factor is None:
        below = dot(coupling[...], got[...].astype(F32)).astype(BF16)
        edge = jnp.where(is_next, below, got[...]).astype(F32)
    else:
        turned = jnp.concatenate([got[:, :columns], got[:, columns:]], 0)
        turned = dot_three(turned, factor, NT)
        edge = jnp.concatenate([turned[:band], turned[band:]], 1)
        edge = jnp.where(is_next, dot_three(coupling[...], edge), edge)
    real, imag = edge[:, :columns], edge[:, columns:]
    at = pl.multiple_of(jnp.where(is_next, rows - band, 0), band)
    under = weights[:, 0:1] * imag + weights[:, 1:2] * real
    return at, jnp.concatenate([combine(weights, real, imag), -under], 0)


def edge_terms(edges, inverse, span, band):
    left = [inverse[0, c, span, pl.ds(at, band)] for at, _ in edges for c in range(2)]
    high, rest = halves_of(jnp.concatenate([edge for _, edge in edges], 0))
    left = jnp.concatenate(left, 1)
    times = lambda right: jnp.dot(left, right, preferred_element_type=F32)
    return times(high) + times(rest)


def products(weights, vectors, inverse, span):
    real = jnp.dot(inverse[0, 0, span], vectors[...], preferred_element_type=F32)
    imag = jnp.dot(inverse[0, 1, span], vectors[...], preferred_element_type=F32)
    return combine(weights, real, imag)


def start_base_kernel(weights_at, source, vectors, coupling, got, base, inverse, weights, arrived):
    rows = vectors.shape[0]
    tile = tile_of(rows, coupling.shape[0])
    spans = [pl.ds(at, tile) for at in range(0, rows, tile)]
    pairs = [(weights_at, weights)]
    pairs += [(source.at[:, :, span], inverse.at[:, :, span]) for span in spans]
    copies = [pltpu.make_async_copy(*pair, arrived.at[i]) for i, pair in enumerate(pairs)]
    for copy in copies:
        copy.start()
    copies[0].wait()
    band = coupling.shape[0]
    edges = [edge_of(weights, got, coupling, rows, True)]
    for copy, span in zip(copies[1:], spans):
        copy.wait()
        term = products(weights, vectors, inverse, span)
        base[span] = term + edge_terms(edges, inverse, span, band)


def start_base(weights, inverse, vectors, coupling, got):
    rows, columns = vectors.shape
    outs = [like((rows, columns)), like(inverse.shape, BF16), like(weights.shape)]
    operands = [(weights, True), (inverse, True), (vectors, False), (coupling, False), (got, False)]
    return from_hbm(start_base_kernel, outs, [], rows // coupling.shape[0] + 1, *operands)


def refined(field, low, factor):
    high, rest = halves_of(factor)
    times = lambda a, b: lax.dot_general(a, b, NT, preferred_element_type=F32)
    return times(field, high) + (times(field, rest) + times(low, high))


def tips_kernel(field, low, coupling, inverse, out_a, out_b):
    band = coupling.shape[0]
    is_even = lax.rem(lax.axis_index("rows"), 2) == 0

    def both(at):
        times = lambda part, x: jnp.dot(
            inverse[0, part, at : at + band], x, preferred_element_type=F32
        )
        of = lambda part: times(part, field[...]) + times(part, low[...])
        return jnp.concatenate([of(0), of(1)], 1)

    first = both(0)
    last = dot_tn(coupling[...], both(field.shape[0] - band))
    out_a[...] = jnp.where(is_even, last, first)
    out_b[...] = jnp.where(is_even, first, last)


def tips(field, low, coupling, inverse):
    message = like((coupling.shape[0], 2 * field.shape[1]))
    return whole(tips_kernel, [message, message], field, low, coupling, inverse)


def emit_term(term, own, sends):
    node = lax.axis_index("node")
    size = own.shape[0]
    steps = lax.axis_size("node")
    for s, out in enumerate((own,) + sends):
        where = pl.multiple_of((node ^ (s if s < steps else s - steps + 1)) * size, 8)
        value = term[pl.ds(where, size), :]
        if s >= steps:
            value = value - value.astype(BF16).astype(F32)
        out[...] = value.astype(out.dtype)


def solve_kernel(weights, field, low, factor, coupling, inverse, got_a, got_b, own, *refs):
    sends, (current, term) = refs[:-2], refs[-2:]
    current[...] = refined(field[...], low[...], factor[...]).astype(BF16)
    rows = field.shape[0]
    band = coupling.shape[0]
    tile = tile_of(rows, band)
    edges = [
        edge_of(weights, got, coupling, rows, on_chip, factor[...])
        for got, on_chip in ((got_a, True), (got_b, False))
    ]
    for at in range(0, rows, tile):
        span = pl.ds(at, tile)
        part = products(weights, current, inverse, span)
        term[span] = part + edge_terms(edges, inverse, span, band)
    emit_term(term, own, sends)


def blocks_of(rows, columns, parts):
    count = lax.axis_size("node")
    size = rows // count
    return [like((size, columns))] + [like((size, columns), BF16)] * (parts * (count - 1))


def solve(weights, field, low, factor, coupling, inverse, got_a, got_b, parts):
    rows, columns = field.shape
    return whole(
        solve_kernel,
        blocks_of(rows, columns, parts),
        weights,
        field,
        low,
        factor,
        coupling,
        inverse,
        got_a,
        got_b,
        scratch=[pltpu.VMEM((rows, columns), BF16), pltpu.VMEM((rows, columns), F32)],
    )


def correct_kernel(weights, base, got, coupling, inverse, own, *refs):
    sends, term = refs[:-1], refs[-1]
    rows = base.shape[0]
    band = coupling.shape[0]
    tile = tile_of(rows, band)
    edges = [edge_of(weights, got, coupling, rows, False)]
    for at in range(0, rows, tile):
        span = pl.ds(at, tile)
        term[span] = base[span] + edge_terms(edges, inverse, span, band)
    emit_term(term, own, sends)


def correct(weights, base, got, coupling, inverse, parts):
    rows, columns = base.shape
    outs = blocks_of(rows, columns, parts)
    scratch = [pltpu.VMEM((rows, columns), F32)]
    return whole(correct_kernel, outs, weights, base, got, coupling, inverse, scratch=scratch)


def place(blocks, out):
    node = lax.axis_index("node")
    size = blocks[0].shape[0]
    for step, block in enumerate(blocks):
        out[pl.ds(pl.multiple_of((node ^ step) * size, 8), size), :] = block[...]


def gram_kernel(*refs):
    *blocks, field, head, part, matrix = refs
    place(blocks, field)
    head[...] = field[: head.shape[0]]
    matrix[...] = lax.dot_general(field[...], field[...], TN, preferred_element_type=F32)
    size = part.shape[0]
    part[...] = matrix[pl.ds(pl.multiple_of(lax.axis_index("node") * size, 8), size), :]


def gram_slice(blocks, band):
    rows, columns = blocks[0].shape
    count = len(blocks)
    outs = [
        like((rows * count, columns), BF16),
        like((band, columns), BF16),
        like((columns // count, columns)),
    ]
    scratch = [pltpu.VMEM((columns, columns), F32)]
    return whole(gram_kernel, outs, *blocks, scratch=scratch)


def join_kernel(*refs):
    place(refs[:-1], refs[-1])


def join(blocks):
    rows, columns = blocks[0].shape
    return whole(join_kernel, like((rows * len(blocks), columns), BF16), *blocks)


def eliminate(block, out, base, spread):
    count = block.shape[0]
    full = (GROUP, count)
    lane = lax.broadcasted_iota(jnp.int32, full, 1)
    span = range(GROUP)
    tiles = [block[t * GROUP : (t + 1) * GROUP] for t in range(count // GROUP)]
    room = GROUP * (GROUP + 1)
    for t in range(len(tiles)):
        k = t * GROUP
        tile = tiles[t]
        slot = (t % 2) * room
        spread[slot : slot + GROUP] = tile
        for j in span:
            at = slot + GROUP * (j + 1)
            spread[at : at + GROUP] = jnp.broadcast_to(tile[:, k + j : k + j + 1], full)
        across = lambda row: spread[pl.ds(slot + row, GROUP, stride=0), :]
        rows = [across(i) for i in span]
        pivot = [[across(GROUP * (j + 1) + i) for j in range(i + 1)] for i in span]
        low = [[None] * GROUP for _ in span]
        inverse = [None] * GROUP
        pivots = [None] * GROUP
        for j in range(0, GROUP, 2):
            lead, side = pivot[j][j], pivot[j + 1][j]
            determinant = lead * pivot[j + 1][j + 1] - side * side
            inverse[j] = 1.0 / lead
            inverse[j + 1] = lead * (1.0 / determinant)
            pivots[j] = lead
            pivots[j + 1] = determinant * inverse[j]
            low[j + 1][j] = side * inverse[j]
            second = [None] * GROUP
            for i in range(j + 2, GROUP):
                low[i][j] = pivot[i][j] * inverse[j]
                second[i] = pivot[i][j + 1] - low[i][j] * side
                low[i][j + 1] = second[i] * inverse[j + 1]
            for i in range(j + 2, GROUP):
                for m in range(j + 2, i + 1):
                    pivot[i][m] = pivot[i][m] - low[i][j] * pivot[m][j] - low[i][j + 1] * second[m]
        inv = [[None] * GROUP for _ in span]
        for j in span:
            for i in range(j + 1, GROUP):
                total = low[i][j]
                for m in range(j + 1, i):
                    total = total + low[i][m] * inv[m][j]
                inv[i][j] = -total
        inside = (lane >= k) & (lane < k + GROUP)
        rows = [jnp.where(inside, jnp.where(lane == k + i, 1.0, 0.0), rows[i]) for i in span]
        done = []
        for i in span:
            total = rows[i]
            for j in range(i):
                total = total + inv[i][j] * rows[j]
            done.append(total)
            at = base + k + i
            row = jnp.where(lane < k + GROUP, total * lax.rsqrt(pivots[i]), 0.0)
            out[at : at + 1, base : base + count] = row[:1]
        if t + 1 < len(tiles):
            scaled = [done[i] * inverse[i] for i in span]
            back = []
            for j in span:
                total = scaled[j]
                for i in range(j + 1, GROUP):
                    total = total + inv[i][j] * scaled[i]
                back.append(total)
            for u in range(t + 1, len(tiles)):
                old = tiles[u]
                new = jnp.where(inside, 0.0, old)
                for j in span:
                    new = new - old[:, k + j : k + j + 1] * back[j]
                tiles[u] = new


def first_factor_kernel(order, *refs):
    *blocks, top, corner, rest, across, matrix, spread = refs
    place(blocks, matrix)
    count = matrix.shape[0]
    half = count // 2
    values = matrix[...] * (1.0 / order)
    eye = lax.broadcasted_iota(jnp.int32, (count, count), 0) == lax.broadcasted_iota(
        jnp.int32, (count, count), 1
    )
    diagonal = jnp.where(eye, values, 0.0)
    scale = lax.rsqrt(jnp.sum(diagonal, 0, keepdims=True))
    down = lax.rsqrt(jnp.sum(diagonal, 1, keepdims=True))
    across[...] = scale
    values = values * scale * down
    eliminate(values[:half, :half], top, 0, spread)
    beside = dot(top[...], values[:half, half:])
    corner[...] = dot_tn(beside, top[...])
    rest[...] = values[half:, half:] - dot_tn(beside, beside)


def second_factor_kernel(top, corner, rest, across, out, spread):
    half = top.shape[0]
    out[:half, :half] = top[...]
    out[:half, half:] = jnp.zeros((half, half), F32)
    eliminate(rest[...], out, half, spread)
    out[half:, :half] = -dot(out[half:, half:], corner[...])
    out[...] = out[...] * across[...]


def spread_room(columns):
    return pltpu.VMEM((2 * GROUP * (GROUP + 1) + GROUP, columns // 2), F32)


def first_factor(blocks, order):
    columns = blocks[0].shape[1]
    half = like((columns // 2, columns // 2))
    return whole(
        functools.partial(first_factor_kernel, order),
        [half, half, half, like((1, columns))],
        *blocks,
        scratch=[pltpu.VMEM((columns, columns), F32), spread_room(columns)],
        flops=6 * 10**9,
    )


def second_factor(halves):
    columns = halves[3].shape[1]
    return whole(
        second_factor_kernel,
        like((columns, columns)),
        *halves,
        scratch=[spread_room(columns)],
        flops=6 * 10**9,
    )


def next_head(head):
    count = lax.axis_size("rows")
    return lax.ppermute(head, "rows", [(i + 1, i) for i in range(count - 1)])


def band_kernel(field, low, after, diag_tiles, upper_tiles, part, image, matrix):
    band = after.shape[0]
    tiles = field.shape[0] // band

    def values(at):
        return field[at].astype(F32) + low[at].astype(F32)

    for t in range(tiles):
        at = slice(t * band, (t + 1) * band)
        following = slice((t + 1) * band, (t + 2) * band)
        following = after[...].astype(F32) if t == tiles - 1 else values(following)
        image[at] = 0.5 * dot_three(diag_tiles[at], values(at)) + dot_three(upper_tiles[at], following)
    matrix[...] = dot_two(field[...], image[...], TN)
    matrix[...] += lax.dot_general(
        low[...], image[...].astype(BF16), TN, preferred_element_type=F32
    )
    size = part.shape[0]
    part[...] = matrix[pl.ds(pl.multiple_of(lax.axis_index("node") * size, 8), size), :]


def band_slice(field, low, after, diag_tiles, upper_tiles):
    rows, columns = field.shape
    return whole(
        band_kernel,
        like((columns // lax.axis_size("node"), columns)),
        field,
        low,
        after,
        diag_tiles,
        upper_tiles,
        scratch=[pltpu.VMEM((rows, columns), F32), pltpu.VMEM((columns, columns), F32)],
    )


def last_kernel(field, low, factor, out):
    out[...] = refined(field[...], low[...], factor[...])


def last(field, low, factor):
    return whole(last_kernel, like(field.shape), field, low, factor)


def finish_kernel(order, vectors, *refs):
    blocks, factors = refs[: -5 - ITERS], refs[-5 - ITERS : -5]
    vectors_at, projected_at, projected, matrix, sent = refs[-5:]
    copies = []

    def send(source, target):
        copies.append(pltpu.make_async_copy(source, target, sent.at[len(copies)]))
        copies[-1].start()

    send(vectors, vectors_at)
    node = lax.axis_index("node")
    size = blocks[0].shape[0] // ITERS
    for k, factor in enumerate(factors):
        for step, block in enumerate(blocks):
            at = pl.multiple_of((node ^ step) * size, 8)
            matrix[pl.ds(at, size), :] = block[k * size : (k + 1) * size]
        value = dot_three(dot_three(factor[...], matrix[...]), factor[...], NT)
        projected[k] = (value + value.T) * (1.0 / order)
        send(projected.at[k], projected_at.at[k])
    for copy in copies:
        copy.wait()


def finish(vectors, blocks, factors, order):
    rows, columns = vectors.shape
    operands = [vectors, *blocks, *factors]
    vmem = pl.BlockSpec(memory_space=pltpu.VMEM)
    shapes = [(rows, columns), (ITERS, columns, columns)]
    return pl.pallas_call(
        functools.partial(finish_kernel, order),
        in_specs=[vmem for _ in operands],
        out_specs=[pl.BlockSpec(memory_space=pltpu.HBM)] * 2,
        out_shape=[jax.ShapeDtypeStruct(x, F32) for x in shapes],
        scratch_shapes=[
            pltpu.VMEM(shapes[1], F32),
            pltpu.VMEM((columns, columns), F32),
            pltpu.SemaphoreType.DMA((1 + ITERS,)),
        ],
        cost_estimate=pl.CostEstimate(flops=10**9, bytes_accessed=10**6, transcendentals=0),
        compiler_params=pltpu.CompilerParams(vmem_limit_bytes=GRANT),
        name="finish",
    )(*[local(x) for x in operands])


def after(value, *others):
    return lax.optimization_barrier((value,) + others)[0]


def per_device(subspace, inverse, weights, diag_tiles, upper_tiles):
    order = float(subspace.shape[0] * lax.axis_size("rows"))
    band = upper_tiles.shape[1]
    partners = lax.axis_size("node") - 1
    factors, pairs = [], []
    for iteration in range(ITERS):
        final = iteration == ITERS - 1
        parts = 1 if final else 2
        if iteration == 0:
            out_a, out_b, coupling, vectors = start(subspace, upper_tiles, inverse)
            got_b = link_swap(out_b)
            got_a = core_swap(out_a)
            base, inverse, weights = start_base(weights, inverse, vectors, coupling, got_a)
            own, *terms = correct(weights, base, got_b, coupling, inverse, parts)
        else:
            own, *terms = solve(
                weights, field, low, factor, coupling, inverse, got_a, got_b, parts
            )
        got = node_spread(terms[:partners])
        if not final:
            low_got = node_spread(terms[partners:])
        total = tree_sum([own] + [x.astype(F32) for x in got])
        piece = total.astype(BF16)
        blocks = [piece] + node_spread([piece] * partners)
        total, sent = lax.optimization_barrier((total, piece))
        if not final:
            total = total + tree_sum([x.astype(F32) for x in low_got])
        low_piece = (total - sent.astype(F32)).astype(BF16)
        low = join([low_piece] + node_spread([low_piece] * partners))
        field, head, part = gram_slice(blocks, band)
        part = part + core_swap(part)
        following = next_head(after(head, part))
        total = chip_sum(part)
        gathered = [total] + node_spread([total] * partners)
        pair = band_slice(field, low, after(following, total), diag_tiles, upper_tiles)
        if not final:
            out_a, out_b = tips(field, low, coupling, inverse)
            got_b = link_swap(out_b)
            got_a = core_swap(out_a)
        halves = first_factor(gathered, order)
        pair = pair + core_swap(pair)
        pairs.append(chip_sum(after(pair, *gathered)))
        if final:
            pair = after(jnp.concatenate(pairs, 0), *halves)
            spread = [pair] + node_spread([pair] * partners)
        factor = second_factor(halves)
        factors.append(factor)
    vectors = last(field, low, factor)
    orthonormal, projected = finish(vectors, spread, factors, order)
    return orthonormal, projected


def solution(mesh):
    placed = (
        P("rows", None),
        P("node", None, "rows", None),
        P("node", None),
        P("rows", None),
        P("rows", None),
    )
    return jax.shard_map(
        per_device, mesh=mesh, in_specs=placed, out_specs=(P("rows", None), P()), check_vma=False
    )
```

```python
import functools

import jax
import jax.numpy as jnp
from jax import lax
from jax.experimental import pallas as pl
from jax.experimental.pallas import tpu as pltpu
from jax.sharding import PartitionSpec as P


ITERS = 2
GROUP = 8
GRANT = 16 * 2**20

precise = lax.Precision.HIGHEST
F32 = jnp.float32
BF16 = jnp.bfloat16


def dot(left, right):
    return jnp.dot(left, right, precision=precise, preferred_element_type=F32)


def dot_tn(left, right):
    dims = (((0,), (0,)), ((), ()))
    return lax.dot_general(left, right, dims, precision=precise, preferred_element_type=F32)


def halves_of(value):
    high = value.astype(BF16)
    return high, (value - high.astype(F32)).astype(BF16)


def dot_three(left, right, dims=(((1,), (0,)), ((), ()))):
    times = lambda a, b: lax.dot_general(a, b, dims, preferred_element_type=F32)
    (a, b), (c, d) = halves_of(left), halves_of(right)
    return times(a, c) + (times(a, d) + times(b, c))


def dot_two(left, right, dims=(((1,), (0,)), ((), ()))):
    times = lambda a, b: lax.dot_general(a, b, dims, preferred_element_type=F32)
    c, d = halves_of(right)
    return times(left, c) + times(left, d)


NT = (((1,), (1,)), ((), ()))
TN = (((0,), (0,)), ((), ()))


def like(shape, dtype=F32):
    return pltpu.VMEM(shape, dtype)


def halves_of(value):
    high = value.astype(BF16)
    return high, (value - high.astype(F32)).astype(BF16)


def dot_three(left, right, dims=(((1,), (0,)), ((), ()))):
    times = lambda a, b: lax.dot_general(a, b, dims, preferred_element_type=F32)
    (a, b), (c, d) = halves_of(left), halves_of(right)
    return times(a, c) + (times(a, d) + times(b, c))


def dot_two(left, right, dims=(((1,), (0,)), ((), ()))):
    times = lambda a, b: lax.dot_general(a, b, dims, preferred_element_type=F32)
    c, d = halves_of(right)
    return times(left, c) + times(left, d)


NT = (((1,), (1,)), ((), ()))
TN = (((0,), (0,)), ((), ()))


def local(value):
    return pltpu.with_memory_space_constraint(value, pltpu.VMEM)


def whole(kernel, out_shape, *operands, scratch=(), flops=10**8):
    size = sum(x.size * x.dtype.itemsize for x in operands)
    vmem = pl.BlockSpec(memory_space=pltpu.VMEM)
    return pl.pallas_call(
        kernel,
        out_shape=out_shape,
        in_specs=[vmem for _ in operands],
        out_specs=jax.tree.map(lambda _: vmem, out_shape),
        scratch_shapes=list(scratch),
        cost_estimate=pl.CostEstimate(flops=flops, bytes_accessed=size, transcendentals=0),
        compiler_params=pltpu.CompilerParams(vmem_limit_bytes=GRANT),
    )(*[local(x) for x in operands])


def node_swap(block, step):
    count = lax.axis_size("node")
    return lax.ppermute(block, "node", [(i, i ^ step) for i in range(count)])


def core_swap(block):
    count = lax.axis_size("rows")
    return lax.ppermute(block, "rows", [(i, i ^ 1) for i in range(count)])


def link_swap(block):
    count = lax.axis_size("rows")
    pairs = [(i, i + 1) for i in range(1, count - 1, 2)]
    return lax.ppermute(block, "rows", pairs + [(b, a) for a, b in pairs])


def node_spread(blocks):
    return [node_swap(block, step + 1) for step, block in enumerate(blocks)]


def tree_sum(blocks):
    while len(blocks) > 1:
        odd = blocks[len(blocks) // 2 * 2 :]
        blocks = [a + b for a, b in zip(blocks[::2], blocks[1::2])] + odd
    return blocks[0]


def chip_sum(block):
    count = lax.axis_size("rows")
    chips = count // 2
    if chips <= 4:
        steps = range(1, chips)
        routes = [[(i, i ^ (2 * s)) for i in range(count)] for s in steps]
        return tree_sum([block] + [lax.ppermute(block, "rows", route) for route in routes])
    step = 2
    while step < count:
        block = block + lax.ppermute(block, "rows", [(i, i ^ step) for i in range(count)])
        step *= 2
    return block


def combine(weights, real, imag):
    return weights[:, 0:1] * real - weights[:, 1:2] * imag


def end_products(vectors, block):
    times = lambda part: jnp.dot(block[part], vectors, preferred_element_type=F32)
    return jnp.concatenate([times(0), times(1)], 1).astype(BF16)


def emit_messages(first, last, coupling, out_a, out_b):
    is_even = lax.rem(lax.axis_index("rows"), 2) == 0
    last = dot_tn(coupling, last.astype(F32)).astype(BF16)
    out_a[...] = jnp.where(is_even, last, first)
    out_b[...] = jnp.where(is_even, first, last)


def start_kernel(source, vectors_at, upper_at, *refs):
    out_a, out_b, coupling, vectors, ends, arrived = refs
    rows = vectors.shape[0]
    band = coupling.shape[0]
    half = rows // 2
    pairs = [(vectors_at.at[pl.ds(at, half)], vectors.at[pl.ds(at, half)]) for at in (0, half)]
    for end, at in ((0, 0), (1, rows - band)):
        pairs += [(source.at[0, c, pl.ds(at, band)], ends.at[end, c]) for c in range(2)]
    pairs.append((upper_at.at[pl.ds(rows - band, band)], coupling))
    copies = [pltpu.make_async_copy(*pair, arrived.at[i]) for i, pair in enumerate(pairs)]
    for copy in copies:
        copy.start()
    for copy in copies[:4]:
        copy.wait()
    first = end_products(vectors[...], ends.at[0])
    for copy in copies[4:]:
        copy.wait()
    last = end_products(vectors[...], ends.at[1])
    emit_messages(first, last, coupling[...], out_a, out_b)


def from_hbm(kernel, outs, scratch, copies, *operands):
    far = lambda x: pltpu.with_memory_space_constraint(x, pltpu.HBM)
    kinds = [pltpu.HBM if is_far else pltpu.VMEM for _, is_far in operands]
    return pl.pallas_call(
        kernel,
        in_specs=[pl.BlockSpec(memory_space=kind) for kind in kinds],
        out_specs=[pl.BlockSpec(memory_space=pltpu.VMEM)] * len(outs),
        out_shape=outs,
        scratch_shapes=scratch + [pltpu.SemaphoreType.DMA((copies,))],
        cost_estimate=pl.CostEstimate(flops=10**8, bytes_accessed=10**6, transcendentals=0),
        compiler_params=pltpu.CompilerParams(vmem_limit_bytes=GRANT),
    )(*[far(x) if is_far else local(x) for x, is_far in operands])


def start(vectors, upper_tiles, inverse):
    rows, columns = vectors.shape
    band = upper_tiles.shape[1]
    message = like((band, 2 * columns), BF16)
    outs = [message, message, like((band, band)), like(vectors.shape, BF16)]
    scratch = [pltpu.VMEM((2, 2, band, rows), BF16)]
    operands = [(inverse, True), (vectors, True), (upper_tiles, True)]
    return from_hbm(start_kernel, outs, scratch, 7, *operands)


def tile_of(rows, band):
    return 2 * band if rows % (2 * band) == 0 else band


def edge_of(weights, got, coupling, rows, on_chip, factor=None):
    columns = got.shape[1] // 2
    band = coupling.shape[0]
    is_even = lax.rem(lax.axis_index("rows"), 2) == 0
    is_next = is_even if on_chip else jnp.logical_not(is_even)
    if factor is None:
        below = dot(coupling[...], got[...].astype(F32)).astype(BF16)
        edge = jnp.where(is_next, below, got[...]).astype(F32)
    else:
        turned = jnp.concatenate([got[:, :columns], got[:, columns:]], 0)
        turned = dot_three(turned, factor, NT)
        edge = jnp.concatenate([turned[:band], turned[band:]], 1)
        edge = jnp.where(is_next, dot_three(coupling[...], edge), edge)
    real, imag = edge[:, :columns], edge[:, columns:]
    at = pl.multiple_of(jnp.where(is_next, rows - band, 0), band)
    under = weights[:, 0:1] * imag + weights[:, 1:2] * real
    return at, jnp.concatenate([combine(weights, real, imag), -under], 0)


def edge_terms(edges, inverse, span, band):
    left = [inverse[0, c, span, pl.ds(at, band)] for at, _ in edges for c in range(2)]
    high, rest = halves_of(jnp.concatenate([edge for _, edge in edges], 0))
    left = jnp.concatenate(left, 1)
    times = lambda right: jnp.dot(left, right, preferred_element_type=F32)
    return times(high) + times(rest)


def products(weights, vectors, inverse, span):
    real = jnp.dot(inverse[0, 0, span], vectors[...], preferred_element_type=F32)
    imag = jnp.dot(inverse[0, 1, span], vectors[...], preferred_element_type=F32)
    return combine(weights, real, imag)


def start_base_kernel(weights_at, source, vectors, coupling, got, base, inverse, weights, arrived):
    rows = vectors.shape[0]
    tile = tile_of(rows, coupling.shape[0])
    spans = [pl.ds(at, tile) for at in range(0, rows, tile)]
    pairs = [(weights_at, weights)]
    pairs += [(source.at[:, :, span], inverse.at[:, :, span]) for span in spans]
    copies = [pltpu.make_async_copy(*pair, arrived.at[i]) for i, pair in enumerate(pairs)]
    for copy in copies:
        copy.start()
    copies[0].wait()
    band = coupling.shape[0]
    edges = [edge_of(weights, got, coupling, rows, True)]
    for copy, span in zip(copies[1:], spans):
        copy.wait()
        term = products(weights, vectors, inverse, span)
        base[span] = term + edge_terms(edges, inverse, span, band)


def start_base(weights, inverse, vectors, coupling, got):
    rows, columns = vectors.shape
    outs = [like((rows, columns)), like(inverse.shape, BF16), like(weights.shape)]
    operands = [(weights, True), (inverse, True), (vectors, False), (coupling, False), (got, False)]
    return from_hbm(start_base_kernel, outs, [], rows // coupling.shape[0] + 1, *operands)


def refined(field, low, factor):
    high, rest = halves_of(factor)
    times = lambda a, b: lax.dot_general(a, b, NT, preferred_element_type=F32)
    return times(field, high) + (times(field, rest) + times(low, high))


def tips_kernel(field, low, coupling, inverse, out_a, out_b):
    band = coupling.shape[0]
    is_even = lax.rem(lax.axis_index("rows"), 2) == 0

    def both(at):
        times = lambda part, x: jnp.dot(
            inverse[0, part, at : at + band], x, preferred_element_type=F32
        )
        of = lambda part: times(part, field[...]) + times(part, low[...])
        return jnp.concatenate([of(0), of(1)], 1)

    first = both(0)
    last = dot_tn(coupling[...], both(field.shape[0] - band))
    out_a[...] = jnp.where(is_even, last, first)
    out_b[...] = jnp.where(is_even, first, last)


def tips(field, low, coupling, inverse):
    message = like((coupling.shape[0], 2 * field.shape[1]))
    return whole(tips_kernel, [message, message], field, low, coupling, inverse)


def emit_term(term, own, sends):
    node = lax.axis_index("node")
    size = own.shape[0]
    steps = lax.axis_size("node")
    for s, out in enumerate((own,) + sends):
        where = pl.multiple_of((node ^ (s if s < steps else s - steps + 1)) * size, 8)
        value = term[pl.ds(where, size), :]
        if s >= steps:
            value = value - value.astype(BF16).astype(F32)
        out[...] = value.astype(out.dtype)


def solve_kernel(weights, field, low, factor, coupling, inverse, got_a, got_b, own, *refs):
    sends, (current, term) = refs[:-2], refs[-2:]
    current[...] = refined(field[...], low[...], factor[...]).astype(BF16)
    rows = field.shape[0]
    band = coupling.shape[0]
    tile = tile_of(rows, band)
    edges = [
        edge_of(weights, got, coupling, rows, on_chip, factor[...])
        for got, on_chip in ((got_a, True), (got_b, False))
    ]
    for at in range(0, rows, tile):
        span = pl.ds(at, tile)
        part = products(weights, current, inverse, span)
        term[span] = part + edge_terms(edges, inverse, span, band)
    emit_term(term, own, sends)


def blocks_of(rows, columns, parts):
    count = lax.axis_size("node")
    size = rows // count
    return [like((size, columns))] + [like((size, columns), BF16)] * (parts * (count - 1))


def solve(weights, field, low, factor, coupling, inverse, got_a, got_b, parts):
    rows, columns = field.shape
    return whole(
        solve_kernel,
        blocks_of(rows, columns, parts),
        weights,
        field,
        low,
        factor,
        coupling,
        inverse,
        got_a,
        got_b,
        scratch=[pltpu.VMEM((rows, columns), BF16), pltpu.VMEM((rows, columns), F32)],
    )


def correct_kernel(weights, base, got, coupling, inverse, own, *refs):
    sends, term = refs[:-1], refs[-1]
    rows = base.shape[0]
    band = coupling.shape[0]
    tile = tile_of(rows, band)
    edges = [edge_of(weights, got, coupling, rows, False)]
    for at in range(0, rows, tile):
        span = pl.ds(at, tile)
        term[span] = base[span] + edge_terms(edges, inverse, span, band)
    emit_term(term, own, sends)


def correct(weights, base, got, coupling, inverse, parts):
    rows, columns = base.shape
    outs = blocks_of(rows, columns, parts)
    scratch = [pltpu.VMEM((rows, columns), F32)]
    return whole(correct_kernel, outs, weights, base, got, coupling, inverse, scratch=scratch)


def place(blocks, out):
    node = lax.axis_index("node")
    size = blocks[0].shape[0]
    for step, block in enumerate(blocks):
        out[pl.ds(pl.multiple_of((node ^ step) * size, 8), size), :] = block[...]


def gram_kernel(*refs):
    *blocks, field, head, part, matrix = refs
    place(blocks, field)
    head[...] = field[: head.shape[0]]
    matrix[...] = lax.dot_general(field[...], field[...], TN, preferred_element_type=F32)
    size = part.shape[0]
    part[...] = matrix[pl.ds(pl.multiple_of(lax.axis_index("node") * size, 8), size), :]


def gram_slice(blocks, band):
    rows, columns = blocks[0].shape
    count = len(blocks)
    outs = [
        like((rows * count, columns), BF16),
        like((band, columns), BF16),
        like((columns // count, columns)),
    ]
    scratch = [pltpu.VMEM((columns, columns), F32)]
    return whole(gram_kernel, outs, *blocks, scratch=scratch)


def join_kernel(*refs):
    place(refs[:-1], refs[-1])


def join(blocks):
    rows, columns = blocks[0].shape
    return whole(join_kernel, like((rows * len(blocks), columns), BF16), *blocks)


def eliminate(block, out, base, spread):
    count = block.shape[0]
    full = (GROUP, count)
    lane = lax.broadcasted_iota(jnp.int32, full, 1)
    span = range(GROUP)
    tiles = [block[t * GROUP : (t + 1) * GROUP] for t in range(count // GROUP)]
    room = GROUP * (GROUP + 1)
    for t in range(len(tiles)):
        k = t * GROUP
        tile = tiles[t]
        slot = (t % 2) * room
        spread[slot : slot + GROUP] = tile
        for j in span:
            at = slot + GROUP * (j + 1)
            spread[at : at + GROUP] = jnp.broadcast_to(tile[:, k + j : k + j + 1], full)
        across = lambda row: spread[pl.ds(slot + row, GROUP, stride=0), :]
        rows = [across(i) for i in span]
        pivot = [[across(GROUP * (j + 1) + i) for j in range(i + 1)] for i in span]
        low = [[None] * GROUP for _ in span]
        inverse = [None] * GROUP
        pivots = [None] * GROUP
        for j in range(0, GROUP, 2):
            lead, side = pivot[j][j], pivot[j + 1][j]
            determinant = lead * pivot[j + 1][j + 1] - side * side
            inverse[j] = 1.0 / lead
            inverse[j + 1] = lead * (1.0 / determinant)
            pivots[j] = lead
            pivots[j + 1] = determinant * inverse[j]
            low[j + 1][j] = side * inverse[j]
            second = [None] * GROUP
            for i in range(j + 2, GROUP):
                low[i][j] = pivot[i][j] * inverse[j]
                second[i] = pivot[i][j + 1] - low[i][j] * side
                low[i][j + 1] = second[i] * inverse[j + 1]
            for i in range(j + 2, GROUP):
                for m in range(j + 2, i + 1):
                    pivot[i][m] = pivot[i][m] - low[i][j] * pivot[m][j] - low[i][j + 1] * second[m]
        inv = [[None] * GROUP for _ in span]
        for j in span:
            for i in range(j + 1, GROUP):
                total = low[i][j]
                for m in range(j + 1, i):
                    total = total + low[i][m] * inv[m][j]
                inv[i][j] = -total
        inside = (lane >= k) & (lane < k + GROUP)
        rows = [jnp.where(inside, jnp.where(lane == k + i, 1.0, 0.0), rows[i]) for i in span]
        done = []
        for i in span:
            total = rows[i]
            for j in range(i):
                total = total + inv[i][j] * rows[j]
            done.append(total)
            at = base + k + i
            row = jnp.where(lane < k + GROUP, total * lax.rsqrt(pivots[i]), 0.0)
            out[at : at + 1, base : base + count] = row[:1]
        if t + 1 < len(tiles):
            scaled = [done[i] * inverse[i] for i in span]
            back = []
            for j in span:
                total = scaled[j]
                for i in range(j + 1, GROUP):
                    total = total + inv[i][j] * scaled[i]
                back.append(total)
            for u in range(t + 1, len(tiles)):
                old = tiles[u]
                new = jnp.where(inside, 0.0, old)
                for j in span:
                    new = new - old[:, k + j : k + j + 1] * back[j]
                tiles[u] = new


def first_factor_kernel(order, *refs):
    *blocks, top, corner, rest, across, matrix, spread = refs
    place(blocks, matrix)
    count = matrix.shape[0]
    half = count // 2
    values = matrix[...] * (1.0 / order)
    eye = lax.broadcasted_iota(jnp.int32, (count, count), 0) == lax.broadcasted_iota(
        jnp.int32, (count, count), 1
    )
    diagonal = jnp.where(eye, values, 0.0)
    scale = lax.rsqrt(jnp.sum(diagonal, 0, keepdims=True))
    down = lax.rsqrt(jnp.sum(diagonal, 1, keepdims=True))
    across[...] = scale
    values = values * scale * down
    eliminate(values[:half, :half], top, 0, spread)
    beside = dot(top[...], values[:half, half:])
    corner[...] = dot_tn(beside, top[...])
    rest[...] = values[half:, half:] - dot_tn(beside, beside)


def second_factor_kernel(top, corner, rest, across, out, spread):
    half = top.shape[0]
    out[:half, :half] = top[...]
    out[:half, half:] = jnp.zeros((half, half), F32)
    eliminate(rest[...], out, half, spread)
    out[half:, :half] = -dot(out[half:, half:], corner[...])
    out[...] = out[...] * across[...]


def spread_room(columns):
    return pltpu.VMEM((2 * GROUP * (GROUP + 1) + GROUP, columns // 2), F32)


def first_factor(blocks, order):
    columns = blocks[0].shape[1]
    half = like((columns // 2, columns // 2))
    return whole(
        functools.partial(first_factor_kernel, order),
        [half, half, half, like((1, columns))],
        *blocks,
        scratch=[pltpu.VMEM((columns, columns), F32), spread_room(columns)],
        flops=6 * 10**9,
    )


def second_factor(halves):
    columns = halves[3].shape[1]
    return whole(
        second_factor_kernel,
        like((columns, columns)),
        *halves,
        scratch=[spread_room(columns)],
        flops=6 * 10**9,
    )


def next_head(head):
    count = lax.axis_size("rows")
    return lax.ppermute(head, "rows", [(i + 1, i) for i in range(count - 1)])


def band_kernel(field, low, after, diag_tiles, upper_tiles, part, image, matrix):
    band = after.shape[0]
    tiles = field.shape[0] // band

    for t in range(tiles):
        at = slice(t * band, (t + 1) * band)
        if t < tiles - 1:
            both = slice(t * band, (t + 2) * band)
            high, rest = field[both], low[both]
        else:
            high = jnp.concatenate([field[at], after[...]], 0)
            rest = jnp.concatenate([low[at], jnp.zeros(after.shape, BF16)], 0)
        left, remainder = halves_of(jnp.concatenate([0.5 * diag_tiles[at], upper_tiles[at]], 1))
        times = lambda x, y: jnp.dot(x, y, preferred_element_type=F32)
        image[at] = times(left, high) + (times(left, rest) + times(remainder, high))
    matrix[...] = dot_two(field[...], image[...], TN)
    matrix[...] += lax.dot_general(
        low[...], image[...].astype(BF16), TN, preferred_element_type=F32
    )
    size = part.shape[0]
    part[...] = matrix[pl.ds(pl.multiple_of(lax.axis_index("node") * size, 8), size), :]


def band_slice(field, low, after, diag_tiles, upper_tiles):
    rows, columns = field.shape
    return whole(
        band_kernel,
        like((columns // lax.axis_size("node"), columns)),
        field,
        low,
        after,
        diag_tiles,
        upper_tiles,
        scratch=[pltpu.VMEM((rows, columns), F32), pltpu.VMEM((columns, columns), F32)],
    )


def last_kernel(field, low, factor, out):
    out[...] = refined(field[...], low[...], factor[...])


def last(field, low, factor):
    return whole(last_kernel, like(field.shape), field, low, factor)


def finish_kernel(order, vectors, *refs):
    blocks, factors = refs[: -5 - ITERS], refs[-5 - ITERS : -5]
    vectors_at, projected_at, projected, matrix, sent = refs[-5:]
    copies = []

    def send(source, target):
        copies.append(pltpu.make_async_copy(source, target, sent.at[len(copies)]))
        copies[-1].start()

    send(vectors, vectors_at)
    node = lax.axis_index("node")
    size = blocks[0].shape[0] // ITERS
    for k, factor in enumerate(factors):
        for step, block in enumerate(blocks):
            at = pl.multiple_of((node ^ step) * size, 8)
            matrix[pl.ds(at, size), :] = block[k * size : (k + 1) * size]
        value = dot_three(dot_three(factor[...], matrix[...]), factor[...], NT)
        projected[k] = (value + value.T) * (1.0 / order)
        send(projected.at[k], projected_at.at[k])
    for copy in copies:
        copy.wait()


def finish(vectors, blocks, factors, order):
    rows, columns = vectors.shape
    operands = [vectors, *blocks, *factors]
    vmem = pl.BlockSpec(memory_space=pltpu.VMEM)
    shapes = [(rows, columns), (ITERS, columns, columns)]
    return pl.pallas_call(
        functools.partial(finish_kernel, order),
        in_specs=[vmem for _ in operands],
        out_specs=[pl.BlockSpec(memory_space=pltpu.HBM)] * 2,
        out_shape=[jax.ShapeDtypeStruct(x, F32) for x in shapes],
        scratch_shapes=[
            pltpu.VMEM(shapes[1], F32),
            pltpu.VMEM((columns, columns), F32),
            pltpu.SemaphoreType.DMA((1 + ITERS,)),
        ],
        cost_estimate=pl.CostEstimate(flops=10**9, bytes_accessed=10**6, transcendentals=0),
        compiler_params=pltpu.CompilerParams(vmem_limit_bytes=GRANT),
        name="finish",
    )(*[local(x) for x in operands])


def after(value, *others):
    return lax.optimization_barrier((value,) + others)[0]


def per_device(subspace, inverse, weights, diag_tiles, upper_tiles):
    order = float(subspace.shape[0] * lax.axis_size("rows"))
    band = upper_tiles.shape[1]
    partners = lax.axis_size("node") - 1
    factors, pairs = [], []
    for iteration in range(ITERS):
        final = iteration == ITERS - 1
        parts = 1 if final else 2
        if iteration == 0:
            out_a, out_b, coupling, vectors = start(subspace, upper_tiles, inverse)
            got_b = link_swap(out_b)
            got_a = core_swap(out_a)
            base, inverse, weights = start_base(weights, inverse, vectors, coupling, got_a)
            own, *terms = correct(weights, base, got_b, coupling, inverse, parts)
        else:
            own, *terms = solve(
                weights, field, low, factor, coupling, inverse, got_a, got_b, parts
            )
        got = node_spread(terms[:partners])
        if not final:
            low_got = node_spread(terms[partners:])
        total = tree_sum([own] + [x.astype(F32) for x in got])
        piece = total.astype(BF16)
        blocks = [piece] + node_spread([piece] * partners)
        total, sent = lax.optimization_barrier((total, piece))
        if not final:
            total = total + tree_sum([x.astype(F32) for x in low_got])
        low_piece = (total - sent.astype(F32)).astype(BF16)
        low = join([low_piece] + node_spread([low_piece] * partners))
        field, head, part = gram_slice(blocks, band)
        part = part + core_swap(part)
        following = next_head(after(head, part))
        total = chip_sum(part)
        gathered = [total] + node_spread([total] * partners)
        pair = band_slice(field, low, after(following, total), diag_tiles, upper_tiles)
        if not final:
            out_a, out_b = tips(field, low, coupling, inverse)
            got_b = link_swap(out_b)
            got_a = core_swap(out_a)
        halves = first_factor(gathered, order)
        pair = pair + core_swap(pair)
        pairs.append(chip_sum(after(pair, *gathered)))
        if final:
            pair = after(jnp.concatenate(pairs, 0), *halves)
            spread = [pair] + node_spread([pair] * partners)
        factor = second_factor(halves)
        factors.append(factor)
    vectors = last(field, low, factor)
    orthonormal, projected = finish(vectors, spread, factors, order)
    return orthonormal, projected


def solution(mesh):
    placed = (
        P("rows", None),
        P("node", None, "rows", None),
        P("node", None),
        P("rows", None),
        P("rows", None),
    )
    return jax.shard_map(
        per_device, mesh=mesh, in_specs=placed, out_specs=(P("rows", None), P()), check_vma=False
    )
```
